32 devices in a mesh: slot: 2 (over core), ctx: 4 (over y, x), wsh: 4 (over z).
Axes of the slice: x: 2, y: 2, z: 4, core: 2. Of those that a mesh axis runs over, the one named last changes fastest.
Arguments:
- tokens: bfloat16 [2, 2048, 2048], P('slot', ('ctx', 'wsh')), may hold values from -6 to 6
- cotangent: bfloat16 [2, 2048, 2048], P('slot', ('ctx', 'wsh')), may hold values from -6 to 6
- lengths: int32 [2], P('slot'), may hold values from 512 to 2048, as said below
- positions: int32 [2, 2048], P('slot', ('ctx', 'wsh')), may hold values from 0 to 2047, as said below
- token_ids: int32 [2, 2048], P('slot', ('ctx', 'wsh')), may hold values from 0 to 131071
- per_layer_table: bfloat16 [131072, 256], P(('slot', 'ctx', 'wsh')), may hold values from -0.375 to 0.375
- w_query: bfloat16 [2048, 2048], P('wsh'), may hold values from -0.125 to 0.125
- w_key: bfloat16 [2048, 512], P('wsh'), may hold values from -0.125 to 0.125
- w_value: bfloat16 [2048, 512], P('wsh'), may hold values from -0.125 to 0.125
- w_output: bfloat16 [2048, 2048], P('wsh'), may hold values from -0.125 to 0.125
- laurel_left: bfloat16 [2048, 64], P('wsh'), may hold values from -0.125 to 0.125
- laurel_right: bfloat16 [2048, 64], P('wsh'), may hold values from -0.75 to 0.75
- w_gate: bfloat16 [2048, 8192], P('wsh'), may hold values from -0.125 to 0.125
- w_up: bfloat16 [2048, 8192], P('wsh'), may hold values from -0.125 to 0.125
- w_down: bfloat16 [8192, 2048], P('wsh'), may hold values from -0.0625 to 0.0625
- w_layer_gate: bfloat16 [2048, 256], P('wsh'), may hold values from -0.125 to 0.125
- w_layer_proj: bfloat16 [256, 2048], P('wsh'), may hold values from -0.375 to 0.375
- norm_gains: bfloat16 [2048, 6], P('wsh'), may hold values from 0.5 to 1.5
- query_gain: bfloat16 [256], P('wsh'), may hold values from 0.049804688 to 0.19921875
- key_gain: bfloat16 [256], P('wsh'), may hold values from 0.5 to 1.5
Outputs:
- layer_out: bfloat16 [2, 2048, 2048], P('slot', ('ctx', 'wsh'))
- tokens_grad: bfloat16 [2, 2048, 2048], P('slot', ('ctx', 'wsh'))
- table_grad: float32 [131072, 256], P(('slot', 'ctx', 'wsh'))
- query_grad: float32 [2048, 2048], P('wsh')
- key_grad: float32 [2048, 512], P('wsh')
- value_grad: float32 [2048, 512], P('wsh')
- output_grad: float32 [2048, 2048], P('wsh')
- left_grad: float32 [2048, 64], P('wsh')
- right_grad: float32 [2048, 64], P('wsh')
- gate_grad: float32 [2048, 8192], P('wsh')
- up_grad: float32 [2048, 8192], P('wsh')
- down_grad: float32 [8192, 2048], P('wsh')
- layer_gate_grad: float32 [2048, 256], P('wsh')
- layer_proj_grad: float32 [256, 2048], P('wsh')
- gains_grad: float32 [2048, 6], P('wsh')
- query_gain_grad: float32 [256], P('wsh')
- key_gain_grad: float32 [256], P('wsh')
The draws below stay inside these ranges and needn't reach their ends.
Inputs may be any that keep to these rules, and one draw needn't show every extreme that they name: `lengths`: in every draw one slot holds 2048 valid tokens; the other holds at least 512. Within a slot every position 0 to 2047 appears once; each device's 128 tokens hold consecutive positions starting at a multiple of 128.
All inputs are finite; a program needn't handle non-finite values.
Results may differ from the reference program's by a relative error of at most 0.024.
Values may be sent and summed in bfloat16 or wider, within the bound.
No kernel may reach another device: no remote copies, remote signals or barrier semaphores. Data moves between devices by JAX's collectives and lax.ppermute only.
A program may use at most 512 MiB of HBM per device.

```python
import math
import jax
import jax.numpy as jnp
import numpy as np
from jax import lax

D = 2048
HEADS = 8
KV_HEADS = 2
HEAD_DIM = 256
FF = 8192
RANK = 64
PL = 256
VOCAB = 131072
TOK_DEV = 128
SEQS = 2
LEN = 2048


def draw_lengths(key, part):
    full_slot = jax.random.randint(jax.random.fold_in(key, 11), (), 0, SEQS)
    others = jax.random.randint(jax.random.fold_in(key, 12), (SEQS,), LEN // 4, LEN + 1)
    return jnp.where(jnp.arange(SEQS) == full_slot, LEN, others).astype(jnp.int32)


def draw_positions(key, part):
    blocks = LEN // TOK_DEV

    def one_slot(slot_key):
        block_order = jax.random.permutation(slot_key, blocks)
        return (block_order[:, None] * TOK_DEV + jnp.arange(TOK_DEV)[None, :]).reshape(LEN)
    slot_keys = jax.random.split(jax.random.fold_in(key, 13), SEQS)
    return jax.vmap(one_slot)(slot_keys).astype(jnp.int32)


def touch_ends(values, own_key, smallest, largest):
    place = [jax.random.randint(jax.random.fold_in(own_key, axis), (), 0, length) for axis, length in enumerate(values.shape)]
    widest = values.shape.index(max(values.shape))
    next_to = place[:widest] + [(place[widest] + 1) % values.shape[widest]] + place[widest + 1:]
    return values.at[tuple(place)].set(smallest).at[tuple(next_to)].set(largest)


def block_levels(rng, extent, cuts, smallest, high):
    level, own = 1.0, jax.random.fold_in(rng, 6)
    for position, parts in cuts:
        draws = jnp.exp(jax.random.uniform(jax.random.fold_in(own, position), (parts,), jnp.float32, smallest / len(cuts), high / len(cuts)))
        level = level * jnp.repeat(draws, extent[position] // parts).reshape([-1 if axis == position else 1 for axis in range(len(extent))])
    return level


def wide_ids(own_key, shape, amount, skew):
    weights = [min(1 << octave, amount + 1 - (1 << octave)) * (1 << 20) // math.isqrt((1 << octave) ** skew) + 1 for octave in range((amount + 1).bit_length()) if 1 << octave <= amount]
    scale = 1 + sum(weights) // (1 << 30)
    table = np.cumsum(np.array([max(1, weight // scale) for weight in weights]))
    pick = jax.random.randint(jax.random.fold_in(own_key, 1), shape, 0, int(table[len(weights) - 1]))
    start = jnp.left_shift(1, jnp.searchsorted(jnp.asarray(table, jnp.int32), pick, side="right").astype(jnp.int32))
    grade = start - 1 + jax.random.randint(jax.random.fold_in(own_key, 4), shape, 0, 1 << 30) % jnp.minimum(start, amount + 1 - start)
    return jax.random.permutation(jax.random.fold_in(own_key, 2), amount)[grade].astype(jnp.int32)


def normal_values(own_key, dims, deviation, limit, pieces=(), kind=jnp.bfloat16):
    array = jax.random.normal(own_key, dims, jnp.float32) * deviation
    if len(pieces) > 0:
        array = block_levels(own_key, dims, pieces, -0.22, 0.18) * array
    return jnp.clip(array, min=-limit, max=limit).astype(kind)


def setup_inputs(seed: int = 0) -> dict:
    arg_keys = jax.random.split(jax.random.key(seed), 21)
    return {
        "tokens": normal_values(arg_keys[0], (SEQS, LEN, D), 1.0, 6.0, ((0, 2), (1, 16))),
        "cotangent": normal_values(arg_keys[1], (SEQS, LEN, D), 1.0, 6.0, ((0, 2), (1, 16))),
        "lengths": draw_lengths(jax.random.fold_in(arg_keys[20], 71), 0),
        "positions": draw_positions(jax.random.fold_in(arg_keys[20], 71), 0),
        "token_ids": touch_ends(wide_ids(arg_keys[4], (SEQS, LEN), VOCAB, 2), jax.random.fold_in(arg_keys[4], 3), 0, VOCAB - 1).astype(jnp.int32),
        "per_layer_table": normal_values(arg_keys[5], (VOCAB, PL), 0.0625, 0.375, ((0, 32),)),
        "w_query": normal_values(arg_keys[6], (D, HEADS * HEAD_DIM), D ** -0.5, 0.125, ((0, 4),)),
        "w_key": normal_values(arg_keys[7], (D, KV_HEADS * HEAD_DIM), D ** -0.5, 0.125, ((0, 4),)),
        "w_value": normal_values(arg_keys[8], (D, KV_HEADS * HEAD_DIM), D ** -0.5, 0.125, ((0, 4),)),
        "w_output": normal_values(arg_keys[9], (HEADS * HEAD_DIM, D), (HEADS * HEAD_DIM) ** -0.5, 0.125, ((0, 4),)),
        "laurel_left": normal_values(arg_keys[10], (D, RANK), D ** -0.5, 0.125, ((0, 4),)),
        "laurel_right": normal_values(arg_keys[11], (D, RANK), RANK ** -0.5, 0.75, ((0, 4),)),
        "w_gate": normal_values(arg_keys[12], (D, FF), D ** -0.5, 0.125, ((0, 4),)),
        "w_up": normal_values(arg_keys[13], (D, FF), D ** -0.5, 0.125, ((0, 4),)),
        "w_down": normal_values(arg_keys[14], (FF, D), FF ** -0.5, 0.0625, ((0, 4),)),
        "w_layer_gate": normal_values(arg_keys[15], (D, PL), D ** -0.5, 0.125, ((0, 4),)),
        "w_layer_proj": normal_values(arg_keys[16], (PL, D), PL ** -0.5, 0.375, ((0, 4),)),
        "norm_gains": jnp.clip(1.0 + 0.1 * jax.random.normal(arg_keys[17], (D, 6), jnp.float32), 0.5, 1.5).astype(jnp.bfloat16),
        "query_gain": jnp.clip(jnp.exp(math.log(0.19921875) - 1.3862944 * jax.random.uniform(arg_keys[18], (HEAD_DIM,), jnp.float32) ** block_levels(arg_keys[18], (HEAD_DIM,), ((0, 4),), -0.2, 0.2)), 0.049804688, 0.19921875).astype(jnp.bfloat16),
        "key_gain": jnp.clip(1.0 + 0.1 * jax.random.normal(arg_keys[19], (HEAD_DIM,), jnp.float32), 0.5, 1.5).astype(jnp.bfloat16),
    }


@jax.custom_vjp
def low(v):
    return lax.optimization_barrier(v.astype(jnp.bfloat16)).astype(jnp.float32)

@jax.custom_vjp
def low_back(v):
    return v

def low_keep(v):
    return (low(v), None)

def low_pass(kept, grad):
    return (grad,)

def back_keep(v):
    return (v, None)

def back_low(kept, grad):
    return (low(grad),)
low.defvjp(low_keep, low_pass)
low_back.defvjp(back_keep, back_low)
EPSILON = 1e-06
ROPE_BASE = 1000000.0
HALF_ROOT = 0.7071067811865476
TANH_SCALE = 0.7978845608028654
NEGATIVE = -1e+30
EMBED_SCALE = 16.0

def matmul(left, right):
    return jnp.dot(left, right, precision=lax.Precision.HIGHEST, preferred_element_type=jnp.float32)

def rms_norm(value, gain):
    return value * lax.rsqrt(lax.optimization_barrier(jnp.mean(value * value, axis=-1, keepdims=True)) + EPSILON) * gain

def gelu_tanh(value):
    return 0.5 * value * (1.0 + jnp.tanh(TANH_SCALE * (value + 0.044715 * value * value * value)))

def rotate(value, places):
    width_all = value.shape[-1]
    half_width = width_all // 2
    inverse = jnp.exp(-math.log(ROPE_BASE) * (2.0 * jnp.arange(half_width, dtype=jnp.float32) / width_all))
    angles = places.astype(jnp.float32)[:, None] * inverse[None, :]
    cosine = jnp.cos(angles)[:, None, :]
    sine = jnp.sin(angles)[:, None, :]
    front = value[..., :half_width]
    behind = value[..., half_width:]
    return jnp.concatenate([front * cosine - behind * sine, behind * cosine + front * sine], axis=-1)

def attention(q_rot, k_rot, v_norm, slot_positions, length):
    seq_rows = q_rot.shape[0]
    block_rows = math.gcd(512, seq_rows)
    groups = HEADS // KV_HEADS
    key_valid = slot_positions < length

    def one_block(block_number):
        begin = block_number * block_rows
        queries = lax.dynamic_slice_in_dim(q_rot, begin, block_rows, 0).reshape(block_rows, KV_HEADS, groups, HEAD_DIM)
        query_places = lax.dynamic_slice_in_dim(slot_positions, begin, block_rows, 0)
        scores = low_back(jnp.einsum('qkgd,tkd->qkgt', queries, k_rot, precision=lax.Precision.HIGHEST))
        allowed = (slot_positions[None, :] <= query_places[:, None]) & key_valid[None, :]
        scores = jnp.where(allowed[:, None, None, :], scores, NEGATIVE)
        peak = lax.optimization_barrier(jnp.max(scores, axis=-1, keepdims=True))
        raised = jnp.exp(scores - peak)
        probs = raised / lax.optimization_barrier(jnp.sum(raised, axis=-1, keepdims=True))
        outputs = jnp.einsum('qkgt,tkd->qkgd', low(probs), v_norm, precision=lax.Precision.HIGHEST)
        return outputs.reshape(block_rows, HEADS * HEAD_DIM)
    blocks = lax.map(jax.checkpoint(one_block), jnp.arange(seq_rows // block_rows, dtype=jnp.int32))
    return blocks.reshape(seq_rows, HEADS * HEAD_DIM)

def layer(tokens_f, params, table_f, slot_ids, slot_positions, length):
    w_query, w_key, w_value, w_output, laurel_left, laurel_right, w_gate, w_up, w_down, w_layer_gate, w_layer_proj, norm_gains, query_gain, key_gain = params
    seq_rows = tokens_f.shape[0]
    normed = rms_norm(tokens_f, norm_gains[:, 0])
    normed_low = low(normed)
    query = low_back(matmul(normed_low, w_query)).reshape(seq_rows, HEADS, HEAD_DIM)
    key = low_back(matmul(normed_low, w_key)).reshape(seq_rows, KV_HEADS, HEAD_DIM)
    value = low_back(matmul(normed_low, w_value)).reshape(seq_rows, KV_HEADS, HEAD_DIM)
    q_rot = low(rotate(rms_norm(query, query_gain), slot_positions))
    k_rot = low(rotate(rms_norm(key, key_gain), slot_positions))
    v_norm = low(rms_norm(value, 1.0))
    attended = low_back(attention(q_rot, k_rot, v_norm, slot_positions, length))
    attn_proj = low_back(matmul(low(attended), w_output))
    first_sum = tokens_f + rms_norm(attn_proj, norm_gains[:, 1])
    low_rank = low_back(matmul(normed_low, laurel_left))
    laurel_out = low_back(matmul(low(low_rank), laurel_right.T))
    laurel = normed + rms_norm(laurel_out, norm_gains[:, 2])
    mixed = (first_sum + laurel) * HALF_ROOT
    ff_in = low(rms_norm(mixed, norm_gains[:, 3]))
    gate = low_back(matmul(ff_in, w_gate))
    upward = low_back(matmul(ff_in, w_up))
    hidden = low(gelu_tanh(gate) * upward)
    ff_out = low_back(matmul(hidden, w_down))
    third_sum = mixed + rms_norm(ff_out, norm_gains[:, 4])
    layer_gate = low_back(matmul(low(third_sum), w_layer_gate))
    layer_input = low_back(EMBED_SCALE * jnp.take(table_f, slot_ids, axis=0))
    gated = low(gelu_tanh(layer_gate) * layer_input)
    layer_proj = low_back(matmul(gated, w_layer_proj))
    return third_sum + rms_norm(layer_proj, norm_gains[:, 5])

def reference(tokens, cotangent, lengths, positions, token_ids, per_layer_table, w_query, w_key, w_value, w_output, laurel_left, laurel_right, w_gate, w_up, w_down, w_layer_gate, w_layer_proj, norm_gains, query_gain, key_gain):
    params = tuple((weight_array.astype(jnp.float32) for weight_array in (w_query, w_key, w_value, w_output, laurel_left, laurel_right, w_gate, w_up, w_down, w_layer_gate, w_layer_proj, norm_gains, query_gain, key_gain)))
    table_f = per_layer_table.astype(jnp.float32)
    start_sums = (jax.tree.map(jnp.zeros_like, params), jnp.zeros_like(table_f))

    def per_slot(carried, slot_data):
        tokens_s, cot_s, ids_s, places_s, length_s = slot_data

        def forward(tokens_in, params_in, table_in):
            return layer(tokens_in, params_in, table_in, ids_s, places_s, length_s)
        result, pullback = jax.vjp(forward, tokens_s.astype(jnp.float32), params, table_f)
        valid = (places_s < length_s).astype(jnp.float32)
        grad_tokens, grad_params, grad_table = pullback(cot_s.astype(jnp.float32) * valid[:, None])
        summed = (jax.tree.map(jnp.add, carried[0], grad_params), carried[1] + grad_table)
        return (summed, (result.astype(jnp.bfloat16), grad_tokens.astype(jnp.bfloat16)))
    (grad_params, grad_table), (layer_out, tokens_grad) = lax.scan(per_slot, start_sums, (tokens, cotangent, token_ids, positions, lengths))
    return (layer_out, tokens_grad, grad_table, grad_params[0], grad_params[1], grad_params[2], grad_params[3], grad_params[4], grad_params[5], grad_params[6], grad_params[7], grad_params[8], grad_params[9], grad_params[10], grad_params[11], grad_params[12], grad_params[13])
```

```python
import functools
import math

import jax
import jax.numpy as jnp
from jax import lax
from jax.experimental import pallas as pl
from jax.experimental.pallas import tpu as pltpu
from jax.sharding import PartitionSpec as P

HEADS = 8
KV_HEADS = 2
HEAD_DIM = 256


EPSILON = 1e-06
ROPE_BASE = 1000000.0
HALF_ROOT = 0.7071067811865476
TANH_SCALE = 0.7978845608028654
NEGATIVE = -1e30
EMBED_SCALE = 16.0


def rms_norm(value, gain):
    return value * lax.rsqrt(jnp.mean(value * value, axis=-1, keepdims=True) + EPSILON) * gain


def gelu_tanh(value):
    return 0.5 * value * (1.0 + jnp.tanh(TANH_SCALE * (value + 0.044715 * value * value * value)))


def gated_product(pre_gate, other_side):
    return gelu_tanh(pre_gate) * other_side


def rotate(value, places):
    width_all = value.shape[-1]
    half_width = width_all // 2
    inverse = jnp.exp(
        -math.log(ROPE_BASE) * (2.0 * jnp.arange(half_width, dtype=jnp.float32) / width_all)
    )
    angles = places.astype(jnp.float32)[:, None] * inverse[None, :]
    cosine = jnp.cos(angles)[:, None, :]
    sine = jnp.sin(angles)[:, None, :]
    front = value[..., :half_width]
    behind = value[..., half_width:]
    return jnp.concatenate(
        [front * cosine - behind * sine, behind * cosine + front * sine], axis=-1
    )


def matmul(left, right):
    return jnp.dot(left, right, preferred_element_type=jnp.float32)


def times_transposed(left, right):
    return lax.dot_general(
        left, right, (((1,), (1,)), ((), ())), preferred_element_type=jnp.float32
    )


def over_rows(left, right):
    return lax.dot_general(
        left, right, (((0,), (0,)), ((), ())), preferred_element_type=jnp.float32
    )


LOW = jnp.bfloat16
WIDE = jnp.float32
EVERY = ("slot", "ctx", "wsh")


def swap(value, axis, bit):
    size = lax.axis_size(axis)
    return lax.ppermute(value, axis, [(i, i ^ bit) for i in range(size)])


def shift(value, amount):
    size = lax.axis_size("wsh")
    return lax.ppermute(value, "wsh", [(i, (i + amount) % size) for i in range(size)])


def ring_gather(value):
    return [value] + [shift(value, k) for k in range(1, lax.axis_size("wsh"))]


def ring_scatter(blocks):
    total = blocks[0].astype(WIDE)
    for k in range(1, len(blocks)):
        total = total + shift(blocks[k], -k).astype(WIDE)
    return total


def row_blocks(value, count):
    rows = value.shape[0] // count
    return [value[k * rows : (k + 1) * rows] for k in range(count)]


def add_low(left, right):
    return (left.astype(WIDE) + right.astype(WIDE)).astype(LOW)


def ctx_gather(piece):
    size = lax.axis_size("ctx")
    if size == 4:
        half = piece.shape[0] // 2
        one = swap(piece, "ctx", 1)
        two = swap(piece, "ctx", 2)
        front = swap(one[:half], "ctx", 2)
        behind = swap(two[half:], "ctx", 1)
        return [piece, one, two, jnp.concatenate([front, behind], axis=0)]
    pieces = [piece]
    bit = 1
    while bit < size:
        pieces = pieces + [swap(p, "ctx", bit) for p in pieces]
        bit *= 2
    return pieces


def ctx_reduce(pieces):
    size = len(pieces)
    if size == 4:
        half = pieces[0].shape[0] // 2
        front = swap(pieces[3][:half], "ctx", 1)
        behind = swap(pieces[3][half:], "ctx", 2)
        two = jnp.concatenate([add_low(pieces[2][:half], front), pieces[2][half:]], axis=0)
        one = jnp.concatenate([pieces[1][:half], add_low(pieces[1][half:], behind)], axis=0)
        one = swap(one, "ctx", 1)
        two = swap(two, "ctx", 2)
        return (pieces[0].astype(WIDE) + one.astype(WIDE) + two.astype(WIDE)).astype(LOW)
    while size > 1:
        size //= 2
        pieces = [add_low(pieces[i], swap(pieces[size + i], "ctx", size)) for i in range(size)]
    return pieces[0]


def chip_gather(piece):
    pieces = ctx_gather(piece)
    return pieces + [swap(p, "slot", 1) for p in pieces]


def assemble_kernel(extent, cuts, own, *refs):
    step = pl.program_id(0)
    ins, outs = refs[:extent], refs[extent:]
    for number in range(extent):

        @pl.when(step == number)
        def _(number=number):
            for (begin, width), out in zip(cuts, outs):
                out[:, 0] = ins[number][:, :, begin : begin + width].astype(out.dtype)


def assemble(pieces, own, kind, cuts=None):
    count = len(pieces)
    outer, inner, width = pieces[0].shape
    cuts = cuts or [(0, width)]
    results = pl.pallas_call(
        functools.partial(assemble_kernel, count, cuts),
        grid_spec=pltpu.PrefetchScalarGridSpec(
            num_scalar_prefetch=1,
            grid=(count,),
            in_specs=[pl.BlockSpec((outer, inner, width), lambda i, o: (0, 0, 0))] * count,
            out_specs=[
                pl.BlockSpec((outer, 1, inner, w), lambda i, o: (0, lax.bitwise_xor(i, o[0]), 0, 0))
                for _, w in cuts
            ],
        ),
        out_shape=[jax.ShapeDtypeStruct((outer, count, inner, w), kind) for _, w in cuts],
    )(own, *pieces)
    return results


def permute_kernel(own, source, out):
    out[0] = source[:, 0]


def relative(value, own):
    outer, count, inner, width = value.shape
    return pl.pallas_call(
        permute_kernel,
        grid_spec=pltpu.PrefetchScalarGridSpec(
            num_scalar_prefetch=1,
            grid=(count,),
            in_specs=[
                pl.BlockSpec(
                    (outer, 1, inner, width), lambda i, o: (0, lax.bitwise_xor(i, o[0]), 0, 0)
                )
            ],
            out_specs=pl.BlockSpec((1, outer, inner, width), lambda i, o: (i, 0, 0, 0)),
        ),
        out_shape=jax.ShapeDtypeStruct((count, outer, inner, width), value.dtype),
    )(own, value)


def pair_kernel(count, columns, *refs):
    step = pl.program_id(0)
    ins, gate, up = refs[:count], refs[count], refs[count + 1]
    inner = pl.num_programs(1)
    for number in range(count):

        @pl.when(step == number)
        def _(number=number):
            gate[...] = ins[number][0, 0].astype(gate.dtype)
            up[...] = ins[number][0, 1].astype(up.dtype)


def assemble_pair(pieces, columns):
    count = len(pieces)
    outer, _, rows, width = pieces[0].shape
    total = count * outer

    def source(number):
        def at(i, k, columns):
            return (jnp.where(i == number, k, jnp.where(i < number, 0, outer - 1)), 0, 0, 0)

        return pl.BlockSpec((1, 2, rows, width), at)

    def place(i, k, columns):
        return (0, columns[i * outer + k])

    return pl.pallas_call(
        lambda columns, *refs: pair_kernel(count, columns, *refs),
        grid_spec=pltpu.PrefetchScalarGridSpec(
            num_scalar_prefetch=1,
            grid=(count, outer),
            in_specs=[source(number) for number in range(count)],
            out_specs=[pl.BlockSpec((rows, width), place)] * 2,
        ),
        out_shape=[jax.ShapeDtypeStruct((rows, width * total), WIDE)] * 2,
    )(columns, *pieces)


def shards(
    tokens,
    cotangent,
    lengths,
    positions,
    token_ids,
    per_layer_table,
    w_query,
    w_key,
    w_value,
    w_output,
    laurel_left,
    laurel_right,
    w_gate,
    w_up,
    w_down,
    w_layer_gate,
    w_layer_proj,
    norm_gains,
    query_gain,
    key_gain,
):
    rows_dev, width = tokens.shape[1:]
    run = lax.axis_size("wsh")
    contexts = lax.axis_size("ctx")
    parts = 2 * contexts
    here = lax.axis_index("wsh")
    chip = lax.axis_index(("slot", "ctx"))
    own = jnp.full((1,), chip, jnp.int32)
    shard_rows = width // run
    heads_here = HEADS // run
    query_width = heads_here * HEAD_DIM
    groups = HEADS // KV_HEADS
    hidden_width = w_gate.shape[1] // run
    order = (here - jnp.arange(run, dtype=jnp.int32)) % run

    def absolute(stacked, axis=0):
        return jnp.take(stacked, order, axis=axis)

    tokens_run = jnp.concatenate(ring_gather(tokens[0]), axis=0)
    small = jnp.concatenate(
        [
            norm_gains.T,
            jnp.pad(
                jnp.concatenate([query_gain, key_gain])[None],
                ((0, 1), (0, shard_rows - 2 * query_gain.shape[0])),
            ),
        ],
        axis=0,
    )
    small_all = absolute(jnp.stack(ring_gather(small)))
    gains_full = small_all.transpose(1, 0, 2).reshape(8, width).astype(WIDE)
    gain_cut = query_gain.shape[0]
    query_gain_full = small_all[:, 6, :gain_cut].reshape(HEAD_DIM).astype(WIDE)
    key_gain_full = small_all[:, 6, gain_cut : 2 * gain_cut].reshape(HEAD_DIM).astype(WIDE)

    piece_rows = shard_rows // parts

    def share(weight):
        return lax.dynamic_slice_in_dim(weight, chip * piece_rows, piece_rows, 0)

    query_rows, key_rows, value_rows = share(w_query), share(w_key), share(w_value)

    def kv_head(index):
        return index * heads_here // groups

    received = []
    for k in range(run):
        target = (here + k) % run
        piece = jnp.concatenate(
            [
                lax.dynamic_slice_in_dim(query_rows, target * query_width, query_width, 1),
                lax.dynamic_slice_in_dim(key_rows, kv_head(target) * HEAD_DIM, HEAD_DIM, 1),
                lax.dynamic_slice_in_dim(value_rows, kv_head(target) * HEAD_DIM, HEAD_DIM, 1),
            ],
            axis=1,
        )
        received.append(piece if k == 0 else shift(piece, k))
    (w_heads,) = assemble(chip_gather(absolute(jnp.stack(received))), own, LOW)
    w_heads = w_heads.reshape(width, query_width + 2 * HEAD_DIM)

    indices = lax.all_gather(jnp.concatenate([token_ids, positions], axis=0), EVERY, axis=0)
    all_ids = indices[:, 0].reshape(-1)
    slot_places = lax.dynamic_index_in_dim(
        indices[:, 1].reshape(2, contexts, run, rows_dev), lax.axis_index("slot"), 0, False
    )
    context_order = jnp.bitwise_xor(
        jnp.arange(contexts, dtype=jnp.int32), lax.axis_index("ctx").astype(jnp.int32)
    )
    key_places = jnp.take(jnp.take(slot_places, context_order, axis=0), order, axis=1)
    run_places = key_places[0].reshape(run * rows_dev)
    key_places = key_places.reshape(-1)
    length = lengths[0]
    own_places = positions[0]

    piece_width = hidden_width // parts
    received = []
    for k in range(run):
        first = ((here + k) % run) * hidden_width + chip * piece_width
        piece = jnp.stack(
            [
                lax.dynamic_slice_in_dim(w_gate, first, piece_width, 1),
                lax.dynamic_slice_in_dim(w_up, first, piece_width, 1),
            ]
        )
        received.append(piece if k == 0 else shift(piece, k))
    mine = absolute(jnp.stack(received, axis=1), axis=1).reshape(2, width, piece_width)
    ff_pieces = chip_gather(mine)
    gate_weight = jnp.concatenate([p[0] for p in ff_pieces], axis=1)
    up_weight = jnp.concatenate([p[1] for p in ff_pieces], axis=1)
    down_weight = relative(w_down.reshape(1, parts, piece_width, width), own).reshape(
        hidden_width, width
    )
    laurel_weights = lax.all_gather(
        jnp.concatenate([laurel_left, laurel_right, w_layer_gate], axis=1), "wsh", axis=0, tiled=True
    )
    rank = laurel_left.shape[1]
    left_full = laurel_weights[:, :rank]
    right_full = laurel_weights[:, rank : 2 * rank]
    layer_gate_full = laurel_weights[:, 2 * rank :]
    layer_proj_full = lax.all_gather(w_layer_proj, "wsh", axis=0, tiled=True)

    vocab_rows = per_layer_table.shape[0]
    vocab_first = lax.axis_index(EVERY) * vocab_rows
    vocab_range = jnp.arange(vocab_rows, dtype=jnp.int32)

    def one_hot():
        return ((all_ids - vocab_first)[:, None] == vocab_range[None, :]).astype(LOW)

    layer_input = EMBED_SCALE * lax.psum_scatter(
        matmul(one_hot(), per_layer_table).astype(LOW), EVERY, scatter_dimension=0, tiled=True
    ).astype(WIDE)

    normed_run = rms_norm(tokens_run.astype(WIDE), gains_full[0])
    normed_low = normed_run.astype(LOW)
    tokens_f = tokens[0].astype(WIDE)
    normed = rms_norm(tokens_f, gains_full[0])
    normed_own = normed_low[:rows_dev]
    total_rows = run * rows_dev
    projected = matmul(normed_low, w_heads)
    query = projected[:, :query_width]
    key = projected[:, query_width : query_width + HEAD_DIM]
    value = projected[:, query_width + HEAD_DIM :]

    def query_path(raw, gain):
        return rotate(rms_norm(raw.reshape(total_rows, heads_here, HEAD_DIM), gain), run_places)

    def key_path(raw, gain):
        return rotate(rms_norm(raw.reshape(total_rows, 1, HEAD_DIM), gain), run_places)[:, 0]

    def value_path(raw):
        return rms_norm(raw, 1.0)

    q_low = query_path(query, query_gain_full).astype(LOW)
    k_low = key_path(key, key_gain_full).astype(LOW)
    v_low = value_path(value).astype(LOW)
    keys_values = jnp.concatenate(
        ctx_gather(jnp.concatenate([k_low, v_low], axis=1)), axis=0
    )
    keys_all = keys_values[:, :HEAD_DIM]
    values_all = keys_values[:, HEAD_DIM:]
    allowed = (key_places[None, :] <= run_places[:, None]) & (key_places < length)[None, :]
    scores = jnp.einsum("qhd,td->hqt", q_low, keys_all, preferred_element_type=WIDE)
    scores = jnp.where(allowed[None], scores, NEGATIVE)
    top = jnp.max(scores, axis=-1, keepdims=True)
    raised = jnp.exp(scores - top)
    probs = raised / jnp.sum(raised, axis=-1, keepdims=True)
    attended = jnp.einsum(
        "hqt,td->qhd", probs.astype(LOW), values_all, preferred_element_type=WIDE
    )
    attended_low = attended.astype(LOW).reshape(total_rows, query_width)
    attn_proj = ring_scatter(row_blocks(matmul(attended_low, w_output).astype(LOW), run))

    first_sum = tokens_f + rms_norm(attn_proj, gains_full[1])
    low_rank = matmul(normed_own, left_full)
    low_rank_low = low_rank.astype(LOW)
    laurel_out = times_transposed(low_rank_low, right_full)
    laurel = normed + rms_norm(laurel_out, gains_full[2])
    mixed = (first_sum + laurel) * HALF_ROOT
    ff_in_low = rms_norm(mixed, gains_full[3]).astype(LOW)

    ff_run = jnp.concatenate(ring_gather(ff_in_low), axis=0)
    gate = matmul(ff_run, gate_weight)
    upward = matmul(ff_run, up_weight)
    hidden_low = gated_product(gate, upward).astype(LOW)
    ff_out = ring_scatter(row_blocks(matmul(hidden_low, down_weight).astype(LOW), run))
    third_sum = mixed + rms_norm(ff_out, gains_full[4])
    third_low = third_sum.astype(LOW)

    layer_gate = matmul(third_low, layer_gate_full)
    gated_low = gated_product(layer_gate, layer_input).astype(LOW)
    layer_proj = matmul(gated_low, layer_proj_full)
    result = third_sum + rms_norm(layer_proj, gains_full[5])
    layer_out = result.astype(LOW)[None]

    valid = (own_places < length).astype(WIDE)
    grad_out = cotangent[0].astype(WIDE) * valid[:, None]
    _, pullback = jax.vjp(rms_norm, layer_proj, gains_full[5])
    grad_proj, grad_gain_five = pullback(grad_out)
    grad_proj_low = grad_proj.astype(LOW)
    grad_gated = times_transposed(grad_proj_low, layer_proj_full)
    _, pullback = jax.vjp(gated_product, layer_gate, layer_input)
    grad_lgate, grad_input = pullback(grad_gated)
    grad_lgate_low = grad_lgate.astype(LOW)
    grad_input_low = grad_input.astype(LOW)
    grad_third = grad_out + times_transposed(grad_lgate_low, layer_gate_full)
    _, pullback = jax.vjp(rms_norm, ff_out, gains_full[4])
    grad_ff, grad_gain_four = pullback(grad_third)
    grad_ff_low = grad_ff.astype(LOW)

    grad_ff_run = jnp.concatenate(ring_gather(grad_ff_low), axis=0)
    grad_hidden = times_transposed(grad_ff_run, down_weight)
    _, pullback = jax.vjp(gated_product, gate, upward)
    grad_gate, grad_upward = pullback(grad_hidden)
    grad_gate_low = grad_gate.astype(LOW)
    grad_upward_low = grad_upward.astype(LOW)
    grad_ff_in = ring_scatter(
        row_blocks(
            (
                times_transposed(grad_gate_low, gate_weight)
                + times_transposed(grad_upward_low, up_weight)
            ).astype(LOW),
            run,
        )
    )
    half = hidden_width // 2

    def slot_sum(make):
        other = swap(make(1), "slot", 1)
        return add_low(make(0), other)

    down_sum = slot_sum(
        lambda side: over_rows(hidden_low[:, side * half : (side + 1) * half], grad_ff_run).astype(LOW)
    )
    down_own = ctx_reduce(row_blocks(down_sum, contexts))
    (down_grad,) = assemble([p[None] for p in chip_gather(down_own)], own, WIDE)
    gate_sum = slot_sum(
        lambda side: over_rows(ff_run, grad_gate_low[:, side * half : (side + 1) * half]).astype(LOW)
    )
    up_sum = slot_sum(
        lambda side: over_rows(ff_run, grad_upward_low[:, side * half : (side + 1) * half]).astype(LOW)
    )
    pair_own = ctx_reduce(
        [
            jnp.stack(
                [
                    gate_sum[:, r * piece_width : (r + 1) * piece_width],
                    up_sum[:, r * piece_width : (r + 1) * piece_width],
                ]
            )
            for r in range(contexts)
        ]
    )
    received = []
    for k in range(run):
        piece = lax.dynamic_slice_in_dim(pair_own, ((here + k) % run) * shard_rows, shard_rows, 1)
        received.append(piece if k == 0 else shift(piece, k))
    pair_pieces = chip_gather(jnp.stack(received))
    part_range = jnp.arange(parts, dtype=jnp.int32)
    if piece_width % 128 == 0:
        columns = order[None, :] * parts + jnp.bitwise_xor(part_range, chip)[:, None]
        gate_grad, up_grad = assemble_pair(pair_pieces, columns.reshape(-1))
    else:
        stacked = absolute(jnp.stack(pair_pieces), axis=1)
        stacked = jnp.take(stacked, jnp.bitwise_xor(part_range, chip), axis=0)
        stacked = stacked.transpose(2, 3, 1, 0, 4).reshape(2, shard_rows, -1).astype(WIDE)
        gate_grad, up_grad = stacked[0], stacked[1]

    _, pullback = jax.vjp(rms_norm, mixed, gains_full[3])
    grad_mixed_norm, grad_gain_three = pullback(grad_ff_in)
    grad_branch = (grad_third + grad_mixed_norm) * HALF_ROOT
    _, pullback = jax.vjp(rms_norm, attn_proj, gains_full[1])
    grad_attn, grad_gain_one = pullback(grad_branch)
    grad_attn_low = grad_attn.astype(LOW)
    grad_attn_run = jnp.concatenate(ring_gather(grad_attn_low), axis=0)
    _, pullback = jax.vjp(rms_norm, laurel_out, gains_full[2])
    grad_laurel, grad_gain_two = pullback(grad_branch)
    grad_laurel_low = grad_laurel.astype(LOW)
    grad_rank_low = matmul(grad_laurel_low, right_full).astype(LOW)

    grad_att_low = times_transposed(grad_attn_run, w_output).astype(LOW)
    grad_att = grad_att_low.reshape(total_rows, heads_here, HEAD_DIM)
    row_delta = jnp.sum(grad_att.astype(WIDE) * attended, axis=-1)
    grad_probs = jnp.einsum("qhd,td->hqt", grad_att, values_all, preferred_element_type=WIDE)
    grad_scores = (probs * (grad_probs - row_delta.T[:, :, None])).astype(LOW)
    grad_q_rot = jnp.einsum("hqt,td->qhd", grad_scores, keys_all, preferred_element_type=WIDE)
    key_part = jnp.einsum("hqt,qhd->td", grad_scores, q_low, preferred_element_type=WIDE)
    value_part = jnp.einsum("hqt,qhd->td", probs.astype(LOW), grad_att, preferred_element_type=WIDE)
    kv_sum = ctx_reduce(
        row_blocks(jnp.concatenate([key_part, value_part], axis=1).astype(LOW), contexts)
    ).astype(WIDE)
    grad_k_rot, grad_v_norm = kv_sum[:, :HEAD_DIM], kv_sum[:, HEAD_DIM:]
    _, pullback = jax.vjp(query_path, query, query_gain_full)
    grad_query, grad_query_gain = pullback(grad_q_rot)
    _, pullback = jax.vjp(key_path, key, key_gain_full)
    grad_key, grad_key_gain = pullback(grad_k_rot)
    _, pullback = jax.vjp(value_path, value)
    (grad_value,) = pullback(grad_v_norm)
    grad_heads_low = jnp.concatenate([grad_query, grad_key, grad_value], axis=1).astype(LOW)
    grad_normed = (
        ring_scatter(row_blocks(times_transposed(grad_heads_low, w_heads).astype(LOW), run))
        + times_transposed(grad_rank_low, left_full)
        + grad_branch
    )
    _, pullback = jax.vjp(rms_norm, tokens_f, gains_full[0])
    grad_tokens, grad_gain_zero = pullback(grad_normed)
    tokens_grad = (grad_tokens + grad_branch).astype(LOW)[None]

    def group_sum(value):
        summed = add_low(value[:contexts], swap(value[contexts:], "slot", 1))
        return ctx_reduce([summed[r] for r in range(contexts)])

    output_part = over_rows(attended_low, grad_attn_run).astype(LOW)
    output_own = group_sum(
        relative(output_part.reshape(1, parts, query_width // parts, width), own)[:, 0]
    )
    (output_grad,) = assemble([p[None] for p in chip_gather(output_own)], own, WIDE)
    heads_part = over_rows(normed_low, grad_heads_low).astype(LOW)
    heads_own = group_sum(
        relative(heads_part.reshape(run, parts, piece_rows, query_width + 2 * HEAD_DIM), own)
    )
    received = []
    for k in range(run):
        piece = lax.dynamic_index_in_dim(heads_own, (here + k) % run, 0, False)
        received.append(piece if k == 0 else shift(piece, k))
    by_run = absolute(jnp.stack(received))
    query_piece = by_run[:, :, :query_width].transpose(1, 0, 2).reshape(piece_rows, -1)
    kv_pieces = []
    for begin in (query_width, query_width + HEAD_DIM):
        one = by_run[:, :, begin : begin + HEAD_DIM].astype(WIDE)
        one = one.reshape(KV_HEADS, run // KV_HEADS, piece_rows, HEAD_DIM).sum(axis=1)
        kv_pieces.append(one.astype(LOW).transpose(1, 0, 2).reshape(piece_rows, -1))
    heads_piece = jnp.concatenate([query_piece] + kv_pieces, axis=1)
    kv_width = KV_HEADS * HEAD_DIM
    query_all = HEADS * HEAD_DIM
    query_grad, key_grad, value_grad = assemble(
        [p[None] for p in chip_gather(heads_piece)],
        own,
        WIDE,
        [(0, query_all), (query_all, kv_width), (query_all + kv_width, kv_width)],
    )

    every_grad = lax.all_gather(grad_input_low, EVERY, axis=0, tiled=True)
    table_grad = EMBED_SCALE * over_rows(one_hot(), every_grad)
    left_grad = over_rows(normed_own, grad_rank_low)
    right_grad = over_rows(grad_laurel_low, low_rank_low)
    layer_gate_grad = over_rows(third_low, grad_lgate_low)
    layer_proj_grad = over_rows(gated_low, grad_proj_low)

    def all_sum(value):
        value = lax.psum_scatter(value.astype(LOW), "wsh", scatter_dimension=0, tiled=True)
        return lax.psum(value, ("slot", "ctx")).astype(WIDE)

    narrow = all_sum(jnp.concatenate([left_grad, right_grad, layer_gate_grad], axis=1))
    layer_proj_grad = all_sum(layer_proj_grad)
    vector = jnp.concatenate(
        [grad_query_gain.reshape(run, gain_cut), grad_key_gain.reshape(run, gain_cut)], axis=1
    )
    vector = jnp.pad(vector, ((0, 0), (0, shard_rows - 2 * gain_cut))).reshape(width)
    gain_sums = all_sum(
        jnp.stack(
            [
                grad_gain_zero,
                grad_gain_one,
                grad_gain_two,
                grad_gain_three,
                grad_gain_four,
                grad_gain_five,
                vector,
                jnp.zeros_like(vector),
            ],
            axis=1,
        )
    )
    return (
        layer_out,
        tokens_grad,
        table_grad,
        query_grad.reshape(shard_rows, query_all),
        key_grad.reshape(shard_rows, kv_width),
        value_grad.reshape(shard_rows, kv_width),
        output_grad.reshape(query_width, width),
        narrow[:, :rank],
        narrow[:, rank : 2 * rank],
        gate_grad,
        up_grad,
        down_grad.reshape(hidden_width, width),
        narrow[:, 2 * rank :],
        layer_proj_grad,
        gain_sums[:, :6],
        gain_sums[:gain_cut, 6],
        gain_sums[gain_cut : 2 * gain_cut, 6],
    )


def solution(mesh):
    placed = (
        P("slot", ("ctx", "wsh"), None),
        P("slot", ("ctx", "wsh"), None),
        P("slot"),
        P("slot", ("ctx", "wsh")),
        P("slot", ("ctx", "wsh")),
        P(("slot", "ctx", "wsh"), None),
        P("wsh", None),
        P("wsh", None),
        P("wsh", None),
        P("wsh", None),
        P("wsh", None),
        P("wsh", None),
        P("wsh", None),
        P("wsh", None),
        P("wsh", None),
        P("wsh", None),
        P("wsh", None),
        P("wsh", None),
        P("wsh"),
        P("wsh"),
    )
    return jax.shard_map(
        shards,
        mesh=mesh,
        in_specs=placed,
        out_specs=(
            P("slot", ("ctx", "wsh"), None),
            P("slot", ("ctx", "wsh"), None),
            P(("slot", "ctx", "wsh"), None),
            P("wsh", None),
            P("wsh", None),
            P("wsh", None),
            P("wsh", None),
            P("wsh", None),
            P("wsh", None),
            P("wsh", None),
            P("wsh", None),
            P("wsh", None),
            P("wsh", None),
            P("wsh", None),
            P("wsh", None),
            P("wsh"),
            P("wsh"),
        ),
        check_vma=False,
    )
```

```python
import functools
import math

import jax
import jax.numpy as jnp
from jax import lax
from jax.experimental import pallas as pl
from jax.experimental.pallas import tpu as pltpu
from jax.sharding import PartitionSpec as P

HEADS = 8
KV_HEADS = 2
HEAD_DIM = 256


EPSILON = 1e-06
ROPE_BASE = 1000000.0
HALF_ROOT = 0.7071067811865476
TANH_SCALE = 0.7978845608028654
NEGATIVE = -1e30
EMBED_SCALE = 16.0


def rms_norm(value, gain):
    return value * lax.rsqrt(jnp.mean(value * value, axis=-1, keepdims=True) + EPSILON) * gain


def gelu_tanh(value):
    return 0.5 * value * (1.0 + jnp.tanh(TANH_SCALE * (value + 0.044715 * value * value * value)))


def gated_product(pre_gate, other_side):
    return gelu_tanh(pre_gate) * other_side


def rotate(value, places):
    width_all = value.shape[-1]
    half_width = width_all // 2
    inverse = jnp.exp(
        -math.log(ROPE_BASE) * (2.0 * jnp.arange(half_width, dtype=jnp.float32) / width_all)
    )
    angles = places.astype(jnp.float32)[:, None] * inverse[None, :]
    cosine = jnp.cos(angles)[:, None, :]
    sine = jnp.sin(angles)[:, None, :]
    front = value[..., :half_width]
    behind = value[..., half_width:]
    return jnp.concatenate(
        [front * cosine - behind * sine, behind * cosine + front * sine], axis=-1
    )


def matmul(left, right):
    return jnp.dot(left, right, preferred_element_type=jnp.float32)


def times_transposed(left, right):
    return lax.dot_general(
        left, right, (((1,), (1,)), ((), ())), preferred_element_type=jnp.float32
    )


def over_rows(left, right):
    return lax.dot_general(
        left, right, (((0,), (0,)), ((), ())), preferred_element_type=jnp.float32
    )


LOW = jnp.bfloat16
WIDE = jnp.float32
EVERY = ("slot", "ctx", "wsh")
COPIES = ("slot", "ctx")


def after(value, *others):
    return lax.optimization_barrier((value, others))[0]


def exchange(value, axis):
    return lax.all_to_all(value, axis, 0, 0, tiled=True)


def spread(value, axis):
    size = lax.axis_size(axis)
    copies = jnp.broadcast_to(value[None], (size,) + value.shape)
    return exchange(copies.reshape((size * value.shape[0],) + value.shape[1:]), axis)


def collect(parts, axis):
    size = lax.axis_size(axis)
    received = exchange(parts, axis)
    received = received.reshape((size, parts.shape[0] // size) + parts.shape[1:])
    return jnp.sum(received.astype(WIDE), axis=0)


def swap(value, axis, bit):
    size = lax.axis_size(axis)
    return lax.ppermute(value, axis, [(i, i ^ bit) for i in range(size)])


def add_low(left, right):
    return (left.astype(WIDE) + right.astype(WIDE)).astype(LOW)


def gather_first(piece):
    if lax.axis_size("ctx") == 4:
        return [swap(piece, "ctx", 1), swap(piece, "ctx", 2)]
    return []


def gather_second(piece, first):
    if first:
        one, two = first
        half = piece.shape[0] // 2
        front = swap(one[:half], "ctx", 2)
        behind = swap(two[half:], "ctx", 1)
        return [piece, one, two, jnp.concatenate([front, behind], axis=0)]
    pieces = [piece]
    bit = 1
    while bit < lax.axis_size("ctx"):
        pieces = pieces + [swap(p, "ctx", bit) for p in pieces]
        bit *= 2
    return pieces


def reduce_first(pieces):
    if len(pieces) == 4:
        half = pieces[0].shape[0] // 2
        return [swap(pieces[3][:half], "ctx", 1), swap(pieces[3][half:], "ctx", 2)]
    return []


def reduce_second(pieces, first):
    if first:
        front, behind = first
        half = pieces[0].shape[0] // 2
        two = jnp.concatenate([add_low(pieces[2][:half], front), pieces[2][half:]], axis=0)
        one = jnp.concatenate([pieces[1][:half], add_low(pieces[1][half:], behind)], axis=0)
        return [swap(one, "ctx", 1), swap(two, "ctx", 2)]
    return []


def reduce_last(pieces, second):
    if second:
        one, two = second
        return (pieces[0].astype(WIDE) + one.astype(WIDE) + two.astype(WIDE)).astype(LOW)
    size = len(pieces)
    while size > 1:
        size //= 2
        pieces = [add_low(pieces[i], swap(pieces[size + i], "ctx", size)) for i in range(size)]
    return pieces[0]


def assemble_kernel(extent, cuts, own, *refs):
    step = pl.program_id(0)
    ins, outs = refs[:extent], refs[extent:]
    for number in range(extent):

        @pl.when(step == number)
        def _(number=number):
            for (begin, width), out in zip(cuts, outs):
                out[:, 0] = ins[number][:, :, begin : begin + width].astype(out.dtype)


def assemble(pieces, own, kind, cuts=None):
    count = len(pieces)
    outer, inner, width = pieces[0].shape
    cuts = cuts or [(0, width)]
    results = pl.pallas_call(
        functools.partial(assemble_kernel, count, cuts),
        grid_spec=pltpu.PrefetchScalarGridSpec(
            num_scalar_prefetch=1,
            grid=(count,),
            in_specs=[pl.BlockSpec((outer, inner, width), lambda i, o: (0, 0, 0))] * count,
            out_specs=[
                pl.BlockSpec((outer, 1, inner, w), lambda i, o: (0, lax.bitwise_xor(i, o[0]), 0, 0))
                for _, w in cuts
            ],
        ),
        out_shape=[jax.ShapeDtypeStruct((outer, count, inner, w), kind) for _, w in cuts],
    )(own, *pieces)
    return results


def halves(blocks):
    count = blocks.shape[0] // 2
    slot = lax.axis_index("slot")
    kept = lax.dynamic_slice_in_dim(blocks, slot * count, count, 0)
    given = lax.dynamic_slice_in_dim(blocks, (1 - slot) * count, count, 0)
    return kept, swap(given, "slot", 1)


def nearest(blocks):
    here = lax.axis_index("ctx")
    count = blocks.shape[0]
    return [lax.dynamic_index_in_dim(blocks, here ^ r, 0, False) for r in range(count)]


def last_gather(pieces):
    return pieces + [swap(p, "slot", 1) for p in pieces]


def contract_last(left, right):
    return lax.dot_general(left, right, (((1,), (1,)), ((), ())), preferred_element_type=WIDE)


def gelu_and_slope(value):
    inner = jnp.tanh(TANH_SCALE * (value + 0.044715 * value * value * value))
    slope = 0.5 * (1.0 + inner) + 0.5 * value * (1.0 - inner * inner) * TANH_SCALE * (
        1.0 + 3.0 * 0.044715 * value * value
    )
    return 0.5 * value * (1.0 + inner), slope


def ff_forward_kernel(piece, count, x_ref, pair_ref, down_ref, both_ref, hidden_ref, out_ref):
    step = pl.program_id(0)

    @pl.when(step < count)
    def _():
        both = contract_last(x_ref[...], pair_ref[...])
        both_ref[...] = both
        hidden = (gelu_tanh(both[:, :piece]) * both[:, piece:]).astype(LOW)
        hidden_ref[:, pl.ds(pl.multiple_of(step * piece, piece), piece)] = hidden

    @pl.when(step >= count)
    def _():
        out_ref[...] = jnp.dot(
            hidden_ref[...], down_ref[...], preferred_element_type=WIDE
        ).astype(LOW)


def ff_forward(x, pair, down, piece):
    rows, width = x.shape
    hidden = down.shape[0]
    count = hidden // piece
    cut = math.gcd(width, 512)

    def now(i):
        return jnp.minimum(i, count - 1)

    def then(i):
        return jnp.maximum(i - count, 0)

    return pl.pallas_call(
        functools.partial(ff_forward_kernel, piece, count),
        grid=(count + width // cut,),
        in_specs=[
            pl.BlockSpec((rows, width), lambda i: (0, 0)),
            pl.BlockSpec((2 * piece, width), lambda i: (now(i), 0)),
            pl.BlockSpec((hidden, cut), lambda i: (0, then(i))),
        ],
        out_specs=[
            pl.BlockSpec((rows, 2 * piece), lambda i: (0, now(i))),
            pl.BlockSpec((rows, hidden), lambda i: (0, 0)),
            pl.BlockSpec((rows, cut), lambda i: (0, then(i))),
        ],
        out_shape=[
            jax.ShapeDtypeStruct((rows, 2 * hidden), WIDE),
            jax.ShapeDtypeStruct((rows, hidden), LOW),
            jax.ShapeDtypeStruct((rows, width), LOW),
        ],
        cost_estimate=pl.CostEstimate(
            flops=6 * rows * width * hidden,
            bytes_accessed=6 * width * hidden + 10 * rows * hidden,
            transcendentals=rows * hidden,
        ),
    )(x, pair, down)


def ff_backward_kernel(piece, count, grad_ref, down_ref, both_ref, pair_ref, grad_both_ref, out_ref):
    step = pl.program_id(0)

    @pl.when(step < count)
    def _():
        grad_hidden = contract_last(grad_ref[...], down_ref[...])
        value, slope = gelu_and_slope(both_ref[:, :piece])
        start = pl.multiple_of(step * 2 * piece, piece)
        grad_both_ref[:, pl.ds(start, piece)] = (grad_hidden * both_ref[:, piece:] * slope).astype(LOW)
        start = pl.multiple_of(step * 2 * piece + piece, piece)
        grad_both_ref[:, pl.ds(start, piece)] = (grad_hidden * value).astype(LOW)

    @pl.when(step >= count)
    def _():
        out_ref[...] = jnp.dot(
            grad_both_ref[...], pair_ref[...], preferred_element_type=WIDE
        ).astype(LOW)


def ff_backward(grad, pair, down, both, piece):
    rows, width = grad.shape
    hidden = down.shape[0]
    count = hidden // piece
    cut = math.gcd(width, 512)

    def now(i):
        return jnp.minimum(i, count - 1)

    def then(i):
        return jnp.maximum(i - count, 0)

    return pl.pallas_call(
        functools.partial(ff_backward_kernel, piece, count),
        grid=(count + width // cut,),
        in_specs=[
            pl.BlockSpec((rows, width), lambda i: (0, 0)),
            pl.BlockSpec((piece, width), lambda i: (now(i), 0)),
            pl.BlockSpec((rows, 2 * piece), lambda i: (0, now(i))),
            pl.BlockSpec((2 * hidden, cut), lambda i: (0, then(i))),
        ],
        out_specs=[
            pl.BlockSpec((rows, 2 * hidden), lambda i: (0, 0)),
            pl.BlockSpec((rows, cut), lambda i: (0, then(i))),
        ],
        out_shape=[
            jax.ShapeDtypeStruct((rows, 2 * hidden), LOW),
            jax.ShapeDtypeStruct((rows, width), LOW),
        ],
        cost_estimate=pl.CostEstimate(
            flops=6 * rows * width * hidden,
            bytes_accessed=6 * width * hidden + 12 * rows * hidden,
            transcendentals=rows * hidden,
        ),
    )(grad, down, both, pair)


def widen_kernel(places, source, gate, up):
    gate[...] = source[0, 0, 0].astype(WIDE)
    up[...] = source[0, 0, 1].astype(WIDE)


def widen_pair(pieces, places):
    parts, run, _, rows, width = pieces.shape
    return pl.pallas_call(
        widen_kernel,
        grid_spec=pltpu.PrefetchScalarGridSpec(
            num_scalar_prefetch=1,
            grid=(run, parts),
            in_specs=[pl.BlockSpec((1, 1, 2, rows, width), lambda k, r, p: (r, k, 0, 0, 0))],
            out_specs=[pl.BlockSpec((rows, width), lambda k, r, p: (0, p[k] * parts + r))] * 2,
        ),
        out_shape=[jax.ShapeDtypeStruct((rows, width * parts * run), WIDE)] * 2,
        cost_estimate=pl.CostEstimate(flops=0, bytes_accessed=6 * pieces.size, transcendentals=0),
    )(places, pieces)


def shift_blocks(make):
    run = lax.axis_size("wsh")
    here = lax.axis_index("wsh")
    received = []
    for k in range(run):
        block = make((here + k) % run)
        if k:
            block = lax.ppermute(block, "wsh", [(i, (i + k) % run) for i in range(run)])
        received.append(block)
    return received


def shift_exchange(make):
    run = lax.axis_size("wsh")
    order = (lax.axis_index("wsh") - jnp.arange(run, dtype=jnp.int32)) % run
    return jnp.take(jnp.stack(shift_blocks(make)), order, axis=0)


def place_kernel(places, *refs):
    step = pl.program_id(0)
    sources, out = refs[:-1], refs[-1]
    for number, source in enumerate(sources):

        @pl.when(step == number)
        def _(source=source):
            out[...] = source[...]


def place_columns(blocks, places):
    rows, width = blocks[0].shape
    count = len(blocks)
    return pl.pallas_call(
        place_kernel,
        grid_spec=pltpu.PrefetchScalarGridSpec(
            num_scalar_prefetch=1,
            grid=(count,),
            in_specs=[pl.BlockSpec((rows, width), lambda k, p: (0, 0))] * count,
            out_specs=pl.BlockSpec((rows, width), lambda k, p: (0, p[k])),
        ),
        out_shape=jax.ShapeDtypeStruct((rows, width * count), blocks[0].dtype),
        cost_estimate=pl.CostEstimate(
            flops=0, bytes_accessed=4 * count * blocks[0].size, transcendentals=0
        ),
    )(places, *blocks)


def entry(stacked):
    return lambda index: lax.dynamic_index_in_dim(stacked, index, 0, False)


def widen_heads_kernel(run, query_width, own, *refs):
    step = pl.program_id(0)
    sources, (query, key, value) = refs[:-3], refs[-3:]
    group = run // KV_HEADS
    for place, source in enumerate(sources):

        @pl.when(step == place)
        def _(source=source):
            for k in range(run):
                begin = k * query_width
                query[:, begin : begin + query_width] = source[k, :, :query_width].astype(WIDE)
            for number, out in enumerate((key, value)):
                begin = query_width + number * HEAD_DIM
                for head in range(KV_HEADS):
                    total = source[head * group, :, begin : begin + HEAD_DIM].astype(WIDE)
                    for k in range(1, group):
                        total += source[head * group + k, :, begin : begin + HEAD_DIM].astype(WIDE)
                    out[:, head * HEAD_DIM : (head + 1) * HEAD_DIM] = total


def widen_heads(pieces, own, query_width):
    parts = len(pieces)
    run, rows, columns = pieces[0].shape
    widths = (HEADS * HEAD_DIM, KV_HEADS * HEAD_DIM, KV_HEADS * HEAD_DIM)
    return pl.pallas_call(
        functools.partial(widen_heads_kernel, run, query_width),
        grid_spec=pltpu.PrefetchScalarGridSpec(
            num_scalar_prefetch=1,
            grid=(parts,),
            in_specs=[pl.BlockSpec((run, rows, columns), lambda r, o: (0, 0, 0))] * parts,
            out_specs=[
                pl.BlockSpec((rows, w), lambda r, o: (lax.bitwise_xor(r, o[0]), 0)) for w in widths
            ],
        ),
        out_shape=[jax.ShapeDtypeStruct((rows * parts, w), WIDE) for w in widths],
        cost_estimate=pl.CostEstimate(
            flops=0, bytes_accessed=6 * parts * pieces[0].size, transcendentals=0
        ),
    )(own, *pieces)


def shards(
    tokens,
    cotangent,
    lengths,
    positions,
    token_ids,
    per_layer_table,
    w_query,
    w_key,
    w_value,
    w_output,
    laurel_left,
    laurel_right,
    w_gate,
    w_up,
    w_down,
    w_layer_gate,
    w_layer_proj,
    norm_gains,
    query_gain,
    key_gain,
):
    rows_dev, width = tokens.shape[1:]
    run = lax.axis_size("wsh")
    contexts = lax.axis_size("ctx")
    parts = 2 * contexts
    chip = lax.axis_index(COPIES)
    shard_rows = width // run
    heads_here = HEADS // run
    groups = HEADS // KV_HEADS
    query_width = heads_here * HEAD_DIM
    head_width = query_width + 2 * HEAD_DIM
    hidden_width = w_gate.shape[1] // run
    head_piece = shard_rows // parts
    piece = hidden_width // parts
    rank = laurel_left.shape[1]
    places = ((lax.axis_index("wsh") - jnp.arange(run)) % run).astype(jnp.int32)
    gain_cut = query_gain.shape[0]

    def joined(make):
        return place_columns(shift_blocks(make), places)

    def share(weight):
        return lax.dynamic_slice_in_dim(weight, chip * head_piece, head_piece, 0)

    query_rows, key_rows, value_rows = share(w_query), share(w_key), share(w_value)

    indices = shift_exchange(lambda k: jnp.concatenate([token_ids, positions], axis=0))
    small = jnp.concatenate(
        [
            norm_gains.T,
            jnp.pad(
                jnp.concatenate([query_gain, key_gain])[None],
                ((0, 1), (0, shard_rows - 2 * gain_cut)),
            ),
        ],
        axis=0,
    )
    proj_rows = w_layer_proj.shape[0]
    proj_share = lax.dynamic_slice_in_dim(w_layer_proj, chip * (width // parts), width // parts, 1)
    common = jnp.concatenate(
        [
            share(laurel_left),
            share(laurel_right),
            share(w_layer_gate),
            proj_share.reshape(head_piece, -1),
        ],
        axis=1,
    )
    fetch_width = head_width + common.shape[1]
    small_flat = jnp.pad(small.reshape(-1), (0, -small.size % fetch_width)).reshape(-1, fetch_width)
    small_flat = jnp.pad(small_flat, ((0, 16 - small_flat.shape[0]), (0, 0)))
    common, query_rows, key_rows, value_rows, small_flat, indices = lax.optimization_barrier(
        (common, query_rows, key_rows, value_rows, small_flat, indices)
    )

    def head_block(index):
        kv = index * heads_here // groups * HEAD_DIM
        block = jnp.concatenate(
            [
                lax.dynamic_slice_in_dim(query_rows, index * query_width, query_width, 1),
                lax.dynamic_slice_in_dim(key_rows, kv, HEAD_DIM, 1),
                lax.dynamic_slice_in_dim(value_rows, kv, HEAD_DIM, 1),
                common,
            ],
            axis=1,
        )
        return jnp.concatenate([small_flat, block], axis=0)

    head_share = shift_exchange(head_block)
    small_all = head_share[:, :16].reshape(run, -1)[:, : small.size].reshape(run, 8, shard_rows)
    fetched = lax.all_gather(head_share[:, 16:], COPIES, axis=0)
    w_heads = fetched[:, :, :, :head_width]
    proj_at = head_width + 2 * rank + w_layer_gate.shape[1]
    layer_proj_full = fetched[:, :, :, proj_at:].reshape(parts, run, proj_rows, width // parts)
    layer_proj_full = layer_proj_full.transpose(1, 2, 0, 3).reshape(run * proj_rows, width)
    laurel_weights = fetched[:, :, :, head_width:proj_at].transpose(1, 0, 2, 3).reshape(width, -1)
    left_full = laurel_weights[:, :rank]
    right_full = laurel_weights[:, rank : 2 * rank]
    layer_gate_full = laurel_weights[:, 2 * rank :]
    w_heads = w_heads.transpose(1, 0, 2, 3).reshape(width, head_width)

    gains_full = small_all.transpose(1, 0, 2).reshape(8, width).astype(WIDE)
    query_gain_full = small_all[:, 6, :gain_cut].reshape(HEAD_DIM).astype(WIDE)
    key_gain_full = small_all[:, 6, gain_cut : 2 * gain_cut].reshape(HEAD_DIM).astype(WIDE)
    tokens_run = spread(tokens[0], "wsh")

    indices = indices[None]
    bit = 1
    while bit < contexts:
        indices = jnp.concatenate([indices, swap(indices, "ctx", bit)], axis=0)
        bit *= 2
    run_places = indices[0, :, 1].reshape(-1)
    here_ctx = lax.axis_index("ctx")
    context_order = jnp.bitwise_xor(jnp.arange(contexts, dtype=jnp.int32), here_ctx)
    key_places = jnp.take(indices[:, :, 1], context_order, axis=0).reshape(-1)
    own_ids = indices[:, :, 0].reshape(-1)
    all_ids = jnp.concatenate([own_ids, swap(own_ids, "slot", 1)])
    length = lengths[0]

    vocab_rows = per_layer_table.shape[0]
    vocab_first = lax.axis_index(EVERY) * vocab_rows
    vocab_range = jnp.arange(vocab_rows, dtype=jnp.int32)

    def one_hot():
        return ((all_ids - vocab_first)[:, None] == vocab_range[None, :]).astype(LOW)

    table_rows = matmul(one_hot(), per_layer_table).astype(LOW)
    def pair_block(index):
        first = index * hidden_width + chip * piece
        gate_cut = lax.dynamic_slice_in_dim(w_gate, first, piece, 1)
        up_cut = lax.dynamic_slice_in_dim(w_up, first, piece, 1)
        gate_cut, up_cut = after((gate_cut, up_cut), tokens_run)
        return jnp.concatenate([gate_cut.T, up_cut.T], axis=0)

    pair_share = joined(pair_block)
    normed_run = rms_norm(tokens_run.astype(WIDE), gains_full[0]).astype(LOW)
    tokens_f = tokens[0].astype(WIDE)
    normed = rms_norm(tokens_f, gains_full[0])
    normed_low = normed.astype(LOW)
    total_rows = run * rows_dev
    projected = matmul(normed_run, w_heads)
    query = projected[:, :query_width]
    key = projected[:, query_width : query_width + HEAD_DIM]
    value = projected[:, query_width + HEAD_DIM :]

    def query_path(raw, gain):
        return rotate(rms_norm(raw.reshape(total_rows, heads_here, HEAD_DIM), gain), run_places)

    def key_path(raw, gain):
        return rotate(rms_norm(raw.reshape(total_rows, 1, HEAD_DIM), gain), run_places)[:, 0]

    def value_path(raw):
        return rms_norm(raw, 1.0)

    k_low = key_path(key, key_gain_full).astype(LOW)
    v_low = value_path(value).astype(LOW)
    keys_values = spread(jnp.concatenate([k_low, v_low], axis=1), "ctx")
    keys_values, table_rows, pair_share = lax.optimization_barrier(
        (keys_values, table_rows, pair_share)
    )
    pair_weight = lax.all_gather(pair_share, COPIES, axis=0, tiled=True)
    half = table_rows.shape[0] // 2
    looked_up = add_low(table_rows[:half], swap(table_rows[half:], "slot", 1))
    bit = contexts // 2
    while bit:
        half = looked_up.shape[0] // 2
        looked_up = add_low(looked_up[:half], swap(looked_up[half:], "ctx", bit))
        bit //= 2
    looked_up = looked_up.reshape(run, rows_dev, -1)
    q_low = query_path(query, query_gain_full).astype(LOW)
    keys_all = keys_values[:, :HEAD_DIM]
    values_all = keys_values[:, HEAD_DIM:]
    allowed = (key_places[None, :] <= run_places[:, None]) & (key_places < length)[None, :]
    scores = jnp.einsum("qhd,td->hqt", q_low, keys_all, preferred_element_type=WIDE)
    scores = jnp.where(allowed[None], scores, NEGATIVE)
    top = jnp.max(scores, axis=-1, keepdims=True)
    raised = jnp.exp(scores - top)
    probs = raised / jnp.sum(raised, axis=-1, keepdims=True)
    attended = jnp.einsum(
        "hqt,td->qhd", probs.astype(LOW), values_all, preferred_element_type=WIDE
    )
    attended_low = attended.astype(LOW).reshape(total_rows, query_width)
    attn_proj = collect(matmul(attended_low, w_output).astype(LOW), "wsh")
    attn_proj, looked_up = lax.optimization_barrier((attn_proj, looked_up))
    layer_input = EMBED_SCALE * jnp.sum(shift_exchange(entry(looked_up)).astype(WIDE), axis=0)

    first_sum = tokens_f + rms_norm(attn_proj, gains_full[1])
    low_rank_low = matmul(normed_low, left_full).astype(LOW)
    laurel_out = times_transposed(low_rank_low, right_full)
    laurel = normed + rms_norm(laurel_out, gains_full[2])
    mixed = (first_sum + laurel) * HALF_ROOT
    ff_in_low = rms_norm(mixed, gains_full[3]).astype(LOW)

    ff_run = spread(ff_in_low, "wsh")
    aligned = piece % 128 == 0
    if aligned:
        both, hidden_low, ff_part = ff_forward(ff_run, pair_weight, w_down, piece)
    else:
        both = times_transposed(ff_run, pair_weight)
        both_parts = both.reshape(total_rows, parts, 2, piece)
        gate = both_parts[:, :, 0].reshape(total_rows, hidden_width)
        upward = both_parts[:, :, 1].reshape(total_rows, hidden_width)
        hidden_low = gated_product(gate, upward).astype(LOW)
        ff_part = matmul(hidden_low, w_down).astype(LOW)
    ff_out = collect(ff_part, "wsh")
    ff_out, layer_input = lax.optimization_barrier((ff_out, layer_input))
    third_sum = mixed + rms_norm(ff_out, gains_full[4])
    third_low = third_sum.astype(LOW)

    layer_gate = matmul(third_low, layer_gate_full)
    gated_low = gated_product(layer_gate, layer_input).astype(LOW)
    layer_proj = matmul(gated_low, layer_proj_full)
    result = third_sum + rms_norm(layer_proj, gains_full[5])
    layer_out = result.astype(LOW)[None]

    valid = (positions[0] < length).astype(WIDE)
    grad_out = cotangent[0].astype(WIDE) * valid[:, None]
    _, pullback = jax.vjp(rms_norm, layer_proj, gains_full[5])
    grad_proj, grad_gain_five = pullback(grad_out)
    grad_proj_low = grad_proj.astype(LOW)
    grad_gated = times_transposed(grad_proj_low, layer_proj_full)
    _, pullback = jax.vjp(gated_product, layer_gate, layer_input)
    grad_lgate, grad_input = pullback(grad_gated)
    grad_lgate_low = grad_lgate.astype(LOW)
    grad_input_low = grad_input.astype(LOW)
    grad_third = grad_out + times_transposed(grad_lgate_low, layer_gate_full)
    _, pullback = jax.vjp(rms_norm, ff_out, gains_full[4])
    grad_ff, grad_gain_four = pullback(grad_third)
    grad_ff_low = grad_ff.astype(LOW)

    grad_ff_run = spread(grad_ff_low, "wsh")
    if aligned:
        grad_both, ff_part = ff_backward(grad_ff_run, pair_weight, w_down, both, piece)
    else:
        grad_hidden = times_transposed(grad_ff_run, w_down)
        _, pullback = jax.vjp(gated_product, gate, upward)
        grad_gate, grad_upward = pullback(grad_hidden)
        grad_both = jnp.stack(
            [
                grad_gate.reshape(total_rows, parts, piece),
                grad_upward.reshape(total_rows, parts, piece),
            ],
            axis=2,
        )
        grad_both = grad_both.reshape(total_rows, 2 * hidden_width).astype(LOW)
        ff_part = matmul(grad_both, pair_weight).astype(LOW)
    grad_ff_in = collect(ff_part, "wsh")
    pair_part = over_rows(after(grad_both, ff_part), ff_run).astype(LOW)
    grad_ff_in, pair_part = lax.optimization_barrier((grad_ff_in, pair_part))
    grad_input_low = after(grad_input_low, pair_part)
    every_grad = shift_exchange(lambda k: grad_input_low).reshape(total_rows, -1)
    pair_own = lax.psum_scatter(pair_part, COPIES, scatter_dimension=0, tiled=True)
    _, pullback = jax.vjp(rms_norm, mixed, gains_full[3])
    grad_mixed_norm, grad_gain_three = pullback(grad_ff_in)
    grad_branch = (grad_third + grad_mixed_norm) * HALF_ROOT
    _, pullback = jax.vjp(rms_norm, attn_proj, gains_full[1])
    grad_attn, grad_gain_one = pullback(grad_branch)
    grad_attn_low = grad_attn.astype(LOW)
    grad_attn_run = spread(grad_attn_low, "wsh")
    down_part = over_rows(after(hidden_low, grad_attn_low), grad_ff_run).astype(LOW)
    grad_attn_run, down_part = lax.optimization_barrier((grad_attn_run, down_part))

    def pair_back(index):
        block = lax.dynamic_slice_in_dim(pair_own, index * shard_rows, shard_rows, 1)
        return block.reshape(2, piece, shard_rows).transpose(0, 2, 1)

    _, pullback = jax.vjp(rms_norm, laurel_out, gains_full[2])
    grad_laurel, grad_gain_two = pullback(grad_branch)
    grad_laurel_low = grad_laurel.astype(LOW)
    grad_rank_low = matmul(grad_laurel_low, right_full).astype(LOW)

    left_grad = over_rows(normed_low, grad_rank_low)
    right_grad = over_rows(grad_laurel_low, low_rank_low)
    layer_gate_grad = over_rows(third_low, grad_lgate_low)
    layer_proj_grad = over_rows(gated_low, grad_proj_low)

    narrow = jnp.concatenate([left_grad, right_grad, layer_gate_grad], axis=1)
    narrow = narrow.reshape(run, shard_rows, -1)
    narrow_columns = narrow.shape[2]
    layer_proj_grad = layer_proj_grad.reshape(run, shard_rows, -1)
    sums = jnp.concatenate([narrow, layer_proj_grad], axis=2).astype(LOW)
    sums = jnp.sum(shift_exchange(entry(after(sums, grad_attn_run))).astype(WIDE), axis=0).astype(LOW)

    grad_att_low = times_transposed(grad_attn_run, w_output).astype(LOW)
    grad_att = grad_att_low.reshape(total_rows, heads_here, HEAD_DIM)
    row_delta = jnp.sum(grad_att.astype(WIDE) * attended, axis=-1)
    grad_probs = jnp.einsum("qhd,td->hqt", grad_att, values_all, preferred_element_type=WIDE)
    grad_scores = (probs * (grad_probs - row_delta.T[:, :, None])).astype(LOW)
    key_part = jnp.einsum("hqt,qhd->td", grad_scores, q_low, preferred_element_type=WIDE)
    value_part = jnp.einsum("hqt,qhd->td", probs.astype(LOW), grad_att, preferred_element_type=WIDE)
    kv_part = jnp.concatenate([key_part, value_part], axis=1).astype(LOW)
    kv_part, pair_own = lax.optimization_barrier((kv_part, pair_own))
    kv_sum = collect(kv_part, "ctx")
    pair_blocks = jnp.stack(shift_blocks(pair_back))
    down_grad = lax.psum(after(down_part, pair_own), COPIES)
    output_part = over_rows(attended_low, grad_attn_run).astype(LOW)
    output_kept, output_given = halves(output_part.reshape(parts, -1, width))
    kv_sum, pair_blocks, output_kept, output_given, sums = lax.optimization_barrier(
        (kv_sum, pair_blocks, output_kept, output_given, sums)
    )
    pair_all = lax.all_gather(pair_blocks, COPIES, axis=0)
    output_pieces = nearest(add_low(output_kept, output_given))
    output_first = reduce_first(output_pieces)
    sums = add_low(sums, swap(sums, "slot", 1))
    grad_q_rot = jnp.einsum("hqt,td->qhd", grad_scores, keys_all, preferred_element_type=WIDE)
    _, pullback = jax.vjp(query_path, query, query_gain_full)
    grad_query, grad_query_gain = pullback(grad_q_rot)
    _, pullback = jax.vjp(key_path, key, key_gain_full)
    grad_key, grad_key_gain = pullback(kv_sum[:, :HEAD_DIM])
    _, pullback = jax.vjp(value_path, value)
    (grad_value,) = pullback(kv_sum[:, HEAD_DIM:])
    grad_heads = jnp.concatenate([grad_query, grad_key, grad_value], axis=1).astype(LOW)
    heads_part = over_rows(normed_run, grad_heads).astype(LOW)
    heads_part = heads_part.reshape(run, parts, head_piece, head_width).transpose(1, 0, 2, 3)
    heads_kept, heads_given = halves(heads_part)
    normed_part = times_transposed(grad_heads, w_heads).astype(LOW)
    normed_part, output_first, heads_kept, heads_given, sums = lax.optimization_barrier(
        (normed_part, output_first, heads_kept, heads_given, sums)
    )
    grad_run = collect(normed_part, "wsh")
    output_second = reduce_second(output_pieces, output_first)
    heads_pieces = nearest(add_low(heads_kept, heads_given))
    heads_second = reduce_second(heads_pieces, reduce_first(heads_pieces))
    heads_own = reduce_last(heads_pieces, heads_second)
    every_grad = after(every_grad, normed_part)
    bit = 1
    while bit < contexts:
        every_grad = jnp.concatenate([every_grad, swap(every_grad, "ctx", bit)], axis=0)
        bit *= 2
    every_grad = jnp.concatenate([every_grad, swap(every_grad, "slot", 1)], axis=0)
    table_grad = EMBED_SCALE * over_rows(one_hot(), every_grad)
    grad_run, output_second, heads_own, table_grad = lax.optimization_barrier(
        (grad_run, output_second, heads_own, table_grad)
    )
    if aligned:
        gate_grad, up_grad = widen_pair(pair_all, places)
    else:
        pair_all = jnp.take(pair_all, places, axis=1)
        pair_all = pair_all.transpose(2, 3, 1, 0, 4).reshape(2, shard_rows, -1).astype(WIDE)
        gate_grad, up_grad = pair_all[0], pair_all[1]
    output_own = reduce_last(output_pieces, output_second)
    own = jnp.full((1,), chip, jnp.int32)
    bit = 1
    while bit < contexts:
        sums = add_low(sums, swap(sums, "ctx", bit))
        bit *= 2
    sums = sums.astype(WIDE)
    narrow = sums[:, :narrow_columns]
    layer_proj_grad = sums[:, narrow_columns:].reshape(proj_rows, width)
    grad_normed = (
        grad_run
        + times_transposed(grad_rank_low, left_full)
        + grad_branch
    )
    _, pullback = jax.vjp(rms_norm, tokens_f, gains_full[0])
    grad_tokens, grad_gain_zero = pullback(grad_normed)
    tokens_grad = (grad_tokens + grad_branch).astype(LOW)[None]

    output_all = last_gather(gather_second(output_own, gather_first(output_own)))
    (output_grad,) = assemble([p[None] for p in output_all], own, WIDE)
    heads_own = shift_exchange(entry(heads_own))
    heads_all = last_gather(gather_second(heads_own, gather_first(heads_own)))
    query_grad, key_grad, value_grad = widen_heads(heads_all, own, query_width)

    vector = jnp.concatenate(
        [grad_query_gain.reshape(run, gain_cut), grad_key_gain.reshape(run, gain_cut)], axis=1
    )
    vector = jnp.pad(vector, ((0, 0), (0, shard_rows - 2 * gain_cut))).reshape(width)
    gain_sums = jnp.stack(
        [
            grad_gain_zero,
            grad_gain_one,
            grad_gain_two,
            grad_gain_three,
            grad_gain_four,
            grad_gain_five,
            vector,
            jnp.zeros_like(vector),
        ]
    )
    gain_sums = gain_sums.reshape(8, run, shard_rows).transpose(1, 0, 2)
    gain_sums = jnp.sum(shift_exchange(entry(gain_sums)), axis=0)
    gain_sums = gain_sums + swap(gain_sums, "slot", 1)
    bit = 1
    while bit < contexts:
        gain_sums = gain_sums + swap(gain_sums, "ctx", bit)
        bit *= 2
    return (
        layer_out,
        tokens_grad,
        table_grad,
        query_grad,
        key_grad,
        value_grad,
        output_grad.reshape(query_width, width),
        narrow[:, :rank],
        narrow[:, rank : 2 * rank],
        gate_grad,
        up_grad,
        down_grad.astype(WIDE),
        narrow[:, 2 * rank :],
        layer_proj_grad,
        gain_sums[:6].T,
        gain_sums[6, :gain_cut],
        gain_sums[6, gain_cut : 2 * gain_cut],
    )


def solution(mesh):
    placed = (
        P("slot", ("ctx", "wsh"), None),
        P("slot", ("ctx", "wsh"), None),
        P("slot"),
        P("slot", ("ctx", "wsh")),
        P("slot", ("ctx", "wsh")),
        P(("slot", "ctx", "wsh"), None),
        P("wsh", None),
        P("wsh", None),
        P("wsh", None),
        P("wsh", None),
        P("wsh", None),
        P("wsh", None),
        P("wsh", None),
        P("wsh", None),
        P("wsh", None),
        P("wsh", None),
        P("wsh", None),
        P("wsh", None),
        P("wsh"),
        P("wsh"),
    )
    return jax.shard_map(
        shards,
        mesh=mesh,
        in_specs=placed,
        out_specs=(
            P("slot", ("ctx", "wsh"), None),
            P("slot", ("ctx", "wsh"), None),
            P(("slot", "ctx", "wsh"), None),
            P("wsh", None),
            P("wsh", None),
            P("wsh", None),
            P("wsh", None),
            P("wsh", None),
            P("wsh", None),
            P("wsh", None),
            P("wsh", None),
            P("wsh", None),
            P("wsh", None),
            P("wsh", None),
            P("wsh", None),
            P("wsh"),
            P("wsh"),
        ),
        check_vma=False,
    )
```

```python
import functools
import math

import jax
import jax.numpy as jnp
from jax import lax
from jax.experimental import pallas as pl
from jax.experimental.pallas import tpu as pltpu
from jax.sharding import PartitionSpec as P

HEADS = 8
KV_HEADS = 2
HEAD_DIM = 256


EPSILON = 1e-06
ROPE_BASE = 1000000.0
HALF_ROOT = 0.7071067811865476
TANH_SCALE = 0.7978845608028654
NEGATIVE = -1e30
EMBED_SCALE = 16.0


def rms_norm(value, gain):
    return value * lax.rsqrt(jnp.mean(value * value, axis=-1, keepdims=True) + EPSILON) * gain


def gelu_tanh(value):
    return 0.5 * value * (1.0 + jnp.tanh(TANH_SCALE * (value + 0.044715 * value * value * value)))


def gated_product(pre_gate, other_side):
    return gelu_tanh(pre_gate) * other_side


def rotate(value, places):
    width_all = value.shape[-1]
    half_width = width_all // 2
    inverse = jnp.exp(
        -math.log(ROPE_BASE) * (2.0 * jnp.arange(half_width, dtype=jnp.float32) / width_all)
    )
    angles = places.astype(jnp.float32)[:, None] * inverse[None, :]
    cosine = jnp.cos(angles)[:, None, :]
    sine = jnp.sin(angles)[:, None, :]
    front = value[..., :half_width]
    behind = value[..., half_width:]
    return jnp.concatenate(
        [front * cosine - behind * sine, behind * cosine + front * sine], axis=-1
    )


def matmul(left, right):
    return jnp.dot(left, right, preferred_element_type=jnp.float32)


def times_transposed(left, right):
    return lax.dot_general(
        left, right, (((1,), (1,)), ((), ())), preferred_element_type=jnp.float32
    )


def over_rows(left, right):
    return lax.dot_general(
        left, right, (((0,), (0,)), ((), ())), preferred_element_type=jnp.float32
    )


LOW = jnp.bfloat16
WIDE = jnp.float32
EVERY = ("slot", "ctx", "wsh")
COPIES = ("slot", "ctx")


def after(value, *others):
    return lax.optimization_barrier((value, others))[0]


def exchange(value, axis):
    return lax.all_to_all(value, axis, 0, 0, tiled=True)


def spread(value, axis):
    size = lax.axis_size(axis)
    copies = jnp.broadcast_to(value[None], (size,) + value.shape)
    return exchange(copies.reshape((size * value.shape[0],) + value.shape[1:]), axis)


def collect(parts, axis):
    size = lax.axis_size(axis)
    received = exchange(parts, axis)
    received = received.reshape((size, parts.shape[0] // size) + parts.shape[1:])
    return jnp.sum(received.astype(WIDE), axis=0)


def swap(value, axis, bit):
    size = lax.axis_size(axis)
    return lax.ppermute(value, axis, [(i, i ^ bit) for i in range(size)])


def add_low(left, right):
    return (left.astype(WIDE) + right.astype(WIDE)).astype(LOW)


def gather_first(piece):
    if lax.axis_size("ctx") == 4:
        return [swap(piece, "ctx", 1), swap(piece, "ctx", 2)]
    return []


def gather_second(piece, first):
    if first:
        one, two = first
        half = piece.shape[0] // 2
        front = swap(one[:half], "ctx", 2)
        behind = swap(two[half:], "ctx", 1)
        return [piece, one, two, jnp.concatenate([front, behind], axis=0)]
    pieces = [piece]
    bit = 1
    while bit < lax.axis_size("ctx"):
        pieces = pieces + [swap(p, "ctx", bit) for p in pieces]
        bit *= 2
    return pieces


def reduce_first(pieces):
    if len(pieces) == 4:
        half = pieces[0].shape[0] // 2
        return [swap(pieces[3][:half], "ctx", 1), swap(pieces[3][half:], "ctx", 2)]
    return []


def reduce_second(pieces, first):
    if first:
        front, behind = first
        half = pieces[0].shape[0] // 2
        two = jnp.concatenate([add_low(pieces[2][:half], front), pieces[2][half:]], axis=0)
        one = jnp.concatenate([pieces[1][:half], add_low(pieces[1][half:], behind)], axis=0)
        return [swap(one, "ctx", 1), swap(two, "ctx", 2)]
    return []


def reduce_last(pieces, second):
    if second:
        one, two = second
        return (pieces[0].astype(WIDE) + one.astype(WIDE) + two.astype(WIDE)).astype(LOW)
    size = len(pieces)
    while size > 1:
        size //= 2
        pieces = [add_low(pieces[i], swap(pieces[size + i], "ctx", size)) for i in range(size)]
    return pieces[0]


def assemble_kernel(extent, cuts, own, *refs):
    step = pl.program_id(0)
    ins, outs = refs[:extent], refs[extent:]
    for number in range(extent):

        @pl.when(step == number)
        def _(number=number):
            for (begin, width), out in zip(cuts, outs):
                out[:, 0] = ins[number][:, :, begin : begin + width].astype(out.dtype)


def assemble(pieces, own, kind, cuts=None):
    count = len(pieces)
    outer, inner, width = pieces[0].shape
    cuts = cuts or [(0, width)]
    results = pl.pallas_call(
        functools.partial(assemble_kernel, count, cuts),
        grid_spec=pltpu.PrefetchScalarGridSpec(
            num_scalar_prefetch=1,
            grid=(count,),
            in_specs=[pl.BlockSpec((outer, inner, width), lambda i, o: (0, 0, 0))] * count,
            out_specs=[
                pl.BlockSpec((outer, 1, inner, w), lambda i, o: (0, lax.bitwise_xor(i, o[0]), 0, 0))
                for _, w in cuts
            ],
        ),
        out_shape=[jax.ShapeDtypeStruct((outer, count, inner, w), kind) for _, w in cuts],
    )(own, *pieces)
    return results


def halves(blocks):
    count = blocks.shape[0] // 2
    slot = lax.axis_index("slot")
    kept = lax.dynamic_slice_in_dim(blocks, slot * count, count, 0)
    given = lax.dynamic_slice_in_dim(blocks, (1 - slot) * count, count, 0)
    return kept, swap(given, "slot", 1)


def nearest(blocks):
    here = lax.axis_index("ctx")
    count = blocks.shape[0]
    return [lax.dynamic_index_in_dim(blocks, here ^ r, 0, False) for r in range(count)]


def last_gather(pieces):
    return pieces + [swap(p, "slot", 1) for p in pieces]


def contract_last(left, right):
    return lax.dot_general(left, right, (((1,), (1,)), ((), ())), preferred_element_type=WIDE)


def gelu_and_slope(value):
    inner = jnp.tanh(TANH_SCALE * (value + 0.044715 * value * value * value))
    slope = 0.5 * (1.0 + inner) + 0.5 * value * (1.0 - inner * inner) * TANH_SCALE * (
        1.0 + 3.0 * 0.044715 * value * value
    )
    return 0.5 * value * (1.0 + inner), slope


def ff_forward_kernel(piece, count, x_ref, pair_ref, down_ref, both_ref, hidden_ref, out_ref):
    step = pl.program_id(0)

    @pl.when(step < count)
    def _():
        both = contract_last(x_ref[...], pair_ref[...])
        both_ref[...] = both
        hidden = (gelu_tanh(both[:, :piece]) * both[:, piece:]).astype(LOW)
        hidden_ref[:, pl.ds(pl.multiple_of(step * piece, piece), piece)] = hidden

    @pl.when(step >= count)
    def _():
        out_ref[...] = jnp.dot(
            hidden_ref[...], down_ref[...], preferred_element_type=WIDE
        ).astype(LOW)


def ff_forward(x, pair, down, piece):
    rows, width = x.shape
    hidden = down.shape[0]
    count = hidden // piece
    cut = math.gcd(width, 512)

    def now(i):
        return jnp.minimum(i, count - 1)

    def then(i):
        return jnp.maximum(i - count, 0)

    return pl.pallas_call(
        functools.partial(ff_forward_kernel, piece, count),
        grid=(count + width // cut,),
        in_specs=[
            pl.BlockSpec((rows, width), lambda i: (0, 0)),
            pl.BlockSpec((2 * piece, width), lambda i: (now(i), 0)),
            pl.BlockSpec((hidden, cut), lambda i: (0, then(i))),
        ],
        out_specs=[
            pl.BlockSpec((rows, 2 * piece), lambda i: (0, now(i))),
            pl.BlockSpec((rows, hidden), lambda i: (0, 0)),
            pl.BlockSpec((rows, cut), lambda i: (0, then(i))),
        ],
        out_shape=[
            jax.ShapeDtypeStruct((rows, 2 * hidden), WIDE),
            jax.ShapeDtypeStruct((rows, hidden), LOW),
            jax.ShapeDtypeStruct((rows, width), LOW),
        ],
        cost_estimate=pl.CostEstimate(
            flops=6 * rows * width * hidden,
            bytes_accessed=6 * width * hidden + 10 * rows * hidden,
            transcendentals=rows * hidden,
        ),
    )(x, pair, down)


def ff_backward_kernel(piece, count, grad_ref, down_ref, both_ref, pair_ref, grad_both_ref, out_ref):
    step = pl.program_id(0)

    @pl.when(step < count)
    def _():
        grad_hidden = contract_last(grad_ref[...], down_ref[...])
        value, slope = gelu_and_slope(both_ref[:, :piece])
        start = pl.multiple_of(step * 2 * piece, piece)
        grad_both_ref[:, pl.ds(start, piece)] = (grad_hidden * both_ref[:, piece:] * slope).astype(LOW)
        start = pl.multiple_of(step * 2 * piece + piece, piece)
        grad_both_ref[:, pl.ds(start, piece)] = (grad_hidden * value).astype(LOW)

    @pl.when(step >= count)
    def _():
        out_ref[...] = jnp.dot(
            grad_both_ref[...], pair_ref[...], preferred_element_type=WIDE
        ).astype(LOW)


def ff_backward(grad, pair, down, both, piece):
    rows, width = grad.shape
    hidden = down.shape[0]
    count = hidden // piece
    cut = math.gcd(width, 512)

    def now(i):
        return jnp.minimum(i, count - 1)

    def then(i):
        return jnp.maximum(i - count, 0)

    return pl.pallas_call(
        functools.partial(ff_backward_kernel, piece, count),
        grid=(count + width // cut,),
        in_specs=[
            pl.BlockSpec((rows, width), lambda i: (0, 0)),
            pl.BlockSpec((piece, width), lambda i: (now(i), 0)),
            pl.BlockSpec((rows, 2 * piece), lambda i: (0, now(i))),
            pl.BlockSpec((2 * hidden, cut), lambda i: (0, then(i))),
        ],
        out_specs=[
            pl.BlockSpec((rows, 2 * hidden), lambda i: (0, 0)),
            pl.BlockSpec((rows, cut), lambda i: (0, then(i))),
        ],
        out_shape=[
            jax.ShapeDtypeStruct((rows, 2 * hidden), LOW),
            jax.ShapeDtypeStruct((rows, width), LOW),
        ],
        cost_estimate=pl.CostEstimate(
            flops=6 * rows * width * hidden,
            bytes_accessed=6 * width * hidden + 12 * rows * hidden,
            transcendentals=rows * hidden,
        ),
    )(grad, down, both, pair)


def attention_kernel(
    raw_ref, gain_ref, cos_ref, sin_ref, places_ref, limit_ref, kv_ref,
    q_ref, probs_ref, wide_ref, low_ref,
):
    raw = raw_ref[...]
    scale = lax.rsqrt(jnp.mean(raw * raw, axis=-1, keepdims=True) + EPSILON)
    raw = raw * scale * gain_ref[...]
    half = raw.shape[1] // 2
    front, behind = raw[:, :half], raw[:, half:]
    cosine, sine = cos_ref[...], sin_ref[...]
    q_ref[:, :half] = (front * cosine - behind * sine).astype(LOW)
    q_ref[:, half:] = (behind * cosine + front * sine).astype(LOW)
    scores = contract_last(q_ref[...], kv_ref[:, :HEAD_DIM])
    scores = jnp.where(limit_ref[...] <= places_ref[...], scores, NEGATIVE)
    raised = jnp.exp(scores - jnp.max(scores, axis=-1, keepdims=True))
    probs = raised * (1.0 / jnp.sum(raised, axis=-1, keepdims=True))
    probs_ref[0] = probs
    attended = jnp.dot(probs.astype(LOW), kv_ref[:, HEAD_DIM:], preferred_element_type=WIDE)
    wide_ref[...] = attended
    low_ref[...] = attended.astype(LOW)


def attention_forward(projected, gain, cosine, sine, query_places, key_limit, keys_values, heads):
    rows = projected.shape[0]
    keys = keys_values.shape[0]
    block = min(rows, 256, (1 << 19) // keys)
    return pl.pallas_call(
        attention_kernel,
        grid=(heads, rows // block),
        in_specs=[
            pl.BlockSpec((block, HEAD_DIM), lambda h, i: (i, h)),
            pl.BlockSpec((1, HEAD_DIM), lambda h, i: (0, 0)),
            pl.BlockSpec((block, HEAD_DIM // 2), lambda h, i: (i, 0)),
            pl.BlockSpec((block, HEAD_DIM // 2), lambda h, i: (i, 0)),
            pl.BlockSpec((block, 1), lambda h, i: (i, 0)),
            pl.BlockSpec((1, keys), lambda h, i: (0, 0)),
            pl.BlockSpec((keys, 2 * HEAD_DIM), lambda h, i: (0, 0)),
        ],
        out_specs=[
            pl.BlockSpec((block, HEAD_DIM), lambda h, i: (i, h)),
            pl.BlockSpec((1, block, keys), lambda h, i: (h, i, 0)),
            pl.BlockSpec((block, HEAD_DIM), lambda h, i: (i, h)),
            pl.BlockSpec((block, HEAD_DIM), lambda h, i: (i, h)),
        ],
        out_shape=[
            jax.ShapeDtypeStruct((rows, heads * HEAD_DIM), LOW),
            jax.ShapeDtypeStruct((heads, rows, keys), WIDE),
            jax.ShapeDtypeStruct((rows, heads * HEAD_DIM), WIDE),
            jax.ShapeDtypeStruct((rows, heads * HEAD_DIM), LOW),
        ],
        cost_estimate=pl.CostEstimate(
            flops=4 * heads * rows * keys * HEAD_DIM,
            bytes_accessed=4 * heads * rows * keys + 4 * keys * HEAD_DIM + 14 * rows * heads * HEAD_DIM,
            transcendentals=heads * rows * keys,
        ),
    )(projected, gain, cosine, sine, query_places, key_limit, keys_values)


def attention_back_kernel(
    grad_ref, wide_ref, probs_ref, q_ref, raw_ref, gain_ref, cos_ref, sin_ref, kv_ref,
    grad_raw_ref, grad_gain_ref, grad_kv_ref, total,
):
    head, step = pl.program_id(0), pl.program_id(1)
    first = jnp.logical_and(head == 0, step == 0)
    last = jnp.logical_and(head == pl.num_programs(0) - 1, step == pl.num_programs(1) - 1)
    grad = grad_ref[...]
    delta = jnp.sum(grad.astype(WIDE) * wide_ref[...], axis=-1, keepdims=True)
    probs = probs_ref[0]
    grad_probs = contract_last(grad, kv_ref[:, HEAD_DIM:])
    grad_scores = (probs * (grad_probs - delta)).astype(LOW)
    rotated = jnp.dot(grad_scores, kv_ref[:, :HEAD_DIM], preferred_element_type=WIDE)
    key_part = over_rows(grad_scores, q_ref[...])
    value_part = over_rows(probs.astype(LOW), grad)

    @pl.when(first)
    def _():
        total[:, :HEAD_DIM] = key_part
        total[:, HEAD_DIM:] = value_part

    @pl.when(jnp.logical_not(first))
    def _():
        total[:, :HEAD_DIM] += key_part
        total[:, HEAD_DIM:] += value_part

    @pl.when(last)
    def _():
        grad_kv_ref[...] = total[...].astype(LOW)

    half = rotated.shape[1] // 2
    front, behind = rotated[:, :half], rotated[:, half:]
    cosine, sine = cos_ref[...], sin_ref[...]
    back = jnp.concatenate([front * cosine + behind * sine, behind * cosine - front * sine], axis=1)
    raw = raw_ref[...]
    scale = lax.rsqrt(jnp.mean(raw * raw, axis=-1, keepdims=True) + EPSILON)
    normed = raw * scale
    gain_part = jnp.sum(back * normed, axis=0, keepdims=True)

    @pl.when(first)
    def _():
        grad_gain_ref[...] = gain_part

    @pl.when(jnp.logical_not(first))
    def _():
        grad_gain_ref[...] += gain_part

    back = back * gain_ref[...]
    grad_raw_ref[...] = (
        scale * (back - normed * jnp.mean(back * normed, axis=-1, keepdims=True))
    ).astype(LOW)


def attention_backward(grad, wide, probs, q_low, projected, gain, cosine, sine, keys_values):
    heads, rows, keys = probs.shape
    block = min(rows, 256, (1 << 19) // keys)

    def tile(h, i):
        return (i, h)

    def whole(h, i):
        return (0, 0)

    return pl.pallas_call(
        attention_back_kernel,
        grid=(heads, rows // block),
        in_specs=[
            pl.BlockSpec((block, HEAD_DIM), tile),
            pl.BlockSpec((block, HEAD_DIM), tile),
            pl.BlockSpec((1, block, keys), lambda h, i: (h, i, 0)),
            pl.BlockSpec((block, HEAD_DIM), tile),
            pl.BlockSpec((block, HEAD_DIM), tile),
            pl.BlockSpec((1, HEAD_DIM), whole),
            pl.BlockSpec((block, HEAD_DIM // 2), lambda h, i: (i, 0)),
            pl.BlockSpec((block, HEAD_DIM // 2), lambda h, i: (i, 0)),
            pl.BlockSpec((keys, 2 * HEAD_DIM), whole),
        ],
        out_specs=[
            pl.BlockSpec((block, HEAD_DIM), tile),
            pl.BlockSpec((1, HEAD_DIM), whole),
            pl.BlockSpec((keys, 2 * HEAD_DIM), whole),
        ],
        out_shape=[
            jax.ShapeDtypeStruct((rows, heads * HEAD_DIM), LOW),
            jax.ShapeDtypeStruct((1, HEAD_DIM), WIDE),
            jax.ShapeDtypeStruct((keys, 2 * HEAD_DIM), LOW),
        ],
        scratch_shapes=[pltpu.VMEM((keys, 2 * HEAD_DIM), WIDE)],
        cost_estimate=pl.CostEstimate(
            flops=8 * heads * rows * keys * HEAD_DIM,
            bytes_accessed=4 * heads * rows * keys + 8 * keys * HEAD_DIM + 14 * rows * heads * HEAD_DIM,
            transcendentals=0,
        ),
    )(grad, wide, probs, q_low, projected, gain, cosine, sine, keys_values)


def widen_kernel(places, source, gate, up):
    gate[...] = source[0, 0, 0].astype(WIDE)
    up[...] = source[0, 0, 1].astype(WIDE)


def widen_pair(pieces, places):
    parts, run, _, rows, width = pieces.shape
    return pl.pallas_call(
        widen_kernel,
        grid_spec=pltpu.PrefetchScalarGridSpec(
            num_scalar_prefetch=1,
            grid=(run, parts),
            in_specs=[pl.BlockSpec((1, 1, 2, rows, width), lambda k, r, p: (r, k, 0, 0, 0))],
            out_specs=[pl.BlockSpec((rows, width), lambda k, r, p: (0, p[k] * parts + r))] * 2,
        ),
        out_shape=[jax.ShapeDtypeStruct((rows, width * parts * run), WIDE)] * 2,
        cost_estimate=pl.CostEstimate(flops=0, bytes_accessed=6 * pieces.size, transcendentals=0),
    )(places, pieces)


def shift_blocks(make):
    run = lax.axis_size("wsh")
    here = lax.axis_index("wsh")
    received = []
    for k in range(run):
        block = make((here + k) % run)
        if k:
            block = lax.ppermute(block, "wsh", [(i, (i + k) % run) for i in range(run)])
        received.append(block)
    return received


def shift_exchange(make):
    run = lax.axis_size("wsh")
    order = (lax.axis_index("wsh") - jnp.arange(run, dtype=jnp.int32)) % run
    return jnp.take(jnp.stack(shift_blocks(make)), order, axis=0)


def place_kernel(places, *refs):
    step = pl.program_id(0)
    sources, out = refs[:-1], refs[-1]
    for number, source in enumerate(sources):

        @pl.when(step == number)
        def _(source=source):
            out[...] = source[...]


def place_columns(blocks, places):
    rows, width = blocks[0].shape
    count = len(blocks)
    return pl.pallas_call(
        place_kernel,
        grid_spec=pltpu.PrefetchScalarGridSpec(
            num_scalar_prefetch=1,
            grid=(count,),
            in_specs=[pl.BlockSpec((rows, width), lambda k, p: (0, 0))] * count,
            out_specs=pl.BlockSpec((rows, width), lambda k, p: (0, p[k])),
        ),
        out_shape=jax.ShapeDtypeStruct((rows, width * count), blocks[0].dtype),
        cost_estimate=pl.CostEstimate(
            flops=0, bytes_accessed=4 * count * blocks[0].size, transcendentals=0
        ),
    )(places, *blocks)


def entry(stacked):
    return lambda index: lax.dynamic_index_in_dim(stacked, index, 0, False)


def shards(
    tokens,
    cotangent,
    lengths,
    positions,
    token_ids,
    per_layer_table,
    w_query,
    w_key,
    w_value,
    w_output,
    laurel_left,
    laurel_right,
    w_gate,
    w_up,
    w_down,
    w_layer_gate,
    w_layer_proj,
    norm_gains,
    query_gain,
    key_gain,
):
    rows_dev, width = tokens.shape[1:]
    run = lax.axis_size("wsh")
    contexts = lax.axis_size("ctx")
    parts = 2 * contexts
    chip = lax.axis_index(COPIES)
    shard_rows = width // run
    heads_here = HEADS // run
    groups = HEADS // KV_HEADS
    query_width = heads_here * HEAD_DIM
    head_width = query_width + 2 * HEAD_DIM
    hidden_width = w_gate.shape[1] // run
    head_piece = shard_rows // parts
    piece = hidden_width // parts
    rank = laurel_left.shape[1]
    places = ((lax.axis_index("wsh") - jnp.arange(run)) % run).astype(jnp.int32)
    gain_cut = query_gain.shape[0]

    def share(weight):
        return lax.dynamic_slice_in_dim(weight, chip * head_piece, head_piece, 0)

    query_rows, key_rows, value_rows = share(w_query), share(w_key), share(w_value)

    indices = shift_exchange(lambda k: jnp.concatenate([token_ids, positions], axis=0))
    small = jnp.concatenate(
        [
            norm_gains.T,
            jnp.pad(
                jnp.concatenate([query_gain, key_gain])[None],
                ((0, 1), (0, shard_rows - 2 * gain_cut)),
            ),
        ],
        axis=0,
    )
    proj_rows = w_layer_proj.shape[0]
    proj_share = lax.dynamic_slice_in_dim(w_layer_proj, chip * (width // parts), width // parts, 1)
    common = jnp.concatenate(
        [
            share(laurel_left),
            share(laurel_right),
            share(w_layer_gate),
            proj_share.reshape(head_piece, -1),
        ],
        axis=1,
    )
    fetch_width = head_width + common.shape[1]
    small_flat = jnp.pad(small.reshape(-1), (0, -small.size % fetch_width)).reshape(-1, fetch_width)
    small_flat = jnp.pad(small_flat, ((0, 16 - small_flat.shape[0]), (0, 0)))
    common, query_rows, key_rows, value_rows, small_flat, indices = lax.optimization_barrier(
        (common, query_rows, key_rows, value_rows, small_flat, indices)
    )

    def head_block(index):
        kv = index * heads_here // groups * HEAD_DIM
        block = jnp.concatenate(
            [
                lax.dynamic_slice_in_dim(query_rows, index * query_width, query_width, 1),
                lax.dynamic_slice_in_dim(key_rows, kv, HEAD_DIM, 1),
                lax.dynamic_slice_in_dim(value_rows, kv, HEAD_DIM, 1),
                common,
            ],
            axis=1,
        )
        return jnp.concatenate([small_flat, block], axis=0)

    head_share = shift_exchange(head_block)
    small_all = head_share[:, :16].reshape(run, -1)[:, : small.size].reshape(run, 8, shard_rows)
    fetched = lax.all_gather(head_share[:, 16:], COPIES, axis=0)
    w_heads = fetched[:, :, :, :head_width]
    proj_at = head_width + 2 * rank + w_layer_gate.shape[1]
    layer_proj_full = fetched[:, :, :, proj_at:].reshape(parts, run, proj_rows, width // parts)
    layer_proj_full = layer_proj_full.transpose(1, 2, 0, 3).reshape(run * proj_rows, width)
    laurel_weights = fetched[:, :, :, head_width:proj_at].transpose(1, 0, 2, 3).reshape(width, -1)
    left_full = laurel_weights[:, :rank]
    right_full = laurel_weights[:, rank : 2 * rank]
    layer_gate_full = laurel_weights[:, 2 * rank :]
    w_heads = w_heads.transpose(1, 0, 2, 3).reshape(width, head_width)

    gains_full = small_all.transpose(1, 0, 2).reshape(8, width).astype(WIDE)
    query_gain_full = small_all[:, 6, :gain_cut].reshape(HEAD_DIM).astype(WIDE)
    key_gain_full = small_all[:, 6, gain_cut : 2 * gain_cut].reshape(HEAD_DIM).astype(WIDE)
    tokens_run = spread(tokens[0], "wsh")

    indices = indices[None]
    bit = 1
    while bit < contexts:
        indices = jnp.concatenate([indices, swap(indices, "ctx", bit)], axis=0)
        bit *= 2
    run_places = indices[0, :, 1].reshape(-1)
    here_ctx = lax.axis_index("ctx")
    context_order = jnp.bitwise_xor(jnp.arange(contexts, dtype=jnp.int32), here_ctx)
    key_places = jnp.take(indices[:, :, 1], context_order, axis=0).reshape(-1)
    own_ids = indices[:, :, 0].reshape(-1)
    all_ids = jnp.concatenate([own_ids, swap(own_ids, "slot", 1)])
    length = lengths[0]

    vocab_rows = per_layer_table.shape[0]
    vocab_first = lax.axis_index(EVERY) * vocab_rows
    vocab_range = jnp.arange(vocab_rows, dtype=jnp.int32)

    def one_hot():
        return ((all_ids - vocab_first)[:, None] == vocab_range[None, :]).astype(LOW)

    table_rows = matmul(one_hot(), per_layer_table).astype(LOW)
    tokens_run, table_rows = lax.optimization_barrier((tokens_run, table_rows))
    def pair_block(index):
        first = index * hidden_width + chip * piece
        gate_cut = lax.dynamic_slice_in_dim(w_gate, first, piece, 1)
        up_cut = lax.dynamic_slice_in_dim(w_up, first, piece, 1)
        gate_cut, up_cut = after((gate_cut, up_cut), head_share)
        return jnp.concatenate([gate_cut.T, up_cut.T], axis=0)

    pair_received = shift_blocks(pair_block)
    normed_run = rms_norm(tokens_run.astype(WIDE), gains_full[0]).astype(LOW)
    tokens_f = tokens[0].astype(WIDE)
    normed = rms_norm(tokens_f, gains_full[0])
    normed_low = normed.astype(LOW)
    total_rows = run * rows_dev
    projected = matmul(normed_run, w_heads)
    key = projected[:, query_width : query_width + HEAD_DIM]
    value = projected[:, query_width + HEAD_DIM :]

    def key_path(raw, gain):
        return rotate(rms_norm(raw.reshape(total_rows, 1, HEAD_DIM), gain), run_places)[:, 0]

    def value_path(raw):
        return rms_norm(raw, 1.0)

    k_low = key_path(key, key_gain_full).astype(LOW)
    v_low = value_path(value).astype(LOW)
    keys_values = spread(jnp.concatenate([k_low, v_low], axis=1), "ctx")
    half = table_rows.shape[0] // 2
    looked_up = add_low(table_rows[:half], swap(table_rows[half:], "slot", 1))
    bit = contexts // 2
    while bit:
        half = looked_up.shape[0] // 2
        looked_up = add_low(looked_up[:half], swap(looked_up[half:], "ctx", bit))
        bit //= 2
    looked_up = looked_up.reshape(run, rows_dev, -1)
    inverse = jnp.exp(
        -math.log(ROPE_BASE)
        * (2.0 * jnp.arange(HEAD_DIM // 2, dtype=jnp.float32) / HEAD_DIM)
    )
    angles = run_places.astype(WIDE)[:, None] * inverse[None, :]
    cosine, sine = jnp.cos(angles), jnp.sin(angles)
    key_limit = jnp.where(key_places < length, key_places, jnp.int32(1 << 30))
    q_low, probs, attended, attended_low = attention_forward(
        projected,
        query_gain_full[None],
        cosine,
        sine,
        run_places[:, None],
        key_limit[None],
        keys_values,
        heads_here,
    )
    attended_low, pair_received = lax.optimization_barrier((attended_low, pair_received))
    pair_share = place_columns(pair_received, places)
    pair_weight = lax.all_gather(pair_share, COPIES, axis=0, tiled=True)
    attn_proj = collect(matmul(attended_low, w_output).astype(LOW), "wsh")
    attn_proj, looked_up = lax.optimization_barrier((attn_proj, looked_up))
    layer_input = EMBED_SCALE * jnp.sum(shift_exchange(entry(looked_up)).astype(WIDE), axis=0)

    first_sum = tokens_f + rms_norm(attn_proj, gains_full[1])
    low_rank_low = matmul(normed_low, left_full).astype(LOW)
    laurel_out = times_transposed(low_rank_low, right_full)
    laurel = normed + rms_norm(laurel_out, gains_full[2])
    mixed = (first_sum + laurel) * HALF_ROOT
    ff_in_low = rms_norm(mixed, gains_full[3]).astype(LOW)

    ff_run = spread(ff_in_low, "wsh")
    aligned = piece % 128 == 0
    if aligned:
        both, hidden_low, ff_part = ff_forward(ff_run, pair_weight, w_down, piece)
    else:
        both = times_transposed(ff_run, pair_weight)
        both_parts = both.reshape(total_rows, parts, 2, piece)
        gate = both_parts[:, :, 0].reshape(total_rows, hidden_width)
        upward = both_parts[:, :, 1].reshape(total_rows, hidden_width)
        hidden_low = gated_product(gate, upward).astype(LOW)
        ff_part = matmul(hidden_low, w_down).astype(LOW)
    ff_part, layer_input = lax.optimization_barrier((ff_part, layer_input))
    ff_out = collect(ff_part, "wsh")
    third_sum = mixed + rms_norm(ff_out, gains_full[4])
    third_low = third_sum.astype(LOW)

    layer_gate = matmul(third_low, layer_gate_full)
    gated_low = gated_product(layer_gate, layer_input).astype(LOW)
    layer_proj = matmul(gated_low, layer_proj_full)
    result = third_sum + rms_norm(layer_proj, gains_full[5])
    layer_out = result.astype(LOW)[None]

    valid = (positions[0] < length).astype(WIDE)
    grad_out = cotangent[0].astype(WIDE) * valid[:, None]
    _, pullback = jax.vjp(rms_norm, layer_proj, gains_full[5])
    grad_proj, grad_gain_five = pullback(grad_out)
    grad_proj_low = grad_proj.astype(LOW)
    grad_gated = times_transposed(grad_proj_low, layer_proj_full)
    _, pullback = jax.vjp(gated_product, layer_gate, layer_input)
    grad_lgate, grad_input = pullback(grad_gated)
    grad_lgate_low = grad_lgate.astype(LOW)
    grad_input_low = grad_input.astype(LOW)
    grad_third = grad_out + times_transposed(grad_lgate_low, layer_gate_full)
    _, pullback = jax.vjp(rms_norm, ff_out, gains_full[4])
    grad_ff, grad_gain_four = pullback(grad_third)
    grad_ff_low = grad_ff.astype(LOW)

    grad_ff_run = spread(grad_ff_low, "wsh")
    every_grad = shift_exchange(lambda k: grad_input_low).reshape(total_rows, -1)
    down_part = over_rows(hidden_low, grad_ff_run).astype(LOW)
    grad_ff_run, every_grad, down_part = lax.optimization_barrier(
        (grad_ff_run, every_grad, down_part)
    )
    down_own = lax.psum_scatter(down_part, COPIES, scatter_dimension=0, tiled=True)

    def wider(rows, axis, bit):
        return jnp.concatenate([rows, swap(rows, axis, bit)], axis=0)

    hops = [1 << power for power in range(contexts.bit_length() - 1)]
    every_grad = wider(every_grad, "ctx", hops[0])
    if aligned:
        grad_both, ff_part = ff_backward(grad_ff_run, pair_weight, w_down, both, piece)
    else:
        grad_hidden = times_transposed(grad_ff_run, w_down)
        _, pullback = jax.vjp(gated_product, gate, upward)
        grad_gate, grad_upward = pullback(grad_hidden)
        grad_both = jnp.stack(
            [
                grad_gate.reshape(total_rows, parts, piece),
                grad_upward.reshape(total_rows, parts, piece),
            ],
            axis=2,
        )
        grad_both = grad_both.reshape(total_rows, 2 * hidden_width).astype(LOW)
        ff_part = matmul(grad_both, pair_weight).astype(LOW)
    ff_part, every_grad = lax.optimization_barrier((ff_part, every_grad))
    for bit in hops[1:]:
        every_grad = wider(every_grad, "ctx", bit)
    grad_ff_in = collect(ff_part, "wsh")
    pair_part = over_rows(after(grad_both, ff_part), ff_run).astype(LOW)
    grad_ff_in, pair_part, every_grad = lax.optimization_barrier((grad_ff_in, pair_part, every_grad))
    every_grad = wider(every_grad, "slot", 1)
    pair_own = lax.psum_scatter(pair_part, COPIES, scatter_dimension=0, tiled=True)
    _, pullback = jax.vjp(rms_norm, mixed, gains_full[3])
    grad_mixed_norm, grad_gain_three = pullback(grad_ff_in)
    grad_branch = (grad_third + grad_mixed_norm) * HALF_ROOT
    _, pullback = jax.vjp(rms_norm, attn_proj, gains_full[1])
    grad_attn, grad_gain_one = pullback(grad_branch)
    grad_attn_low = grad_attn.astype(LOW)
    grad_attn_run = spread(grad_attn_low, "wsh")
    grad_attn_run, down_own, every_grad = lax.optimization_barrier(
        (grad_attn_run, down_own, every_grad)
    )
    down_grad = lax.all_gather(down_own, COPIES, axis=0, tiled=True)

    def pair_back(index):
        block = lax.dynamic_slice_in_dim(pair_own, index * shard_rows, shard_rows, 1)
        return block.reshape(2, piece, shard_rows).transpose(0, 2, 1)

    _, pullback = jax.vjp(rms_norm, laurel_out, gains_full[2])
    grad_laurel, grad_gain_two = pullback(grad_branch)
    grad_laurel_low = grad_laurel.astype(LOW)
    grad_rank_low = matmul(grad_laurel_low, right_full).astype(LOW)

    left_grad = over_rows(normed_low, grad_rank_low)
    right_grad = over_rows(grad_laurel_low, low_rank_low)
    layer_gate_grad = over_rows(third_low, grad_lgate_low)
    layer_proj_grad = over_rows(gated_low, grad_proj_low)

    narrow = jnp.concatenate([left_grad, right_grad, layer_gate_grad], axis=1).astype(LOW)
    narrow_columns = narrow.shape[1]
    proj_back = layer_proj_grad.astype(LOW).reshape(run, proj_rows, parts, width // parts)
    proj_back = proj_back.transpose(0, 2, 1, 3).reshape(run, parts, head_piece, -1)
    narrow = jnp.concatenate(
        [narrow.reshape(run, parts, head_piece, narrow_columns), proj_back], axis=3
    )

    grad_att_low = times_transposed(grad_attn_run, w_output).astype(LOW)
    grad_query, grad_query_gain, kv_part = attention_backward(
        grad_att_low,
        attended,
        probs,
        q_low,
        projected,
        query_gain_full[None],
        cosine,
        sine,
        keys_values,
    )
    grad_query_gain = grad_query_gain[0]
    kv_sum = collect(kv_part, "ctx")
    output_part = over_rows(attended_low, grad_attn_run).astype(LOW)
    output_kept, output_given = halves(output_part.reshape(parts, -1, width))
    kv_sum, pair_own, output_kept, output_given, narrow = lax.optimization_barrier(
        (kv_sum, pair_own, output_kept, output_given, narrow)
    )
    pair_blocks = jnp.stack(shift_blocks(pair_back))
    output_pieces = nearest(add_low(output_kept, output_given))
    output_first = reduce_first(output_pieces)
    _, pullback = jax.vjp(key_path, key, key_gain_full)
    grad_key, grad_key_gain = pullback(kv_sum[:, :HEAD_DIM])
    _, pullback = jax.vjp(value_path, value)
    (grad_value,) = pullback(kv_sum[:, HEAD_DIM:])
    grad_heads = jnp.concatenate(
        [grad_query, grad_key.astype(LOW), grad_value.astype(LOW)], axis=1
    )
    heads_part = over_rows(normed_run, grad_heads).astype(LOW)
    heads_part = heads_part.reshape(run, parts, head_piece, head_width)
    heads_part = jnp.concatenate([heads_part, narrow], axis=3).transpose(1, 0, 2, 3)
    heads_kept, heads_given = halves(heads_part)
    normed_part = times_transposed(grad_heads, w_heads).astype(LOW)
    normed_part, output_first, heads_kept, heads_given, pair_blocks = lax.optimization_barrier(
        (normed_part, output_first, heads_kept, heads_given, pair_blocks)
    )
    pair_all = lax.all_gather(pair_blocks, COPIES, axis=0)
    table_grad = EMBED_SCALE * over_rows(one_hot(), after(every_grad, normed_part))
    heads_pieces = nearest(add_low(heads_kept, heads_given))
    heads_first = reduce_first(heads_pieces)
    heads_second = reduce_second(heads_pieces, heads_first)
    output_second = reduce_second(output_pieces, output_first)
    grad_run = collect(normed_part, "wsh")
    grad_run, heads_second, output_second, table_grad = lax.optimization_barrier(
        (grad_run, heads_second, output_second, table_grad)
    )
    heads_own = reduce_last(heads_pieces, heads_second)
    heads_own = shift_exchange(entry(heads_own)).astype(WIDE)
    pieces = [heads_own[:, :, :query_width].transpose(1, 0, 2).reshape(head_piece, -1)]
    for begin in (query_width, query_width + HEAD_DIM):
        one = heads_own[:, :, begin : begin + HEAD_DIM]
        one = one.reshape(KV_HEADS, run // KV_HEADS, head_piece, HEAD_DIM).sum(axis=1)
        pieces.append(one.transpose(1, 0, 2).reshape(head_piece, -1))
    pieces.append(heads_own[:, :, head_width : head_width + narrow_columns].sum(axis=0))
    pieces.append(heads_own[:, :, head_width + narrow_columns :].sum(axis=0))
    cuts = []
    for one in pieces:
        cuts.append((sum(w for _, w in cuts), one.shape[1]))
    heads_piece = jnp.concatenate(pieces, axis=1).astype(LOW)
    heads_near = gather_second(heads_piece, gather_first(heads_piece))
    output_own = reduce_last(output_pieces, output_second)
    output_near = gather_first(output_own)
    down_grad = after(down_grad, grad_run).astype(WIDE)
    own = jnp.full((1,), chip, jnp.int32)
    if aligned:
        gate_grad, up_grad = widen_pair(pair_all, places)
    else:
        pair_all = jnp.take(pair_all, places, axis=1)
        pair_all = pair_all.transpose(2, 3, 1, 0, 4).reshape(2, shard_rows, -1).astype(WIDE)
        gate_grad, up_grad = pair_all[0], pair_all[1]
    grad_normed = (
        grad_run
        + times_transposed(grad_rank_low, left_full)
        + grad_branch
    )
    _, pullback = jax.vjp(rms_norm, tokens_f, gains_full[0])
    grad_tokens, grad_gain_zero = pullback(grad_normed)
    tokens_grad = (grad_tokens + grad_branch).astype(LOW)[None]

    output_all = last_gather(gather_second(output_own, output_near))
    (output_grad,) = assemble([p[None] for p in output_all], own, WIDE)
    query_grad, key_grad, value_grad, narrow, layer_proj_grad = assemble(
        [p[None] for p in last_gather(heads_near)], own, WIDE, cuts
    )
    narrow = narrow.reshape(shard_rows, -1)
    layer_proj_grad = layer_proj_grad.reshape(parts, proj_rows, width // parts)
    layer_proj_grad = layer_proj_grad.transpose(1, 0, 2).reshape(proj_rows, width)

    vector = jnp.concatenate(
        [grad_query_gain.reshape(run, gain_cut), grad_key_gain.reshape(run, gain_cut)], axis=1
    )
    vector = jnp.pad(vector, ((0, 0), (0, shard_rows - 2 * gain_cut))).reshape(width)
    gain_sums = jnp.stack(
        [
            grad_gain_zero,
            grad_gain_one,
            grad_gain_two,
            grad_gain_three,
            grad_gain_four,
            grad_gain_five,
            vector,
            jnp.zeros_like(vector),
        ]
    )
    gain_sums = gain_sums.reshape(8, run, shard_rows).transpose(1, 0, 2).reshape(8 * run, shard_rows)
    gain_sums = collect(gain_sums, "wsh")
    gain_sums = jnp.sum(spread(gain_sums[None], COPIES), axis=0)
    return (
        layer_out,
        tokens_grad,
        table_grad,
        query_grad.reshape(shard_rows, -1),
        key_grad.reshape(shard_rows, -1),
        value_grad.reshape(shard_rows, -1),
        output_grad.reshape(query_width, width),
        narrow[:, :rank],
        narrow[:, rank : 2 * rank],
        gate_grad,
        up_grad,
        down_grad,
        narrow[:, 2 * rank :],
        layer_proj_grad,
        gain_sums[:6].T,
        gain_sums[6, :gain_cut],
        gain_sums[6, gain_cut : 2 * gain_cut],
    )


def solution(mesh):
    placed = (
        P("slot", ("ctx", "wsh"), None),
        P("slot", ("ctx", "wsh"), None),
        P("slot"),
        P("slot", ("ctx", "wsh")),
        P("slot", ("ctx", "wsh")),
        P(("slot", "ctx", "wsh"), None),
        P("wsh", None),
        P("wsh", None),
        P("wsh", None),
        P("wsh", None),
        P("wsh", None),
        P("wsh", None),
        P("wsh", None),
        P("wsh", None),
        P("wsh", None),
        P("wsh", None),
        P("wsh", None),
        P("wsh", None),
        P("wsh"),
        P("wsh"),
    )
    return jax.shard_map(
        shards,
        mesh=mesh,
        in_specs=placed,
        out_specs=(
            P("slot", ("ctx", "wsh"), None),
            P("slot", ("ctx", "wsh"), None),
            P(("slot", "ctx", "wsh"), None),
            P("wsh", None),
            P("wsh", None),
            P("wsh", None),
            P("wsh", None),
            P("wsh", None),
            P("wsh", None),
            P("wsh", None),
            P("wsh", None),
            P("wsh", None),
            P("wsh", None),
            P("wsh", None),
            P("wsh", None),
            P("wsh"),
            P("wsh"),
        ),
        check_vma=False,
    )
```

```python
import functools
import math

import jax
import jax.numpy as jnp
from jax import lax
from jax.experimental import pallas as pl
from jax.experimental.pallas import tpu as pltpu
from jax.sharding import PartitionSpec as P

HEADS = 8
KV_HEADS = 2
HEAD_DIM = 256


EPSILON = 1e-06
ROPE_BASE = 1000000.0
HALF_ROOT = 0.7071067811865476
TANH_SCALE = 0.7978845608028654
NEGATIVE = -1e30
EMBED_SCALE = 16.0


def rms_norm(value, gain):
    return value * lax.rsqrt(jnp.mean(value * value, axis=-1, keepdims=True) + EPSILON) * gain


def gelu_tanh(value):
    return 0.5 * value * (1.0 + jnp.tanh(TANH_SCALE * (value + 0.044715 * value * value * value)))


def gated_product(pre_gate, other_side):
    return gelu_tanh(pre_gate) * other_side


def rotate(value, places):
    width_all = value.shape[-1]
    half_width = width_all // 2
    inverse = jnp.exp(
        -math.log(ROPE_BASE) * (2.0 * jnp.arange(half_width, dtype=jnp.float32) / width_all)
    )
    angles = places.astype(jnp.float32)[:, None] * inverse[None, :]
    cosine = jnp.cos(angles)[:, None, :]
    sine = jnp.sin(angles)[:, None, :]
    front = value[..., :half_width]
    behind = value[..., half_width:]
    return jnp.concatenate(
        [front * cosine - behind * sine, behind * cosine + front * sine], axis=-1
    )


def matmul(left, right):
    return jnp.dot(left, right, preferred_element_type=jnp.float32)


def times_transposed(left, right):
    return lax.dot_general(
        left, right, (((1,), (1,)), ((), ())), preferred_element_type=jnp.float32
    )


def over_rows(left, right):
    return lax.dot_general(
        left, right, (((0,), (0,)), ((), ())), preferred_element_type=jnp.float32
    )


LOW = jnp.bfloat16
WIDE = jnp.float32
EVERY = ("slot", "ctx", "wsh")
COPIES = ("slot", "ctx")


def after(value, *others):
    return lax.optimization_barrier((value, others))[0]


def exchange(value, axis):
    return lax.all_to_all(value, axis, 0, 0, tiled=True)


def spread(value, axis):
    size = lax.axis_size(axis)
    copies = jnp.broadcast_to(value[None], (size,) + value.shape)
    return exchange(copies.reshape((size * value.shape[0],) + value.shape[1:]), axis)


def collect(parts, axis):
    size = lax.axis_size(axis)
    received = exchange(parts, axis)
    received = received.reshape((size, parts.shape[0] // size) + parts.shape[1:])
    return jnp.sum(received.astype(WIDE), axis=0)


def swap(value, axis, bit):
    size = lax.axis_size(axis)
    return lax.ppermute(value, axis, [(i, i ^ bit) for i in range(size)])


def add_low(left, right):
    return (left.astype(WIDE) + right.astype(WIDE)).astype(LOW)


def gather_first(piece):
    if lax.axis_size("ctx") == 4:
        return [swap(piece, "ctx", 1), swap(piece, "ctx", 2)]
    return []


def gather_second(piece, first):
    if first:
        one, two = first
        half = piece.shape[0] // 2
        front = swap(one[:half], "ctx", 2)
        behind = swap(two[half:], "ctx", 1)
        return [piece, one, two, jnp.concatenate([front, behind], axis=0)]
    pieces = [piece]
    bit = 1
    while bit < lax.axis_size("ctx"):
        pieces = pieces + [swap(p, "ctx", bit) for p in pieces]
        bit *= 2
    return pieces


def reduce_first(pieces):
    if len(pieces) == 4:
        half = pieces[0].shape[0] // 2
        return [swap(pieces[3][:half], "ctx", 1), swap(pieces[3][half:], "ctx", 2)]
    return []


def reduce_second(pieces, first):
    if first:
        front, behind = first
        half = pieces[0].shape[0] // 2
        two = jnp.concatenate([add_low(pieces[2][:half], front), pieces[2][half:]], axis=0)
        one = jnp.concatenate([pieces[1][:half], add_low(pieces[1][half:], behind)], axis=0)
        return [swap(one, "ctx", 1), swap(two, "ctx", 2)]
    return []


def reduce_last(pieces, second):
    if second:
        one, two = second
        return (pieces[0].astype(WIDE) + one.astype(WIDE) + two.astype(WIDE)).astype(LOW)
    size = len(pieces)
    while size > 1:
        size //= 2
        pieces = [add_low(pieces[i], swap(pieces[size + i], "ctx", size)) for i in range(size)]
    return pieces[0]


def assemble_kernel(extent, cuts, own, *refs):
    step = pl.program_id(0)
    ins, outs = refs[:extent], refs[extent:]
    for number in range(extent):

        @pl.when(step == number)
        def _(number=number):
            for (begin, width), out in zip(cuts, outs):
                out[:, 0] = ins[number][:, :, begin : begin + width].astype(out.dtype)


def assemble(pieces, own, kind, cuts=None):
    count = len(pieces)
    outer, inner, width = pieces[0].shape
    cuts = cuts or [(0, width)]
    results = pl.pallas_call(
        functools.partial(assemble_kernel, count, cuts),
        grid_spec=pltpu.PrefetchScalarGridSpec(
            num_scalar_prefetch=1,
            grid=(count,),
            in_specs=[pl.BlockSpec((outer, inner, width), lambda i, o: (0, 0, 0))] * count,
            out_specs=[
                pl.BlockSpec((outer, 1, inner, w), lambda i, o: (0, lax.bitwise_xor(i, o[0]), 0, 0))
                for _, w in cuts
            ],
        ),
        out_shape=[jax.ShapeDtypeStruct((outer, count, inner, w), kind) for _, w in cuts],
    )(own, *pieces)
    return results


def halves(blocks):
    count = blocks.shape[0] // 2
    slot = lax.axis_index("slot")
    kept = lax.dynamic_slice_in_dim(blocks, slot * count, count, 0)
    given = lax.dynamic_slice_in_dim(blocks, (1 - slot) * count, count, 0)
    return kept, swap(given, "slot", 1)


def nearest(blocks):
    here = lax.axis_index("ctx")
    count = blocks.shape[0]
    return [lax.dynamic_index_in_dim(blocks, here ^ r, 0, False) for r in range(count)]


def last_gather(pieces):
    return pieces + [swap(p, "slot", 1) for p in pieces]


def contract_last(left, right):
    return lax.dot_general(left, right, (((1,), (1,)), ((), ())), preferred_element_type=WIDE)


def gelu_and_slope(value):
    inner = jnp.tanh(TANH_SCALE * (value + 0.044715 * value * value * value))
    slope = 0.5 * (1.0 + inner) + 0.5 * value * (1.0 - inner * inner) * TANH_SCALE * (
        1.0 + 3.0 * 0.044715 * value * value
    )
    return 0.5 * value * (1.0 + inner), slope


def ff_forward_kernel(piece, count, x_ref, pair_ref, down_ref, both_ref, hidden_ref, out_ref):
    step = pl.program_id(0)

    @pl.when(step < count)
    def _():
        both = contract_last(x_ref[...], pair_ref[...])
        both_ref[...] = both
        hidden = (gelu_tanh(both[:, :piece]) * both[:, piece:]).astype(LOW)
        hidden_ref[:, pl.ds(pl.multiple_of(step * piece, piece), piece)] = hidden

    @pl.when(step >= count)
    def _():
        out_ref[...] = jnp.dot(
            hidden_ref[...], down_ref[...], preferred_element_type=WIDE
        ).astype(LOW)


def ff_forward(x, pair, down, piece):
    rows, width = x.shape
    hidden = down.shape[0]
    count = hidden // piece
    cut = math.gcd(width, 512)

    def now(i):
        return jnp.minimum(i, count - 1)

    def then(i):
        return jnp.maximum(i - count, 0)

    return pl.pallas_call(
        functools.partial(ff_forward_kernel, piece, count),
        grid=(count + width // cut,),
        in_specs=[
            pl.BlockSpec((rows, width), lambda i: (0, 0)),
            pl.BlockSpec((2 * piece, width), lambda i: (now(i), 0)),
            pl.BlockSpec((hidden, cut), lambda i: (0, then(i))),
        ],
        out_specs=[
            pl.BlockSpec((rows, 2 * piece), lambda i: (0, now(i))),
            pl.BlockSpec((rows, hidden), lambda i: (0, 0)),
            pl.BlockSpec((rows, cut), lambda i: (0, then(i))),
        ],
        out_shape=[
            jax.ShapeDtypeStruct((rows, 2 * hidden), WIDE),
            jax.ShapeDtypeStruct((rows, hidden), LOW),
            jax.ShapeDtypeStruct((rows, width), LOW),
        ],
        cost_estimate=pl.CostEstimate(
            flops=6 * rows * width * hidden,
            bytes_accessed=6 * width * hidden + 10 * rows * hidden,
            transcendentals=rows * hidden,
        ),
    )(x, pair, down)


def ff_backward_kernel(piece, count, grad_ref, down_ref, both_ref, pair_ref, grad_both_ref, out_ref):
    step = pl.program_id(0)

    @pl.when(step < count)
    def _():
        grad_hidden = contract_last(grad_ref[...], down_ref[...])
        value, slope = gelu_and_slope(both_ref[:, :piece])
        start = pl.multiple_of(step * 2 * piece, piece)
        grad_both_ref[:, pl.ds(start, piece)] = (grad_hidden * both_ref[:, piece:] * slope).astype(LOW)
        start = pl.multiple_of(step * 2 * piece + piece, piece)
        grad_both_ref[:, pl.ds(start, piece)] = (grad_hidden * value).astype(LOW)

    @pl.when(step >= count)
    def _():
        out_ref[...] = jnp.dot(
            grad_both_ref[...], pair_ref[...], preferred_element_type=WIDE
        ).astype(LOW)


def ff_backward(grad, pair, down, both, piece):
    rows, width = grad.shape
    hidden = down.shape[0]
    count = hidden // piece
    cut = math.gcd(width, 512)

    def now(i):
        return jnp.minimum(i, count - 1)

    def then(i):
        return jnp.maximum(i - count, 0)

    return pl.pallas_call(
        functools.partial(ff_backward_kernel, piece, count),
        grid=(count + width // cut,),
        in_specs=[
            pl.BlockSpec((rows, width), lambda i: (0, 0)),
            pl.BlockSpec((piece, width), lambda i: (now(i), 0)),
            pl.BlockSpec((rows, 2 * piece), lambda i: (0, now(i))),
            pl.BlockSpec((2 * hidden, cut), lambda i: (0, then(i))),
        ],
        out_specs=[
            pl.BlockSpec((rows, 2 * hidden), lambda i: (0, 0)),
            pl.BlockSpec((rows, cut), lambda i: (0, then(i))),
        ],
        out_shape=[
            jax.ShapeDtypeStruct((rows, 2 * hidden), LOW),
            jax.ShapeDtypeStruct((rows, width), LOW),
        ],
        cost_estimate=pl.CostEstimate(
            flops=6 * rows * width * hidden,
            bytes_accessed=6 * width * hidden + 12 * rows * hidden,
            transcendentals=rows * hidden,
        ),
    )(grad, down, both, pair)


def attention_kernel(
    raw_ref, gain_ref, cos_ref, sin_ref, places_ref, limit_ref, kv_ref,
    q_ref, probs_ref, wide_ref, low_ref,
):
    raw = raw_ref[...]
    scale = lax.rsqrt(jnp.mean(raw * raw, axis=-1, keepdims=True) + EPSILON)
    raw = raw * scale * gain_ref[...]
    half = raw.shape[1] // 2
    front, behind = raw[:, :half], raw[:, half:]
    cosine, sine = cos_ref[...], sin_ref[...]
    q_ref[:, :half] = (front * cosine - behind * sine).astype(LOW)
    q_ref[:, half:] = (behind * cosine + front * sine).astype(LOW)
    scores = contract_last(q_ref[...], kv_ref[:, :HEAD_DIM])
    scores = jnp.where(limit_ref[...] <= places_ref[...], scores, NEGATIVE)
    raised = jnp.exp(scores - jnp.max(scores, axis=-1, keepdims=True))
    probs = raised * (1.0 / jnp.sum(raised, axis=-1, keepdims=True))
    probs_ref[0] = probs
    attended = jnp.dot(probs.astype(LOW), kv_ref[:, HEAD_DIM:], preferred_element_type=WIDE)
    wide_ref[...] = attended
    low_ref[...] = attended.astype(LOW)


def attention_forward(projected, gain, cosine, sine, query_places, key_limit, keys_values, heads):
    rows = projected.shape[0]
    keys = keys_values.shape[0]
    block = min(rows, 256, (1 << 19) // keys)
    return pl.pallas_call(
        attention_kernel,
        grid=(heads, rows // block),
        in_specs=[
            pl.BlockSpec((block, HEAD_DIM), lambda h, i: (i, h)),
            pl.BlockSpec((1, HEAD_DIM), lambda h, i: (0, 0)),
            pl.BlockSpec((block, HEAD_DIM // 2), lambda h, i: (i, 0)),
            pl.BlockSpec((block, HEAD_DIM // 2), lambda h, i: (i, 0)),
            pl.BlockSpec((block, 1), lambda h, i: (i, 0)),
            pl.BlockSpec((1, keys), lambda h, i: (0, 0)),
            pl.BlockSpec((keys, 2 * HEAD_DIM), lambda h, i: (0, 0)),
        ],
        out_specs=[
            pl.BlockSpec((block, HEAD_DIM), lambda h, i: (i, h)),
            pl.BlockSpec((1, block, keys), lambda h, i: (h, i, 0)),
            pl.BlockSpec((block, HEAD_DIM), lambda h, i: (i, h)),
            pl.BlockSpec((block, HEAD_DIM), lambda h, i: (i, h)),
        ],
        out_shape=[
            jax.ShapeDtypeStruct((rows, heads * HEAD_DIM), LOW),
            jax.ShapeDtypeStruct((heads, rows, keys), WIDE),
            jax.ShapeDtypeStruct((rows, heads * HEAD_DIM), WIDE),
            jax.ShapeDtypeStruct((rows, heads * HEAD_DIM), LOW),
        ],
        cost_estimate=pl.CostEstimate(
            flops=4 * heads * rows * keys * HEAD_DIM,
            bytes_accessed=4 * heads * rows * keys + 4 * keys * HEAD_DIM + 14 * rows * heads * HEAD_DIM,
            transcendentals=heads * rows * keys,
        ),
    )(projected, gain, cosine, sine, query_places, key_limit, keys_values)


def attention_back_kernel(
    grad_ref, wide_ref, probs_ref, q_ref, raw_ref, gain_ref, cos_ref, sin_ref, kv_ref,
    grad_raw_ref, grad_gain_ref, grad_kv_ref, total,
):
    head, step = pl.program_id(0), pl.program_id(1)
    first = jnp.logical_and(head == 0, step == 0)
    last = jnp.logical_and(head == pl.num_programs(0) - 1, step == pl.num_programs(1) - 1)
    grad = grad_ref[...]
    delta = jnp.sum(grad.astype(WIDE) * wide_ref[...], axis=-1, keepdims=True)
    probs = probs_ref[0]
    grad_probs = contract_last(grad, kv_ref[:, HEAD_DIM:])
    grad_scores = (probs * (grad_probs - delta)).astype(LOW)
    rotated = jnp.dot(grad_scores, kv_ref[:, :HEAD_DIM], preferred_element_type=WIDE)
    key_part = over_rows(grad_scores, q_ref[...])
    value_part = over_rows(probs.astype(LOW), grad)

    @pl.when(first)
    def _():
        total[:, :HEAD_DIM] = key_part
        total[:, HEAD_DIM:] = value_part

    @pl.when(jnp.logical_not(first))
    def _():
        total[:, :HEAD_DIM] += key_part
        total[:, HEAD_DIM:] += value_part

    @pl.when(last)
    def _():
        grad_kv_ref[...] = total[...].astype(LOW)

    half = rotated.shape[1] // 2
    front, behind = rotated[:, :half], rotated[:, half:]
    cosine, sine = cos_ref[...], sin_ref[...]
    back = jnp.concatenate([front * cosine + behind * sine, behind * cosine - front * sine], axis=1)
    raw = raw_ref[...]
    scale = lax.rsqrt(jnp.mean(raw * raw, axis=-1, keepdims=True) + EPSILON)
    normed = raw * scale
    gain_part = jnp.sum(back * normed, axis=0, keepdims=True)

    @pl.when(first)
    def _():
        grad_gain_ref[...] = gain_part

    @pl.when(jnp.logical_not(first))
    def _():
        grad_gain_ref[...] += gain_part

    back = back * gain_ref[...]
    grad_raw_ref[...] = (
        scale * (back - normed * jnp.mean(back * normed, axis=-1, keepdims=True))
    ).astype(LOW)


def attention_backward(grad, wide, probs, q_low, projected, gain, cosine, sine, keys_values):
    heads, rows, keys = probs.shape
    block = min(rows, 256, (1 << 19) // keys)

    def tile(h, i):
        return (i, h)

    def whole(h, i):
        return (0, 0)

    return pl.pallas_call(
        attention_back_kernel,
        grid=(heads, rows // block),
        in_specs=[
            pl.BlockSpec((block, HEAD_DIM), tile),
            pl.BlockSpec((block, HEAD_DIM), tile),
            pl.BlockSpec((1, block, keys), lambda h, i: (h, i, 0)),
            pl.BlockSpec((block, HEAD_DIM), tile),
            pl.BlockSpec((block, HEAD_DIM), tile),
            pl.BlockSpec((1, HEAD_DIM), whole),
            pl.BlockSpec((block, HEAD_DIM // 2), lambda h, i: (i, 0)),
            pl.BlockSpec((block, HEAD_DIM // 2), lambda h, i: (i, 0)),
            pl.BlockSpec((keys, 2 * HEAD_DIM), whole),
        ],
        out_specs=[
            pl.BlockSpec((block, HEAD_DIM), tile),
            pl.BlockSpec((1, HEAD_DIM), whole),
            pl.BlockSpec((keys, 2 * HEAD_DIM), whole),
        ],
        out_shape=[
            jax.ShapeDtypeStruct((rows, heads * HEAD_DIM), LOW),
            jax.ShapeDtypeStruct((1, HEAD_DIM), WIDE),
            jax.ShapeDtypeStruct((keys, 2 * HEAD_DIM), LOW),
        ],
        scratch_shapes=[pltpu.VMEM((keys, 2 * HEAD_DIM), WIDE)],
        cost_estimate=pl.CostEstimate(
            flops=8 * heads * rows * keys * HEAD_DIM,
            bytes_accessed=4 * heads * rows * keys + 8 * keys * HEAD_DIM + 14 * rows * heads * HEAD_DIM,
            transcendentals=0,
        ),
    )(grad, wide, probs, q_low, projected, gain, cosine, sine, keys_values)


def widen_kernel(places, source, gate, up):
    gate[...] = source[0, 0, 0].astype(WIDE)
    up[...] = source[0, 0, 1].astype(WIDE)


def widen_pair(pieces, places):
    parts, run, _, rows, width = pieces.shape
    return pl.pallas_call(
        widen_kernel,
        grid_spec=pltpu.PrefetchScalarGridSpec(
            num_scalar_prefetch=1,
            grid=(run, parts),
            in_specs=[pl.BlockSpec((1, 1, 2, rows, width), lambda k, r, p: (r, k, 0, 0, 0))],
            out_specs=[pl.BlockSpec((rows, width), lambda k, r, p: (0, p[k] * parts + r))] * 2,
        ),
        out_shape=[jax.ShapeDtypeStruct((rows, width * parts * run), WIDE)] * 2,
        cost_estimate=pl.CostEstimate(flops=0, bytes_accessed=6 * pieces.size, transcendentals=0),
    )(places, pieces)


def shift_blocks(make):
    run = lax.axis_size("wsh")
    here = lax.axis_index("wsh")
    received = []
    for k in range(run):
        block = make((here + k) % run)
        if k:
            block = lax.ppermute(block, "wsh", [(i, (i + k) % run) for i in range(run)])
        received.append(block)
    return received


def shift_exchange(make):
    run = lax.axis_size("wsh")
    order = (lax.axis_index("wsh") - jnp.arange(run, dtype=jnp.int32)) % run
    return jnp.take(jnp.stack(shift_blocks(make)), order, axis=0)


def place_kernel(places, *refs):
    step = pl.program_id(0)
    sources, out = refs[:-1], refs[-1]
    for number, source in enumerate(sources):

        @pl.when(step == number)
        def _(source=source):
            out[...] = source[...]


def place_columns(blocks, places):
    rows, width = blocks[0].shape
    count = len(blocks)
    return pl.pallas_call(
        place_kernel,
        grid_spec=pltpu.PrefetchScalarGridSpec(
            num_scalar_prefetch=1,
            grid=(count,),
            in_specs=[pl.BlockSpec((rows, width), lambda k, p: (0, 0))] * count,
            out_specs=pl.BlockSpec((rows, width), lambda k, p: (0, p[k])),
        ),
        out_shape=jax.ShapeDtypeStruct((rows, width * count), blocks[0].dtype),
        cost_estimate=pl.CostEstimate(
            flops=0, bytes_accessed=4 * count * blocks[0].size, transcendentals=0
        ),
    )(places, *blocks)


def entry(stacked):
    return lambda index: lax.dynamic_index_in_dim(stacked, index, 0, False)


def shards(
    tokens,
    cotangent,
    lengths,
    positions,
    token_ids,
    per_layer_table,
    w_query,
    w_key,
    w_value,
    w_output,
    laurel_left,
    laurel_right,
    w_gate,
    w_up,
    w_down,
    w_layer_gate,
    w_layer_proj,
    norm_gains,
    query_gain,
    key_gain,
):
    rows_dev, width = tokens.shape[1:]
    run = lax.axis_size("wsh")
    contexts = lax.axis_size("ctx")
    parts = 2 * contexts
    chip = lax.axis_index(COPIES)
    shard_rows = width // run
    heads_here = HEADS // run
    groups = HEADS // KV_HEADS
    query_width = heads_here * HEAD_DIM
    head_width = query_width + 2 * HEAD_DIM
    hidden_width = w_gate.shape[1] // run
    head_piece = shard_rows // parts
    piece = hidden_width // parts
    rank = laurel_left.shape[1]
    places = ((lax.axis_index("wsh") - jnp.arange(run)) % run).astype(jnp.int32)
    gain_cut = query_gain.shape[0]

    def share(weight):
        return lax.dynamic_slice_in_dim(weight, chip * head_piece, head_piece, 0)

    query_rows, key_rows, value_rows = share(w_query), share(w_key), share(w_value)

    indices = shift_exchange(lambda k: jnp.concatenate([token_ids, positions], axis=0))
    small = jnp.concatenate(
        [
            norm_gains.T,
            jnp.pad(
                jnp.concatenate([query_gain, key_gain])[None],
                ((0, 1), (0, shard_rows - 2 * gain_cut)),
            ),
        ],
        axis=0,
    )
    proj_rows = w_layer_proj.shape[0]
    proj_share = lax.dynamic_slice_in_dim(w_layer_proj, chip * (width // parts), width // parts, 1)
    common = jnp.concatenate(
        [
            share(laurel_left),
            share(laurel_right),
            share(w_layer_gate),
            proj_share.reshape(head_piece, -1),
        ],
        axis=1,
    )
    fetch_width = head_width + common.shape[1]
    small_flat = jnp.pad(small.reshape(-1), (0, -small.size % fetch_width)).reshape(-1, fetch_width)
    small_flat = jnp.pad(small_flat, ((0, 16 - small_flat.shape[0]), (0, 0)))
    common, query_rows, key_rows, value_rows, small_flat, indices = lax.optimization_barrier(
        (common, query_rows, key_rows, value_rows, small_flat, indices)
    )

    def head_block(index):
        kv = index * heads_here // groups * HEAD_DIM
        block = jnp.concatenate(
            [
                lax.dynamic_slice_in_dim(query_rows, index * query_width, query_width, 1),
                lax.dynamic_slice_in_dim(key_rows, kv, HEAD_DIM, 1),
                lax.dynamic_slice_in_dim(value_rows, kv, HEAD_DIM, 1),
                common,
            ],
            axis=1,
        )
        return jnp.concatenate([small_flat, block], axis=0)

    head_share = shift_exchange(head_block)
    small_all = head_share[:, :16].reshape(run, -1)[:, : small.size].reshape(run, 8, shard_rows)
    fetched = lax.all_gather(head_share[:, 16:], COPIES, axis=0)
    w_heads = fetched[:, :, :, :head_width]
    proj_at = head_width + 2 * rank + w_layer_gate.shape[1]
    layer_proj_full = fetched[:, :, :, proj_at:].reshape(parts, run, proj_rows, width // parts)
    layer_proj_full = layer_proj_full.transpose(1, 2, 0, 3).reshape(run * proj_rows, width)
    laurel_weights = fetched[:, :, :, head_width:proj_at].transpose(1, 0, 2, 3).reshape(width, -1)
    left_full = laurel_weights[:, :rank]
    right_full = laurel_weights[:, rank : 2 * rank]
    layer_gate_full = laurel_weights[:, 2 * rank :]
    w_heads = w_heads.transpose(1, 0, 2, 3).reshape(width, head_width)

    gains_full = small_all.transpose(1, 0, 2).reshape(8, width).astype(WIDE)
    query_gain_full = small_all[:, 6, :gain_cut].reshape(HEAD_DIM).astype(WIDE)
    key_gain_full = small_all[:, 6, gain_cut : 2 * gain_cut].reshape(HEAD_DIM).astype(WIDE)
    tokens_run = spread(tokens[0], "wsh")

    indices = indices[None]
    bit = 1
    while bit < contexts:
        indices = jnp.concatenate([indices, swap(indices, "ctx", bit)], axis=0)
        bit *= 2
    run_places = indices[0, :, 1].reshape(-1)
    here_ctx = lax.axis_index("ctx")
    context_order = jnp.bitwise_xor(jnp.arange(contexts, dtype=jnp.int32), here_ctx)
    key_places = jnp.take(indices[:, :, 1], context_order, axis=0).reshape(-1)
    own_ids = indices[:, :, 0].reshape(-1)
    all_ids = jnp.concatenate([own_ids, swap(own_ids, "slot", 1)])
    length = lengths[0]

    vocab_rows = per_layer_table.shape[0]
    vocab_first = lax.axis_index(EVERY) * vocab_rows
    vocab_range = jnp.arange(vocab_rows, dtype=jnp.int32)

    def one_hot():
        return ((all_ids - vocab_first)[:, None] == vocab_range[None, :]).astype(LOW)

    table_rows = matmul(one_hot(), per_layer_table).astype(LOW)
    tokens_run, table_rows = lax.optimization_barrier((tokens_run, table_rows))
    def pair_block(index):
        first = index * hidden_width + chip * piece
        gate_cut = lax.dynamic_slice_in_dim(w_gate, first, piece, 1)
        up_cut = lax.dynamic_slice_in_dim(w_up, first, piece, 1)
        gate_cut, up_cut = after((gate_cut, up_cut), head_share)
        return jnp.concatenate([gate_cut.T, up_cut.T], axis=0)

    pair_received = shift_blocks(pair_block)
    normed_run = rms_norm(tokens_run.astype(WIDE), gains_full[0]).astype(LOW)
    tokens_f = tokens[0].astype(WIDE)
    normed = rms_norm(tokens_f, gains_full[0])
    normed_low = normed.astype(LOW)
    total_rows = run * rows_dev
    projected = matmul(normed_run, w_heads)
    key = projected[:, query_width : query_width + HEAD_DIM]
    value = projected[:, query_width + HEAD_DIM :]

    def key_path(raw, gain):
        return rotate(rms_norm(raw.reshape(total_rows, 1, HEAD_DIM), gain), run_places)[:, 0]

    def value_path(raw):
        return rms_norm(raw, 1.0)

    k_low = key_path(key, key_gain_full).astype(LOW)
    v_low = value_path(value).astype(LOW)
    keys_values = spread(jnp.concatenate([k_low, v_low], axis=1), "ctx")
    half = table_rows.shape[0] // 2
    looked_up = add_low(table_rows[:half], swap(table_rows[half:], "slot", 1))
    bit = contexts // 2
    while bit:
        half = looked_up.shape[0] // 2
        looked_up = add_low(looked_up[:half], swap(looked_up[half:], "ctx", bit))
        bit //= 2
    looked_up = looked_up.reshape(run, rows_dev, -1)
    inverse = jnp.exp(
        -math.log(ROPE_BASE)
        * (2.0 * jnp.arange(HEAD_DIM // 2, dtype=jnp.float32) / HEAD_DIM)
    )
    angles = run_places.astype(WIDE)[:, None] * inverse[None, :]
    cosine, sine = jnp.cos(angles), jnp.sin(angles)
    key_limit = jnp.where(key_places < length, key_places, jnp.int32(1 << 30))
    q_low, probs, attended, attended_low = attention_forward(
        projected,
        query_gain_full[None],
        cosine,
        sine,
        run_places[:, None],
        key_limit[None],
        keys_values,
        heads_here,
    )
    attended_low, pair_received = lax.optimization_barrier((attended_low, pair_received))
    pair_share = place_columns(pair_received, places)
    pair_weight = lax.all_gather(pair_share, COPIES, axis=0, tiled=True)
    attn_proj = collect(matmul(attended_low, w_output).astype(LOW), "wsh")
    attn_proj, looked_up = lax.optimization_barrier((attn_proj, looked_up))

    first_sum = tokens_f + rms_norm(attn_proj, gains_full[1])
    low_rank_low = matmul(normed_low, left_full).astype(LOW)
    laurel_out = times_transposed(low_rank_low, right_full)
    laurel = normed + rms_norm(laurel_out, gains_full[2])
    mixed = (first_sum + laurel) * HALF_ROOT
    ff_in_low = rms_norm(mixed, gains_full[3]).astype(LOW)

    ff_run = spread(ff_in_low, "wsh")
    looked_up = after(looked_up, ff_run)
    layer_input = EMBED_SCALE * jnp.sum(shift_exchange(entry(looked_up)).astype(WIDE), axis=0)
    aligned = piece % 128 == 0
    if aligned:
        both, hidden_low, ff_part = ff_forward(ff_run, pair_weight, w_down, piece)
    else:
        both = times_transposed(ff_run, pair_weight)
        both_parts = both.reshape(total_rows, parts, 2, piece)
        gate = both_parts[:, :, 0].reshape(total_rows, hidden_width)
        upward = both_parts[:, :, 1].reshape(total_rows, hidden_width)
        hidden_low = gated_product(gate, upward).astype(LOW)
        ff_part = matmul(hidden_low, w_down).astype(LOW)
    ff_part, layer_input = lax.optimization_barrier((ff_part, layer_input))
    ff_out = collect(ff_part, "wsh")
    third_sum = mixed + rms_norm(ff_out, gains_full[4])
    third_low = third_sum.astype(LOW)

    layer_gate = matmul(third_low, layer_gate_full)
    gated_low = gated_product(layer_gate, layer_input).astype(LOW)
    layer_proj = matmul(gated_low, layer_proj_full)
    result = third_sum + rms_norm(layer_proj, gains_full[5])
    layer_out = result.astype(LOW)[None]

    valid = (positions[0] < length).astype(WIDE)
    grad_out = cotangent[0].astype(WIDE) * valid[:, None]
    _, pullback = jax.vjp(rms_norm, layer_proj, gains_full[5])
    grad_proj, grad_gain_five = pullback(grad_out)
    grad_proj_low = grad_proj.astype(LOW)
    grad_gated = times_transposed(grad_proj_low, layer_proj_full)
    _, pullback = jax.vjp(gated_product, layer_gate, layer_input)
    grad_lgate, grad_input = pullback(grad_gated)
    grad_lgate_low = grad_lgate.astype(LOW)
    grad_input_low = grad_input.astype(LOW)
    grad_third = grad_out + times_transposed(grad_lgate_low, layer_gate_full)
    _, pullback = jax.vjp(rms_norm, ff_out, gains_full[4])
    grad_ff, grad_gain_four = pullback(grad_third)
    grad_ff_low = grad_ff.astype(LOW)

    grad_ff_run = spread(grad_ff_low, "wsh")
    down_part = over_rows(hidden_low, grad_ff_run).astype(LOW)
    grad_ff_run, down_part = lax.optimization_barrier((grad_ff_run, down_part))
    down_own = lax.psum_scatter(down_part, COPIES, scatter_dimension=0, tiled=True)
    grad_input_low = after(grad_input_low, grad_ff_run)
    every_grad = shift_exchange(lambda k: grad_input_low).reshape(total_rows, -1)

    def wider(rows, axis, bit):
        return jnp.concatenate([rows, swap(rows, axis, bit)], axis=0)

    hops = [1 << power for power in range(contexts.bit_length() - 1)]
    if aligned:
        grad_both, ff_part = ff_backward(grad_ff_run, pair_weight, w_down, both, piece)
    else:
        grad_hidden = times_transposed(grad_ff_run, w_down)
        _, pullback = jax.vjp(gated_product, gate, upward)
        grad_gate, grad_upward = pullback(grad_hidden)
        grad_both = jnp.stack(
            [
                grad_gate.reshape(total_rows, parts, piece),
                grad_upward.reshape(total_rows, parts, piece),
            ],
            axis=2,
        )
        grad_both = grad_both.reshape(total_rows, 2 * hidden_width).astype(LOW)
        ff_part = matmul(grad_both, pair_weight).astype(LOW)
    ff_part, every_grad = lax.optimization_barrier((ff_part, every_grad))
    every_grad = wider(every_grad, "ctx", hops[0])
    grad_ff_in = collect(ff_part, "wsh")
    pair_part = over_rows(after(grad_both, ff_part), ff_run).astype(LOW)
    grad_ff_in, pair_part, every_grad = lax.optimization_barrier((grad_ff_in, pair_part, every_grad))
    for bit in hops[1:]:
        every_grad = wider(every_grad, "ctx", bit)
    pair_own = lax.psum_scatter(pair_part, COPIES, scatter_dimension=0, tiled=True)
    _, pullback = jax.vjp(rms_norm, mixed, gains_full[3])
    grad_mixed_norm, grad_gain_three = pullback(grad_ff_in)
    grad_branch = (grad_third + grad_mixed_norm) * HALF_ROOT
    _, pullback = jax.vjp(rms_norm, attn_proj, gains_full[1])
    grad_attn, grad_gain_one = pullback(grad_branch)
    grad_attn_low = grad_attn.astype(LOW)
    grad_attn_run = spread(grad_attn_low, "wsh")
    grad_attn_run, down_own, every_grad = lax.optimization_barrier(
        (grad_attn_run, down_own, every_grad)
    )
    every_grad = wider(every_grad, "slot", 1)
    down_grad = lax.all_gather(down_own, COPIES, axis=0, tiled=True)

    def pair_back(index):
        block = lax.dynamic_slice_in_dim(pair_own, index * shard_rows, shard_rows, 1)
        return block.reshape(2, piece, shard_rows).transpose(0, 2, 1)

    _, pullback = jax.vjp(rms_norm, laurel_out, gains_full[2])
    grad_laurel, grad_gain_two = pullback(grad_branch)
    grad_laurel_low = grad_laurel.astype(LOW)
    grad_rank_low = matmul(grad_laurel_low, right_full).astype(LOW)

    left_grad = over_rows(normed_low, grad_rank_low)
    right_grad = over_rows(grad_laurel_low, low_rank_low)
    layer_gate_grad = over_rows(third_low, grad_lgate_low)
    layer_proj_grad = over_rows(gated_low, grad_proj_low)

    narrow = jnp.concatenate([left_grad, right_grad, layer_gate_grad], axis=1).astype(LOW)
    narrow_columns = narrow.shape[1]
    proj_back = layer_proj_grad.astype(LOW).reshape(run, proj_rows, parts, width // parts)
    proj_back = proj_back.transpose(0, 2, 1, 3).reshape(run, parts, head_piece, -1)
    narrow = jnp.concatenate(
        [narrow.reshape(run, parts, head_piece, narrow_columns), proj_back], axis=3
    )

    grad_att_low = times_transposed(grad_attn_run, w_output).astype(LOW)
    grad_query, grad_query_gain, kv_part = attention_backward(
        grad_att_low,
        attended,
        probs,
        q_low,
        projected,
        query_gain_full[None],
        cosine,
        sine,
        keys_values,
    )
    grad_query_gain = grad_query_gain[0]
    kv_sum = collect(kv_part, "ctx")
    output_part = over_rows(attended_low, grad_attn_run).astype(LOW)
    kv_sum, pair_own, output_part, narrow, every_grad = lax.optimization_barrier(
        (kv_sum, pair_own, output_part, narrow, every_grad)
    )
    pair_blocks = jnp.stack(shift_blocks(pair_back))
    _, pullback = jax.vjp(key_path, key, key_gain_full)
    grad_key, grad_key_gain = pullback(kv_sum[:, :HEAD_DIM])
    _, pullback = jax.vjp(value_path, value)
    (grad_value,) = pullback(kv_sum[:, HEAD_DIM:])
    grad_heads = jnp.concatenate(
        [grad_query, grad_key.astype(LOW), grad_value.astype(LOW)], axis=1
    )
    heads_part = over_rows(normed_run, grad_heads).astype(LOW)
    heads_part = heads_part.reshape(run, parts, head_piece, head_width)
    heads_part = jnp.concatenate(
        [one[index] for index in range(run) for one in (heads_part, narrow)]
        + [output_part.reshape(parts, head_piece, width)],
        axis=2,
    )
    fetch_back = head_width + narrow.shape[3]
    heads_kept, heads_given = halves(heads_part)
    normed_part = times_transposed(grad_heads, w_heads).astype(LOW)
    heads_pieces = [add_low(a, b) for a, b in zip(nearest(heads_kept), nearest(heads_given))]
    heads_first = reduce_first(heads_pieces)
    normed_part, heads_first, pair_blocks, down_grad = lax.optimization_barrier(
        (normed_part, heads_first, pair_blocks, down_grad)
    )
    pair_all = lax.all_gather(pair_blocks, COPIES, axis=0)
    table_grad = EMBED_SCALE * over_rows(one_hot(), after(every_grad, normed_part))
    heads_second = reduce_second(heads_pieces, heads_first)
    grad_run = collect(normed_part, "wsh")
    grad_run, heads_second, table_grad = lax.optimization_barrier(
        (grad_run, heads_second, table_grad)
    )
    heads_own = reduce_last(heads_pieces, heads_second)
    output_own = heads_own[:, run * fetch_back :]

    def head_back(index):
        return lax.dynamic_slice_in_dim(heads_own, index * fetch_back, fetch_back, 1)

    heads_sent = shift_exchange(head_back).astype(WIDE)
    grad_normed = (
        grad_run
        + times_transposed(grad_rank_low, left_full)
        + grad_branch
    )
    _, pullback = jax.vjp(rms_norm, tokens_f, gains_full[0])
    grad_tokens, grad_gain_zero = pullback(grad_normed)
    tokens_grad = (grad_tokens + grad_branch).astype(LOW)[None]

    vector = jnp.concatenate(
        [grad_query_gain.reshape(run, gain_cut), grad_key_gain.reshape(run, gain_cut)], axis=1
    )
    vector = jnp.pad(vector, ((0, 0), (0, shard_rows - 2 * gain_cut))).reshape(width)
    gain_sums = jnp.stack(
        [
            grad_gain_zero,
            grad_gain_one,
            grad_gain_two,
            grad_gain_three,
            grad_gain_four,
            grad_gain_five,
            vector,
            jnp.zeros_like(vector),
        ]
    )
    gain_sums = gain_sums.reshape(8, run, shard_rows).transpose(1, 0, 2).reshape(8 * run, shard_rows)
    gain_sums = collect(gain_sums, "wsh")
    pieces = [heads_sent[:, :, :query_width].transpose(1, 0, 2).reshape(head_piece, -1)]
    for begin in (query_width, query_width + HEAD_DIM):
        one = heads_sent[:, :, begin : begin + HEAD_DIM]
        one = one.reshape(KV_HEADS, run // KV_HEADS, head_piece, HEAD_DIM).sum(axis=1)
        pieces.append(one.transpose(1, 0, 2).reshape(head_piece, -1))
    begin = head_width
    for size in (rank, rank, w_layer_gate.shape[1]):
        pieces.append(heads_sent[:, :, begin : begin + size].sum(axis=0))
        begin += size
    pieces.append(heads_sent[:, :, head_width + narrow_columns :].sum(axis=0))
    pieces.append(output_own.astype(WIDE))
    cuts = []
    for one in pieces:
        cuts.append((sum(w for _, w in cuts), one.shape[1]))
    heads_piece = jnp.concatenate(pieces, axis=1).astype(LOW)
    heads_piece, gain_sums = lax.optimization_barrier((heads_piece, gain_sums))
    heads_near = gather_first(heads_piece)
    gain_sums = jnp.sum(spread(gain_sums[None], COPIES), axis=0)
    own = jnp.full((1,), chip, jnp.int32)
    if aligned:
        gate_grad, up_grad = widen_pair(pair_all, places)
    else:
        pair_all = jnp.take(pair_all, places, axis=1)
        pair_all = pair_all.transpose(2, 3, 1, 0, 4).reshape(2, shard_rows, -1).astype(WIDE)
        gate_grad, up_grad = pair_all[0], pair_all[1]
    down_grad = after(down_grad, heads_piece).astype(WIDE)
    heads_near, down_grad, gain_sums = lax.optimization_barrier((heads_near, down_grad, gain_sums))
    heads_near = gather_second(heads_piece, heads_near)
    heads_near, gate_grad, up_grad = lax.optimization_barrier((heads_near, gate_grad, up_grad))
    heads_all = last_gather(heads_near)
    (
        query_grad,
        key_grad,
        value_grad,
        left_grad,
        right_grad,
        layer_gate_grad,
        layer_proj_grad,
        output_grad,
    ) = assemble(
        [p[None] for p in heads_all], own, WIDE, cuts
    )
    layer_proj_grad = layer_proj_grad.reshape(parts, proj_rows, width // parts)
    layer_proj_grad = layer_proj_grad.transpose(1, 0, 2).reshape(proj_rows, width)

    return (
        layer_out,
        tokens_grad,
        table_grad,
        query_grad.reshape(shard_rows, -1),
        key_grad.reshape(shard_rows, -1),
        value_grad.reshape(shard_rows, -1),
        output_grad.reshape(query_width, width),
        left_grad.reshape(shard_rows, -1),
        right_grad.reshape(shard_rows, -1),
        gate_grad,
        up_grad,
        down_grad,
        layer_gate_grad.reshape(shard_rows, -1),
        layer_proj_grad,
        gain_sums[:6].T,
        gain_sums[6, :gain_cut],
        gain_sums[6, gain_cut : 2 * gain_cut],
    )


def solution(mesh):
    placed = (
        P("slot", ("ctx", "wsh"), None),
        P("slot", ("ctx", "wsh"), None),
        P("slot"),
        P("slot", ("ctx", "wsh")),
        P("slot", ("ctx", "wsh")),
        P(("slot", "ctx", "wsh"), None),
        P("wsh", None),
        P("wsh", None),
        P("wsh", None),
        P("wsh", None),
        P("wsh", None),
        P("wsh", None),
        P("wsh", None),
        P("wsh", None),
        P("wsh", None),
        P("wsh", None),
        P("wsh", None),
        P("wsh", None),
        P("wsh"),
        P("wsh"),
    )
    return jax.shard_map(
        shards,
        mesh=mesh,
        in_specs=placed,
        out_specs=(
            P("slot", ("ctx", "wsh"), None),
            P("slot", ("ctx", "wsh"), None),
            P(("slot", "ctx", "wsh"), None),
            P("wsh", None),
            P("wsh", None),
            P("wsh", None),
            P("wsh", None),
            P("wsh", None),
            P("wsh", None),
            P("wsh", None),
            P("wsh", None),
            P("wsh", None),
            P("wsh", None),
            P("wsh", None),
            P("wsh", None),
            P("wsh"),
            P("wsh"),
        ),
        check_vma=False,
    )
```

```python
import functools
import math

import jax
import jax.numpy as jnp
from jax import lax
from jax.experimental import pallas as pl
from jax.experimental.pallas import tpu as pltpu
from jax.sharding import PartitionSpec as P

HEADS = 8
KV_HEADS = 2
HEAD_DIM = 256


EPSILON = 1e-06
ROPE_BASE = 1000000.0
HALF_ROOT = 0.7071067811865476
TANH_SCALE = 0.7978845608028654
NEGATIVE = -1e30
EMBED_SCALE = 16.0


def rms_norm(value, gain):
    return value * lax.rsqrt(jnp.mean(value * value, axis=-1, keepdims=True) + EPSILON) * gain


def gelu_tanh(value):
    return 0.5 * value * (1.0 + jnp.tanh(TANH_SCALE * (value + 0.044715 * value * value * value)))


def gated_product(pre_gate, other_side):
    return gelu_tanh(pre_gate) * other_side


def rotate(value, places):
    width_all = value.shape[-1]
    half_width = width_all // 2
    inverse = jnp.exp(
        -math.log(ROPE_BASE) * (2.0 * jnp.arange(half_width, dtype=jnp.float32) / width_all)
    )
    angles = places.astype(jnp.float32)[:, None] * inverse[None, :]
    cosine = jnp.cos(angles)[:, None, :]
    sine = jnp.sin(angles)[:, None, :]
    front = value[..., :half_width]
    behind = value[..., half_width:]
    return jnp.concatenate(
        [front * cosine - behind * sine, behind * cosine + front * sine], axis=-1
    )


def matmul(left, right):
    return jnp.dot(left, right, preferred_element_type=jnp.float32)


def times_transposed(left, right):
    return lax.dot_general(
        left, right, (((1,), (1,)), ((), ())), preferred_element_type=jnp.float32
    )


def over_rows(left, right):
    return lax.dot_general(
        left, right, (((0,), (0,)), ((), ())), preferred_element_type=jnp.float32
    )


LOW = jnp.bfloat16
WIDE = jnp.float32
EVERY = ("slot", "ctx", "wsh")
COPIES = ("slot", "ctx")


def after(value, *others):
    return lax.optimization_barrier((value, others))[0]


def exchange(value, axis):
    return lax.all_to_all(value, axis, 0, 0, tiled=True)


def spread(value, axis):
    size = lax.axis_size(axis)
    copies = jnp.broadcast_to(value[None], (size,) + value.shape)
    return exchange(copies.reshape((size * value.shape[0],) + value.shape[1:]), axis)


def collect(parts, axis):
    size = lax.axis_size(axis)
    received = exchange(parts, axis)
    received = received.reshape((size, parts.shape[0] // size) + parts.shape[1:])
    return jnp.sum(received.astype(WIDE), axis=0)


def swap(value, axis, bit):
    size = lax.axis_size(axis)
    return lax.ppermute(value, axis, [(i, i ^ bit) for i in range(size)])


def add_low(left, right):
    return (left.astype(WIDE) + right.astype(WIDE)).astype(LOW)


def gather_first(piece):
    if lax.axis_size("ctx") == 4:
        return [swap(piece, "ctx", 1), swap(piece, "ctx", 2)]
    return []


def gather_second(piece, first):
    if first:
        one, two = first
        half = piece.shape[0] // 2
        front = swap(one[:half], "ctx", 2)
        behind = swap(two[half:], "ctx", 1)
        return [piece, one, two, jnp.concatenate([front, behind], axis=0)]
    pieces = [piece]
    bit = 1
    while bit < lax.axis_size("ctx"):
        pieces = pieces + [swap(p, "ctx", bit) for p in pieces]
        bit *= 2
    return pieces


def reduce_first(pieces):
    if len(pieces) == 4:
        half = pieces[0].shape[0] // 2
        return [swap(pieces[3][:half], "ctx", 1), swap(pieces[3][half:], "ctx", 2)]
    return []


def reduce_second(pieces, first):
    if first:
        front, behind = first
        half = pieces[0].shape[0] // 2
        two = jnp.concatenate([add_low(pieces[2][:half], front), pieces[2][half:]], axis=0)
        one = jnp.concatenate([pieces[1][:half], add_low(pieces[1][half:], behind)], axis=0)
        return [swap(one, "ctx", 1), swap(two, "ctx", 2)]
    return []


def reduce_last(pieces, second):
    if second:
        one, two = second
        return (pieces[0].astype(WIDE) + one.astype(WIDE) + two.astype(WIDE)).astype(LOW)
    size = len(pieces)
    while size > 1:
        size //= 2
        pieces = [add_low(pieces[i], swap(pieces[size + i], "ctx", size)) for i in range(size)]
    return pieces[0]


def assemble_kernel(extent, cuts, own, *refs):
    step = pl.program_id(0)
    ins, outs = refs[:extent], refs[extent:]
    for number in range(extent):

        @pl.when(step == number)
        def _(number=number):
            for (begin, width), out in zip(cuts, outs):
                out[:, 0] = ins[number][:, :, begin : begin + width].astype(out.dtype)


def assemble(pieces, own, kind, cuts=None):
    count = len(pieces)
    outer, inner, width = pieces[0].shape
    cuts = cuts or [(0, width)]
    results = pl.pallas_call(
        functools.partial(assemble_kernel, count, cuts),
        grid_spec=pltpu.PrefetchScalarGridSpec(
            num_scalar_prefetch=1,
            grid=(count,),
            in_specs=[pl.BlockSpec((outer, inner, width), lambda i, o: (0, 0, 0))] * count,
            out_specs=[
                pl.BlockSpec((outer, 1, inner, w), lambda i, o: (0, lax.bitwise_xor(i, o[0]), 0, 0))
                for _, w in cuts
            ],
        ),
        out_shape=[jax.ShapeDtypeStruct((outer, count, inner, w), kind) for _, w in cuts],
    )(own, *pieces)
    return results


def halves(blocks):
    count = blocks.shape[0] // 2
    slot = lax.axis_index("slot")
    kept = lax.dynamic_slice_in_dim(blocks, slot * count, count, 0)
    given = lax.dynamic_slice_in_dim(blocks, (1 - slot) * count, count, 0)
    return kept, swap(given, "slot", 1)


def nearest(blocks):
    here = lax.axis_index("ctx")
    count = blocks.shape[0]
    return [lax.dynamic_index_in_dim(blocks, here ^ r, 0, False) for r in range(count)]


def last_gather(pieces):
    return pieces + [swap(p, "slot", 1) for p in pieces]


def contract_last(left, right):
    return lax.dot_general(left, right, (((1,), (1,)), ((), ())), preferred_element_type=WIDE)


def gelu_and_slope(value):
    inner = jnp.tanh(TANH_SCALE * (value + 0.044715 * value * value * value))
    slope = 0.5 * (1.0 + inner) + 0.5 * value * (1.0 - inner * inner) * TANH_SCALE * (
        1.0 + 3.0 * 0.044715 * value * value
    )
    return 0.5 * value * (1.0 + inner), slope


def ff_forward_kernel(piece, many, count, x_ref, pair_ref, down_ref, both_ref, hidden_ref, out_ref):
    step = pl.program_id(0)

    @pl.when(step < count)
    def _():
        both = contract_last(x_ref[...], pair_ref[...])
        both_ref[...] = both
        for part in range(many):
            begin = 2 * part * piece
            gate = both[:, begin : begin + piece]
            upward = both[:, begin + piece : begin + 2 * piece]
            start = pl.multiple_of((step * many + part) * piece, piece)
            hidden_ref[:, pl.ds(start, piece)] = (gelu_tanh(gate) * upward).astype(LOW)

    @pl.when(step >= count)
    def _():
        out_ref[...] = jnp.dot(
            hidden_ref[...], down_ref[...], preferred_element_type=WIDE
        ).astype(LOW)


def ff_forward(x, pair, down, piece):
    rows, width = x.shape
    hidden = down.shape[0]
    many = math.gcd(hidden // piece, 2)
    count = hidden // piece // many
    cut = math.gcd(width, 1024)

    def now(i):
        return jnp.minimum(i, count - 1)

    def then(i):
        return jnp.maximum(i - count, 0)

    return pl.pallas_call(
        functools.partial(ff_forward_kernel, piece, many, count),
        grid=(count + width // cut,),
        in_specs=[
            pl.BlockSpec((rows, width), lambda i: (0, 0)),
            pl.BlockSpec((2 * many * piece, width), lambda i: (now(i), 0)),
            pl.BlockSpec((hidden, cut), lambda i: (0, then(i))),
        ],
        out_specs=[
            pl.BlockSpec((rows, 2 * many * piece), lambda i: (0, now(i))),
            pl.BlockSpec((rows, hidden), lambda i: (0, 0)),
            pl.BlockSpec((rows, cut), lambda i: (0, then(i))),
        ],
        out_shape=[
            jax.ShapeDtypeStruct((rows, 2 * hidden), WIDE),
            jax.ShapeDtypeStruct((rows, hidden), LOW),
            jax.ShapeDtypeStruct((rows, width), LOW),
        ],
        cost_estimate=pl.CostEstimate(
            flops=6 * rows * width * hidden,
            bytes_accessed=6 * width * hidden + 10 * rows * hidden,
            transcendentals=rows * hidden,
        ),
    )(x, pair, down)


def ff_backward_kernel(
    piece, many, count, grad_ref, down_ref, both_ref, pair_ref, grad_both_ref, out_ref
):
    step = pl.program_id(0)

    @pl.when(step < count)
    def _():
        grad_hidden = contract_last(grad_ref[...], down_ref[...])
        for part in range(many):
            grad = grad_hidden[:, part * piece : (part + 1) * piece]
            begin = 2 * part * piece
            value, slope = gelu_and_slope(both_ref[:, begin : begin + piece])
            upward = both_ref[:, begin + piece : begin + 2 * piece]
            start = pl.multiple_of((step * many + part) * 2 * piece, piece)
            grad_both_ref[:, pl.ds(start, piece)] = (grad * upward * slope).astype(LOW)
            start = pl.multiple_of((step * many + part) * 2 * piece + piece, piece)
            grad_both_ref[:, pl.ds(start, piece)] = (grad * value).astype(LOW)

    @pl.when(step >= count)
    def _():
        out_ref[...] = jnp.dot(
            grad_both_ref[...], pair_ref[...], preferred_element_type=WIDE
        ).astype(LOW)


def ff_backward(grad, pair, down, both, piece):
    rows, width = grad.shape
    hidden = down.shape[0]
    many = math.gcd(hidden // piece, 2)
    count = hidden // piece // many
    cut = math.gcd(width, 512)

    def now(i):
        return jnp.minimum(i, count - 1)

    def then(i):
        return jnp.maximum(i - count, 0)

    return pl.pallas_call(
        functools.partial(ff_backward_kernel, piece, many, count),
        grid=(count + width // cut,),
        in_specs=[
            pl.BlockSpec((rows, width), lambda i: (0, 0)),
            pl.BlockSpec((many * piece, width), lambda i: (now(i), 0)),
            pl.BlockSpec((rows, 2 * many * piece), lambda i: (0, now(i))),
            pl.BlockSpec((2 * hidden, cut), lambda i: (0, then(i))),
        ],
        out_specs=[
            pl.BlockSpec((rows, 2 * hidden), lambda i: (0, 0)),
            pl.BlockSpec((rows, cut), lambda i: (0, then(i))),
        ],
        out_shape=[
            jax.ShapeDtypeStruct((rows, 2 * hidden), LOW),
            jax.ShapeDtypeStruct((rows, width), LOW),
        ],
        cost_estimate=pl.CostEstimate(
            flops=6 * rows * width * hidden,
            bytes_accessed=6 * width * hidden + 12 * rows * hidden,
            transcendentals=rows * hidden,
        ),
    )(grad, down, both, pair)


def attention_kernel(
    raw_ref, gain_ref, cos_ref, sin_ref, places_ref, limit_ref, kv_ref,
    q_ref, probs_ref, wide_ref, low_ref,
):
    raw = raw_ref[...]
    scale = lax.rsqrt(jnp.mean(raw * raw, axis=-1, keepdims=True) + EPSILON)
    raw = raw * scale * gain_ref[...]
    half = raw.shape[1] // 2
    front, behind = raw[:, :half], raw[:, half:]
    cosine, sine = cos_ref[...], sin_ref[...]
    q_ref[:, :half] = (front * cosine - behind * sine).astype(LOW)
    q_ref[:, half:] = (behind * cosine + front * sine).astype(LOW)
    scores = contract_last(q_ref[...], kv_ref[:, :HEAD_DIM])
    scores = jnp.where(limit_ref[...] <= places_ref[...], scores, NEGATIVE)
    raised = jnp.exp(scores - jnp.max(scores, axis=-1, keepdims=True))
    probs = raised * (1.0 / jnp.sum(raised, axis=-1, keepdims=True))
    probs_ref[0] = probs
    attended = jnp.dot(probs.astype(LOW), kv_ref[:, HEAD_DIM:], preferred_element_type=WIDE)
    wide_ref[...] = attended
    low_ref[...] = attended.astype(LOW)


def attention_forward(projected, gain, cosine, sine, query_places, key_limit, keys_values, heads):
    rows = projected.shape[0]
    keys = keys_values.shape[0]
    block = min(rows, 256, (1 << 19) // keys)
    return pl.pallas_call(
        attention_kernel,
        grid=(heads, rows // block),
        in_specs=[
            pl.BlockSpec((block, HEAD_DIM), lambda h, i: (i, h)),
            pl.BlockSpec((1, HEAD_DIM), lambda h, i: (0, 0)),
            pl.BlockSpec((block, HEAD_DIM // 2), lambda h, i: (i, 0)),
            pl.BlockSpec((block, HEAD_DIM // 2), lambda h, i: (i, 0)),
            pl.BlockSpec((block, 1), lambda h, i: (i, 0)),
            pl.BlockSpec((1, keys), lambda h, i: (0, 0)),
            pl.BlockSpec((keys, 2 * HEAD_DIM), lambda h, i: (0, 0)),
        ],
        out_specs=[
            pl.BlockSpec((block, HEAD_DIM), lambda h, i: (i, h)),
            pl.BlockSpec((1, block, keys), lambda h, i: (h, i, 0)),
            pl.BlockSpec((block, HEAD_DIM), lambda h, i: (i, h)),
            pl.BlockSpec((block, HEAD_DIM), lambda h, i: (i, h)),
        ],
        out_shape=[
            jax.ShapeDtypeStruct((rows, heads * HEAD_DIM), LOW),
            jax.ShapeDtypeStruct((heads, rows, keys), WIDE),
            jax.ShapeDtypeStruct((rows, heads * HEAD_DIM), WIDE),
            jax.ShapeDtypeStruct((rows, heads * HEAD_DIM), LOW),
        ],
        cost_estimate=pl.CostEstimate(
            flops=4 * heads * rows * keys * HEAD_DIM,
            bytes_accessed=4 * heads * rows * keys + 4 * keys * HEAD_DIM + 14 * rows * heads * HEAD_DIM,
            transcendentals=heads * rows * keys,
        ),
    )(projected, gain, cosine, sine, query_places, key_limit, keys_values)


def attention_back_kernel(
    grad_ref, wide_ref, probs_ref, q_ref, raw_ref, gain_ref, cos_ref, sin_ref, kv_ref,
    grad_raw_ref, grad_gain_ref, grad_kv_ref, total,
):
    head, step = pl.program_id(0), pl.program_id(1)
    first = jnp.logical_and(head == 0, step == 0)
    last = jnp.logical_and(head == pl.num_programs(0) - 1, step == pl.num_programs(1) - 1)
    grad = grad_ref[...]
    delta = jnp.sum(grad.astype(WIDE) * wide_ref[...], axis=-1, keepdims=True)
    probs = probs_ref[0]
    grad_probs = contract_last(grad, kv_ref[:, HEAD_DIM:])
    grad_scores = (probs * (grad_probs - delta)).astype(LOW)
    rotated = jnp.dot(grad_scores, kv_ref[:, :HEAD_DIM], preferred_element_type=WIDE)
    key_part = over_rows(grad_scores, q_ref[...])
    value_part = over_rows(probs.astype(LOW), grad)

    @pl.when(first)
    def _():
        total[:, :HEAD_DIM] = key_part
        total[:, HEAD_DIM:] = value_part

    @pl.when(jnp.logical_not(first))
    def _():
        total[:, :HEAD_DIM] += key_part
        total[:, HEAD_DIM:] += value_part

    @pl.when(last)
    def _():
        grad_kv_ref[...] = total[...].astype(LOW)

    half = rotated.shape[1] // 2
    front, behind = rotated[:, :half], rotated[:, half:]
    cosine, sine = cos_ref[...], sin_ref[...]
    back = jnp.concatenate([front * cosine + behind * sine, behind * cosine - front * sine], axis=1)
    raw = raw_ref[...]
    scale = lax.rsqrt(jnp.mean(raw * raw, axis=-1, keepdims=True) + EPSILON)
    normed = raw * scale
    gain_part = jnp.sum(back * normed, axis=0, keepdims=True)

    @pl.when(first)
    def _():
        grad_gain_ref[...] = gain_part

    @pl.when(jnp.logical_not(first))
    def _():
        grad_gain_ref[...] += gain_part

    back = back * gain_ref[...]
    grad_raw_ref[...] = (
        scale * (back - normed * jnp.mean(back * normed, axis=-1, keepdims=True))
    ).astype(LOW)


def attention_backward(grad, wide, probs, q_low, projected, gain, cosine, sine, keys_values):
    heads, rows, keys = probs.shape
    block = min(rows, 256, (1 << 19) // keys)

    def tile(h, i):
        return (i, h)

    def whole(h, i):
        return (0, 0)

    return pl.pallas_call(
        attention_back_kernel,
        grid=(heads, rows // block),
        in_specs=[
            pl.BlockSpec((block, HEAD_DIM), tile),
            pl.BlockSpec((block, HEAD_DIM), tile),
            pl.BlockSpec((1, block, keys), lambda h, i: (h, i, 0)),
            pl.BlockSpec((block, HEAD_DIM), tile),
            pl.BlockSpec((block, HEAD_DIM), tile),
            pl.BlockSpec((1, HEAD_DIM), whole),
            pl.BlockSpec((block, HEAD_DIM // 2), lambda h, i: (i, 0)),
            pl.BlockSpec((block, HEAD_DIM // 2), lambda h, i: (i, 0)),
            pl.BlockSpec((keys, 2 * HEAD_DIM), whole),
        ],
        out_specs=[
            pl.BlockSpec((block, HEAD_DIM), tile),
            pl.BlockSpec((1, HEAD_DIM), whole),
            pl.BlockSpec((keys, 2 * HEAD_DIM), whole),
        ],
        out_shape=[
            jax.ShapeDtypeStruct((rows, heads * HEAD_DIM), LOW),
            jax.ShapeDtypeStruct((1, HEAD_DIM), WIDE),
            jax.ShapeDtypeStruct((keys, 2 * HEAD_DIM), LOW),
        ],
        scratch_shapes=[pltpu.VMEM((keys, 2 * HEAD_DIM), WIDE)],
        cost_estimate=pl.CostEstimate(
            flops=8 * heads * rows * keys * HEAD_DIM,
            bytes_accessed=4 * heads * rows * keys + 8 * keys * HEAD_DIM + 14 * rows * heads * HEAD_DIM,
            transcendentals=0,
        ),
    )(grad, wide, probs, q_low, projected, gain, cosine, sine, keys_values)


def widen_kernel(places, source, gate, up):
    gate[...] = source[0, 0, 0].astype(WIDE)
    up[...] = source[0, 0, 1].astype(WIDE)


def widen_pair(pieces, places):
    parts, run, _, rows, width = pieces.shape
    return pl.pallas_call(
        widen_kernel,
        grid_spec=pltpu.PrefetchScalarGridSpec(
            num_scalar_prefetch=1,
            grid=(run, parts),
            in_specs=[pl.BlockSpec((1, 1, 2, rows, width), lambda k, r, p: (r, k, 0, 0, 0))],
            out_specs=[pl.BlockSpec((rows, width), lambda k, r, p: (0, p[k] * parts + r))] * 2,
        ),
        out_shape=[jax.ShapeDtypeStruct((rows, width * parts * run), WIDE)] * 2,
        cost_estimate=pl.CostEstimate(flops=0, bytes_accessed=6 * pieces.size, transcendentals=0),
    )(places, pieces)


def shift_blocks(make):
    run = lax.axis_size("wsh")
    here = lax.axis_index("wsh")
    received = []
    for k in range(run):
        block = make((here + k) % run)
        if k:
            block = lax.ppermute(block, "wsh", [(i, (i + k) % run) for i in range(run)])
        received.append(block)
    return received


def head_piece_kernel(run, query_width, places, *refs):
    sources, (own_ref, out_ref, total) = refs[:run], refs[run:]
    kv_width = KV_HEADS * HEAD_DIM
    query_all = run * query_width
    head_width = query_width + 2 * HEAD_DIM
    total[...] = jnp.zeros_like(total)
    rest = jnp.zeros((out_ref.shape[0], sources[0].shape[1] - head_width), WIDE)
    for k, source in enumerate(sources):
        place = places[k]
        out_ref[:, pl.ds(pl.multiple_of(place * query_width, query_width), query_width)] = source[
            :, :query_width
        ]
        head = place * KV_HEADS // run
        for number in range(2):
            begin = query_width + number * HEAD_DIM
            at = pl.multiple_of(head * HEAD_DIM + number * kv_width, HEAD_DIM)
            total[:, pl.ds(at, HEAD_DIM)] += source[:, begin : begin + HEAD_DIM].astype(WIDE)
        rest += source[:, head_width:].astype(WIDE)
    begin = query_all + 2 * kv_width
    out_ref[:, query_all:begin] = total[...].astype(LOW)
    out_ref[:, begin : begin + rest.shape[1]] = rest.astype(LOW)
    out_ref[:, begin + rest.shape[1] :] = own_ref[:, run * sources[0].shape[1] :]


def head_piece_sum(sources, own, places, query_width):
    run = len(sources)
    rows, columns = sources[0].shape
    kv_width = KV_HEADS * HEAD_DIM
    rest = columns - query_width - 2 * HEAD_DIM
    width = run * query_width + 2 * kv_width + rest + own.shape[1] - run * columns

    def whole(i, p):
        return (0, 0)

    return pl.pallas_call(
        functools.partial(head_piece_kernel, run, query_width),
        grid_spec=pltpu.PrefetchScalarGridSpec(
            num_scalar_prefetch=1,
            grid=(1,),
            in_specs=[pl.BlockSpec((rows, columns), whole)] * run
            + [pl.BlockSpec(own.shape, whole)],
            out_specs=pl.BlockSpec((rows, width), whole),
            scratch_shapes=[pltpu.VMEM((rows, 2 * kv_width), WIDE)],
        ),
        out_shape=jax.ShapeDtypeStruct((rows, width), LOW),
        cost_estimate=pl.CostEstimate(
            flops=0, bytes_accessed=2 * (own.size + 2 * rows * width), transcendentals=0
        ),
    )(places, *sources, own)


def shift_exchange(make):
    run = lax.axis_size("wsh")
    order = (lax.axis_index("wsh") - jnp.arange(run, dtype=jnp.int32)) % run
    return jnp.take(jnp.stack(shift_blocks(make)), order, axis=0)


def place_kernel(places, *refs):
    step = pl.program_id(0)
    sources, out = refs[:-1], refs[-1]
    for number, source in enumerate(sources):

        @pl.when(step == number)
        def _(source=source):
            out[...] = source[...]


def place_columns(blocks, places):
    rows, width = blocks[0].shape
    count = len(blocks)
    return pl.pallas_call(
        place_kernel,
        grid_spec=pltpu.PrefetchScalarGridSpec(
            num_scalar_prefetch=1,
            grid=(count,),
            in_specs=[pl.BlockSpec((rows, width), lambda k, p: (0, 0))] * count,
            out_specs=pl.BlockSpec((rows, width), lambda k, p: (0, p[k])),
        ),
        out_shape=jax.ShapeDtypeStruct((rows, width * count), blocks[0].dtype),
        cost_estimate=pl.CostEstimate(
            flops=0, bytes_accessed=4 * count * blocks[0].size, transcendentals=0
        ),
    )(places, *blocks)


def entry(stacked):
    return lambda index: lax.dynamic_index_in_dim(stacked, index, 0, False)


def shards(
    tokens,
    cotangent,
    lengths,
    positions,
    token_ids,
    per_layer_table,
    w_query,
    w_key,
    w_value,
    w_output,
    laurel_left,
    laurel_right,
    w_gate,
    w_up,
    w_down,
    w_layer_gate,
    w_layer_proj,
    norm_gains,
    query_gain,
    key_gain,
):
    rows_dev, width = tokens.shape[1:]
    run = lax.axis_size("wsh")
    contexts = lax.axis_size("ctx")
    parts = 2 * contexts
    chip = lax.axis_index(COPIES)
    shard_rows = width // run
    heads_here = HEADS // run
    groups = HEADS // KV_HEADS
    query_width = heads_here * HEAD_DIM
    head_width = query_width + 2 * HEAD_DIM
    hidden_width = w_gate.shape[1] // run
    head_piece = shard_rows // parts
    piece = hidden_width // parts
    rank = laurel_left.shape[1]
    places = ((lax.axis_index("wsh") - jnp.arange(run)) % run).astype(jnp.int32)
    gain_cut = query_gain.shape[0]

    def share(weight):
        return lax.dynamic_slice_in_dim(weight, chip * head_piece, head_piece, 0)

    query_rows, key_rows, value_rows = share(w_query), share(w_key), share(w_value)

    indices = shift_exchange(lambda k: jnp.concatenate([token_ids, positions], axis=0))
    small = jnp.concatenate(
        [
            norm_gains.T,
            jnp.pad(
                jnp.concatenate([query_gain, key_gain])[None],
                ((0, 1), (0, shard_rows - 2 * gain_cut)),
            ),
        ],
        axis=0,
    )
    proj_rows = w_layer_proj.shape[0]
    proj_share = lax.dynamic_slice_in_dim(w_layer_proj, chip * (width // parts), width // parts, 1)
    common = jnp.concatenate(
        [
            share(laurel_left),
            share(laurel_right),
            share(w_layer_gate),
            proj_share.reshape(head_piece, -1),
        ],
        axis=1,
    )
    fetch_width = head_width + common.shape[1]
    small_flat = jnp.pad(small.reshape(-1), (0, -small.size % fetch_width)).reshape(-1, fetch_width)
    small_flat = jnp.pad(small_flat, ((0, 16 - small_flat.shape[0]), (0, 0)))
    common, query_rows, key_rows, value_rows, small_flat, indices = lax.optimization_barrier(
        (common, query_rows, key_rows, value_rows, small_flat, indices)
    )

    def head_block(index):
        kv = index * heads_here // groups * HEAD_DIM
        block = jnp.concatenate(
            [
                lax.dynamic_slice_in_dim(query_rows, index * query_width, query_width, 1),
                lax.dynamic_slice_in_dim(key_rows, kv, HEAD_DIM, 1),
                lax.dynamic_slice_in_dim(value_rows, kv, HEAD_DIM, 1),
                common,
            ],
            axis=1,
        )
        return jnp.concatenate([small_flat, block], axis=0)

    head_share = shift_exchange(head_block)
    small_all = head_share[:, :16].reshape(run, -1)[:, : small.size].reshape(run, 8, shard_rows)
    fetched = lax.all_gather(head_share[:, 16:], COPIES, axis=0)
    w_heads = fetched[:, :, :, :head_width]
    proj_at = head_width + 2 * rank + w_layer_gate.shape[1]
    layer_proj_full = fetched[:, :, :, proj_at:].reshape(parts, run, proj_rows, width // parts)
    layer_proj_full = layer_proj_full.transpose(1, 2, 0, 3).reshape(run * proj_rows, width)
    laurel_weights = fetched[:, :, :, head_width:proj_at].transpose(1, 0, 2, 3).reshape(width, -1)
    left_full = laurel_weights[:, :rank]
    right_full = laurel_weights[:, rank : 2 * rank]
    layer_gate_full = laurel_weights[:, 2 * rank :]
    w_heads = w_heads.transpose(1, 0, 2, 3).reshape(width, head_width)

    gains_full = small_all.transpose(1, 0, 2).reshape(8, width).astype(WIDE)
    query_gain_full = small_all[:, 6, :gain_cut].reshape(HEAD_DIM).astype(WIDE)
    key_gain_full = small_all[:, 6, gain_cut : 2 * gain_cut].reshape(HEAD_DIM).astype(WIDE)
    tokens_run = spread(tokens[0], "wsh")

    indices = indices[None]
    bit = 1
    while bit < contexts:
        indices = jnp.concatenate([indices, swap(indices, "ctx", bit)], axis=0)
        bit *= 2
    run_places = indices[0, :, 1].reshape(-1)
    here_ctx = lax.axis_index("ctx")
    context_order = jnp.bitwise_xor(jnp.arange(contexts, dtype=jnp.int32), here_ctx)
    key_places = jnp.take(indices[:, :, 1], context_order, axis=0).reshape(-1)
    own_ids = indices[:, :, 0].reshape(-1)
    all_ids = jnp.concatenate([own_ids, swap(own_ids, "slot", 1)])
    length = lengths[0]

    vocab_rows = per_layer_table.shape[0]
    vocab_first = lax.axis_index(EVERY) * vocab_rows
    vocab_range = jnp.arange(vocab_rows, dtype=jnp.int32)

    def one_hot():
        return ((all_ids - vocab_first)[:, None] == vocab_range[None, :]).astype(LOW)

    table_rows = matmul(one_hot(), per_layer_table).astype(LOW)
    tokens_run, table_rows = lax.optimization_barrier((tokens_run, table_rows))
    def pair_block(index):
        first = index * hidden_width + chip * piece
        gate_cut = lax.dynamic_slice_in_dim(w_gate, first, piece, 1)
        up_cut = lax.dynamic_slice_in_dim(w_up, first, piece, 1)
        gate_cut, up_cut = after((gate_cut, up_cut), head_share)
        return jnp.concatenate([gate_cut.T, up_cut.T], axis=0)

    pair_received = shift_blocks(pair_block)
    normed_run = rms_norm(tokens_run.astype(WIDE), gains_full[0]).astype(LOW)
    tokens_f = tokens[0].astype(WIDE)
    normed = rms_norm(tokens_f, gains_full[0])
    normed_low = normed.astype(LOW)
    total_rows = run * rows_dev
    projected = matmul(normed_run, w_heads)
    key = projected[:, query_width : query_width + HEAD_DIM]
    value = projected[:, query_width + HEAD_DIM :]

    def key_path(raw, gain):
        return rotate(rms_norm(raw.reshape(total_rows, 1, HEAD_DIM), gain), run_places)[:, 0]

    def value_path(raw):
        return rms_norm(raw, 1.0)

    k_low = key_path(key, key_gain_full).astype(LOW)
    v_low = value_path(value).astype(LOW)
    keys_values = spread(jnp.concatenate([k_low, v_low], axis=1), "ctx")
    half = table_rows.shape[0] // 2
    looked_up = add_low(table_rows[:half], swap(table_rows[half:], "slot", 1))
    bit = contexts // 2
    while bit:
        half = looked_up.shape[0] // 2
        looked_up = add_low(looked_up[:half], swap(looked_up[half:], "ctx", bit))
        bit //= 2
    looked_up = looked_up.reshape(run, rows_dev, -1)
    inverse = jnp.exp(
        -math.log(ROPE_BASE)
        * (2.0 * jnp.arange(HEAD_DIM // 2, dtype=jnp.float32) / HEAD_DIM)
    )
    angles = run_places.astype(WIDE)[:, None] * inverse[None, :]
    cosine, sine = jnp.cos(angles), jnp.sin(angles)
    key_limit = jnp.where(key_places < length, key_places, jnp.int32(1 << 30))
    q_low, probs, attended, attended_low = attention_forward(
        projected,
        query_gain_full[None],
        cosine,
        sine,
        run_places[:, None],
        key_limit[None],
        keys_values,
        heads_here,
    )
    attended_low, pair_received = lax.optimization_barrier((attended_low, pair_received))
    pair_share = place_columns(pair_received, places)
    pair_weight = lax.all_gather(pair_share, COPIES, axis=0, tiled=True)
    attn_proj = collect(matmul(attended_low, w_output).astype(LOW), "wsh")
    attn_proj, looked_up = lax.optimization_barrier((attn_proj, looked_up))

    first_sum = tokens_f + rms_norm(attn_proj, gains_full[1])
    low_rank_low = matmul(normed_low, left_full).astype(LOW)
    laurel_out = times_transposed(low_rank_low, right_full)
    laurel = normed + rms_norm(laurel_out, gains_full[2])
    mixed = (first_sum + laurel) * HALF_ROOT
    ff_in_low = rms_norm(mixed, gains_full[3]).astype(LOW)

    ff_run = spread(ff_in_low, "wsh")
    looked_up = after(looked_up, ff_run)
    layer_input = EMBED_SCALE * jnp.sum(shift_exchange(entry(looked_up)).astype(WIDE), axis=0)
    aligned = piece % 128 == 0
    if aligned:
        both, hidden_low, ff_part = ff_forward(ff_run, pair_weight, w_down, piece)
    else:
        both = times_transposed(ff_run, pair_weight)
        both_parts = both.reshape(total_rows, parts, 2, piece)
        gate = both_parts[:, :, 0].reshape(total_rows, hidden_width)
        upward = both_parts[:, :, 1].reshape(total_rows, hidden_width)
        hidden_low = gated_product(gate, upward).astype(LOW)
        ff_part = matmul(hidden_low, w_down).astype(LOW)
    ff_part, layer_input = lax.optimization_barrier((ff_part, layer_input))
    ff_out = collect(ff_part, "wsh")
    third_sum = mixed + rms_norm(ff_out, gains_full[4])
    third_low = third_sum.astype(LOW)

    layer_gate = matmul(third_low, layer_gate_full)
    gated_low = gated_product(layer_gate, layer_input).astype(LOW)
    layer_proj = matmul(gated_low, layer_proj_full)
    result = third_sum + rms_norm(layer_proj, gains_full[5])
    layer_out = result.astype(LOW)[None]

    valid = (positions[0] < length).astype(WIDE)
    grad_out = cotangent[0].astype(WIDE) * valid[:, None]
    _, pullback = jax.vjp(rms_norm, layer_proj, gains_full[5])
    grad_proj, grad_gain_five = pullback(grad_out)
    grad_proj_low = grad_proj.astype(LOW)
    grad_gated = times_transposed(grad_proj_low, layer_proj_full)
    _, pullback = jax.vjp(gated_product, layer_gate, layer_input)
    grad_lgate, grad_input = pullback(grad_gated)
    grad_lgate_low = grad_lgate.astype(LOW)
    grad_input_low = grad_input.astype(LOW)
    grad_third = grad_out + times_transposed(grad_lgate_low, layer_gate_full)
    _, pullback = jax.vjp(rms_norm, ff_out, gains_full[4])
    grad_ff, grad_gain_four = pullback(grad_third)
    grad_ff_low = grad_ff.astype(LOW)

    grad_ff_run = spread(grad_ff_low, "wsh")
    down_part = over_rows(hidden_low, grad_ff_run).astype(LOW)
    grad_ff_run, down_part = lax.optimization_barrier((grad_ff_run, down_part))
    down_own = lax.psum_scatter(down_part, COPIES, scatter_dimension=0, tiled=True)
    grad_input_low = after(grad_input_low, grad_ff_run)
    every_grad = shift_exchange(lambda k: grad_input_low).reshape(total_rows, -1)

    def wider(rows, axis, bit):
        return jnp.concatenate([rows, swap(rows, axis, bit)], axis=0)

    hops = [1 << power for power in range(contexts.bit_length() - 1)]
    if aligned:
        grad_both, ff_part = ff_backward(grad_ff_run, pair_weight, w_down, both, piece)
    else:
        grad_hidden = times_transposed(grad_ff_run, w_down)
        _, pullback = jax.vjp(gated_product, gate, upward)
        grad_gate, grad_upward = pullback(grad_hidden)
        grad_both = jnp.stack(
            [
                grad_gate.reshape(total_rows, parts, piece),
                grad_upward.reshape(total_rows, parts, piece),
            ],
            axis=2,
        )
        grad_both = grad_both.reshape(total_rows, 2 * hidden_width).astype(LOW)
        ff_part = matmul(grad_both, pair_weight).astype(LOW)
    ff_part, every_grad = lax.optimization_barrier((ff_part, every_grad))
    every_grad = wider(every_grad, "ctx", hops[0])
    grad_ff_in = collect(ff_part, "wsh")
    pair_part = over_rows(after(grad_both, ff_part), ff_run).astype(LOW)
    grad_ff_in, pair_part, every_grad = lax.optimization_barrier((grad_ff_in, pair_part, every_grad))
    for bit in hops[1:]:
        every_grad = wider(every_grad, "ctx", bit)
    pair_own = lax.psum_scatter(pair_part, COPIES, scatter_dimension=0, tiled=True)
    _, pullback = jax.vjp(rms_norm, mixed, gains_full[3])
    grad_mixed_norm, grad_gain_three = pullback(grad_ff_in)
    grad_branch = (grad_third + grad_mixed_norm) * HALF_ROOT
    _, pullback = jax.vjp(rms_norm, attn_proj, gains_full[1])
    grad_attn, grad_gain_one = pullback(grad_branch)
    grad_attn_low = grad_attn.astype(LOW)
    grad_attn_run = spread(grad_attn_low, "wsh")
    grad_attn_run, down_own, every_grad = lax.optimization_barrier(
        (grad_attn_run, down_own, every_grad)
    )
    every_grad = wider(every_grad, "slot", 1)
    down_grad = lax.all_gather(down_own, COPIES, axis=0, tiled=True)

    def pair_back(index):
        block = lax.dynamic_slice_in_dim(pair_own, index * shard_rows, shard_rows, 1)
        return block.reshape(2, piece, shard_rows).transpose(0, 2, 1)

    _, pullback = jax.vjp(rms_norm, laurel_out, gains_full[2])
    grad_laurel, grad_gain_two = pullback(grad_branch)
    grad_laurel_low = grad_laurel.astype(LOW)
    grad_rank_low = matmul(grad_laurel_low, right_full).astype(LOW)

    left_grad = over_rows(normed_low, grad_rank_low)
    right_grad = over_rows(grad_laurel_low, low_rank_low)
    layer_gate_grad = over_rows(third_low, grad_lgate_low)
    layer_proj_grad = over_rows(gated_low, grad_proj_low)

    narrow = jnp.concatenate([left_grad, right_grad, layer_gate_grad], axis=1).astype(LOW)
    narrow_columns = narrow.shape[1]
    proj_back = layer_proj_grad.astype(LOW).reshape(run, proj_rows, parts, width // parts)
    proj_back = proj_back.transpose(0, 2, 1, 3).reshape(run, parts, head_piece, -1)
    narrow = jnp.concatenate(
        [narrow.reshape(run, parts, head_piece, narrow_columns), proj_back], axis=3
    )

    grad_att_low = times_transposed(grad_attn_run, w_output).astype(LOW)
    grad_query, grad_query_gain, kv_part = attention_backward(
        grad_att_low,
        attended,
        probs,
        q_low,
        projected,
        query_gain_full[None],
        cosine,
        sine,
        keys_values,
    )
    grad_query_gain = grad_query_gain[0]
    kv_sum = collect(kv_part, "ctx")
    output_part = over_rows(attended_low, grad_attn_run).astype(LOW)
    kv_sum, pair_own, output_part, narrow, every_grad = lax.optimization_barrier(
        (kv_sum, pair_own, output_part, narrow, every_grad)
    )
    pair_blocks = jnp.stack(shift_blocks(pair_back))
    _, pullback = jax.vjp(key_path, key, key_gain_full)
    grad_key, grad_key_gain = pullback(kv_sum[:, :HEAD_DIM])
    _, pullback = jax.vjp(value_path, value)
    (grad_value,) = pullback(kv_sum[:, HEAD_DIM:])
    grad_heads = jnp.concatenate(
        [grad_query, grad_key.astype(LOW), grad_value.astype(LOW)], axis=1
    )
    heads_part = over_rows(normed_run, grad_heads).astype(LOW)
    heads_part = heads_part.reshape(run, parts, head_piece, head_width)
    heads_part = jnp.concatenate(
        [one[index] for index in range(run) for one in (heads_part, narrow)]
        + [output_part.reshape(parts, head_piece, width)],
        axis=2,
    )
    fetch_back = head_width + narrow.shape[3]
    heads_kept, heads_given = halves(heads_part)
    normed_part = times_transposed(grad_heads, w_heads).astype(LOW)
    heads_pieces = [add_low(a, b) for a, b in zip(nearest(heads_kept), nearest(heads_given))]
    heads_first = reduce_first(heads_pieces)
    normed_part, heads_first, pair_blocks, down_grad = lax.optimization_barrier(
        (normed_part, heads_first, pair_blocks, down_grad)
    )
    pair_all = lax.all_gather(pair_blocks, COPIES, axis=0)
    table_grad = EMBED_SCALE * over_rows(one_hot(), after(every_grad, normed_part))
    heads_second = reduce_second(heads_pieces, heads_first)
    grad_run = collect(normed_part, "wsh")
    down_grad = after(down_grad, table_grad).astype(WIDE)
    grad_run, heads_second, table_grad, down_grad = lax.optimization_barrier(
        (grad_run, heads_second, table_grad, down_grad)
    )
    heads_own = reduce_last(heads_pieces, heads_second)

    def head_back(index):
        return lax.dynamic_slice_in_dim(heads_own, index * fetch_back, fetch_back, 1)

    heads_sent = shift_blocks(head_back)
    grad_normed = (
        grad_run
        + times_transposed(grad_rank_low, left_full)
        + grad_branch
    )
    _, pullback = jax.vjp(rms_norm, tokens_f, gains_full[0])
    grad_tokens, grad_gain_zero = pullback(grad_normed)
    tokens_grad = (grad_tokens + grad_branch).astype(LOW)[None]

    vector = jnp.concatenate(
        [grad_query_gain.reshape(run, gain_cut), grad_key_gain.reshape(run, gain_cut)], axis=1
    )
    vector = jnp.pad(vector, ((0, 0), (0, shard_rows - 2 * gain_cut))).reshape(width)
    gain_sums = jnp.stack(
        [
            grad_gain_zero,
            grad_gain_one,
            grad_gain_two,
            grad_gain_three,
            grad_gain_four,
            grad_gain_five,
            vector,
            jnp.zeros_like(vector),
        ]
    )
    gain_sums = gain_sums.reshape(8, run, shard_rows).transpose(1, 0, 2).reshape(8 * run, shard_rows)
    gain_sums = collect(gain_sums, "wsh")
    heads_piece = head_piece_sum(heads_sent, heads_own, places, query_width)
    kv_width = KV_HEADS * HEAD_DIM
    cuts = []
    for size in (
        HEADS * HEAD_DIM,
        kv_width,
        kv_width,
        rank,
        rank,
        w_layer_gate.shape[1],
        narrow.shape[3] - narrow_columns,
        width,
    ):
        cuts.append((sum(w for _, w in cuts), size))
    heads_piece, gain_sums = after((heads_piece, gain_sums), pair_all)
    heads_near = gather_first(heads_piece)
    gain_sums = jnp.sum(spread(gain_sums[None], COPIES), axis=0)
    own = jnp.full((1,), chip, jnp.int32)
    if aligned:
        gate_grad, up_grad = widen_pair(pair_all, places)
    else:
        pair_all = jnp.take(pair_all, places, axis=1)
        pair_all = pair_all.transpose(2, 3, 1, 0, 4).reshape(2, shard_rows, -1).astype(WIDE)
        gate_grad, up_grad = pair_all[0], pair_all[1]

    heads_near, gain_sums, gate_grad, up_grad = lax.optimization_barrier(
        (heads_near, gain_sums, gate_grad, up_grad)
    )
    heads_near = gather_second(heads_piece, heads_near)
    heads_all = last_gather(heads_near)
    (
        query_grad,
        key_grad,
        value_grad,
        left_grad,
        right_grad,
        layer_gate_grad,
        layer_proj_grad,
        output_grad,
    ) = assemble(
        [p[None] for p in heads_all], own, WIDE, cuts
    )
    layer_proj_grad = layer_proj_grad.reshape(parts, proj_rows, width // parts)
    layer_proj_grad = layer_proj_grad.transpose(1, 0, 2).reshape(proj_rows, width)

    return (
        layer_out,
        tokens_grad,
        table_grad,
        query_grad.reshape(shard_rows, -1),
        key_grad.reshape(shard_rows, -1),
        value_grad.reshape(shard_rows, -1),
        output_grad.reshape(query_width, width),
        left_grad.reshape(shard_rows, -1),
        right_grad.reshape(shard_rows, -1),
        gate_grad,
        up_grad,
        down_grad,
        layer_gate_grad.reshape(shard_rows, -1),
        layer_proj_grad,
        gain_sums[:6].T,
        gain_sums[6, :gain_cut],
        gain_sums[6, gain_cut : 2 * gain_cut],
    )


def solution(mesh):
    placed = (
        P("slot", ("ctx", "wsh"), None),
        P("slot", ("ctx", "wsh"), None),
        P("slot"),
        P("slot", ("ctx", "wsh")),
        P("slot", ("ctx", "wsh")),
        P(("slot", "ctx", "wsh"), None),
        P("wsh", None),
        P("wsh", None),
        P("wsh", None),
        P("wsh", None),
        P("wsh", None),
        P("wsh", None),
        P("wsh", None),
        P("wsh", None),
        P("wsh", None),
        P("wsh", None),
        P("wsh", None),
        P("wsh", None),
        P("wsh"),
        P("wsh"),
    )
    return jax.shard_map(
        shards,
        mesh=mesh,
        in_specs=placed,
        out_specs=(
            P("slot", ("ctx", "wsh"), None),
            P("slot", ("ctx", "wsh"), None),
            P(("slot", "ctx", "wsh"), None),
            P("wsh", None),
            P("wsh", None),
            P("wsh", None),
            P("wsh", None),
            P("wsh", None),
            P("wsh", None),
            P("wsh", None),
            P("wsh", None),
            P("wsh", None),
            P("wsh", None),
            P("wsh", None),
            P("wsh", None),
            P("wsh"),
            P("wsh"),
        ),
        check_vma=False,
    )
```

```python
import functools
import math

import jax
import jax.numpy as jnp
from jax import lax
from jax.experimental import pallas as pl
from jax.experimental.pallas import tpu as pltpu
from jax.sharding import PartitionSpec as P

HEADS = 8
KV_HEADS = 2
HEAD_DIM = 256


EPSILON = 1e-06
ROPE_BASE = 1000000.0
HALF_ROOT = 0.7071067811865476
TANH_SCALE = 0.7978845608028654
NEGATIVE = -1e30
EMBED_SCALE = 16.0


def rms_norm(value, gain):
    return value * lax.rsqrt(jnp.mean(value * value, axis=-1, keepdims=True) + EPSILON) * gain


def gelu_tanh(value):
    return 0.5 * value * (1.0 + jnp.tanh(TANH_SCALE * (value + 0.044715 * value * value * value)))


def gated_product(pre_gate, other_side):
    return gelu_tanh(pre_gate) * other_side


def rotate(value, places):
    width_all = value.shape[-1]
    half_width = width_all // 2
    inverse = jnp.exp(
        -math.log(ROPE_BASE) * (2.0 * jnp.arange(half_width, dtype=jnp.float32) / width_all)
    )
    angles = places.astype(jnp.float32)[:, None] * inverse[None, :]
    cosine = jnp.cos(angles)[:, None, :]
    sine = jnp.sin(angles)[:, None, :]
    front = value[..., :half_width]
    behind = value[..., half_width:]
    return jnp.concatenate(
        [front * cosine - behind * sine, behind * cosine + front * sine], axis=-1
    )


def matmul(left, right):
    return jnp.dot(left, right, preferred_element_type=jnp.float32)


def times_transposed(left, right):
    return lax.dot_general(
        left, right, (((1,), (1,)), ((), ())), preferred_element_type=jnp.float32
    )


def over_rows(left, right):
    return lax.dot_general(
        left, right, (((0,), (0,)), ((), ())), preferred_element_type=jnp.float32
    )


LOW = jnp.bfloat16
WIDE = jnp.float32
EVERY = ("slot", "ctx", "wsh")
COPIES = ("slot", "ctx")


def after(value, *others):
    return lax.optimization_barrier((value, others))[0]


def exchange(value, axis):
    return lax.all_to_all(value, axis, 0, 0, tiled=True)


def spread(value, axis):
    size = lax.axis_size(axis)
    copies = jnp.broadcast_to(value[None], (size,) + value.shape)
    return exchange(copies.reshape((size * value.shape[0],) + value.shape[1:]), axis)


def collect(parts, axis):
    size = lax.axis_size(axis)
    received = exchange(parts, axis)
    received = received.reshape((size, parts.shape[0] // size) + parts.shape[1:])
    return jnp.sum(received.astype(WIDE), axis=0)


def swap(value, axis, bit):
    size = lax.axis_size(axis)
    return lax.ppermute(value, axis, [(i, i ^ bit) for i in range(size)])


def add_low(left, right):
    return (left.astype(WIDE) + right.astype(WIDE)).astype(LOW)


def gather_first(piece):
    if lax.axis_size("ctx") == 4:
        return [swap(piece, "ctx", 1), swap(piece, "ctx", 2)]
    return []


def gather_second(piece, first):
    if first:
        one, two = first
        half = piece.shape[0] // 2
        front = swap(one[:half], "ctx", 2)
        behind = swap(two[half:], "ctx", 1)
        return [piece, one, two, jnp.concatenate([front, behind], axis=0)]
    pieces = [piece]
    bit = 1
    while bit < lax.axis_size("ctx"):
        pieces = pieces + [swap(p, "ctx", bit) for p in pieces]
        bit *= 2
    return pieces


def reduce_first(pieces):
    if len(pieces) == 4:
        half = pieces[0].shape[0] // 2
        return [swap(pieces[3][:half], "ctx", 1), swap(pieces[3][half:], "ctx", 2)]
    return []


def reduce_second(pieces, first):
    if first:
        front, behind = first
        half = pieces[0].shape[0] // 2
        two = jnp.concatenate([add_low(pieces[2][:half], front), pieces[2][half:]], axis=0)
        one = jnp.concatenate([pieces[1][:half], add_low(pieces[1][half:], behind)], axis=0)
        return [swap(one, "ctx", 1), swap(two, "ctx", 2)]
    return []


def reduce_last(pieces, second):
    if second:
        one, two = second
        return (pieces[0].astype(WIDE) + one.astype(WIDE) + two.astype(WIDE)).astype(LOW)
    size = len(pieces)
    while size > 1:
        size //= 2
        pieces = [add_low(pieces[i], swap(pieces[size + i], "ctx", size)) for i in range(size)]
    return pieces[0]


def assemble_kernel(extent, cuts, own, *refs):
    step = pl.program_id(0)
    ins, outs = refs[:extent], refs[extent:]
    for number in range(extent):

        @pl.when(step == number)
        def _(number=number):
            for (begin, width), out in zip(cuts, outs):
                out[:, 0] = ins[number][:, :, begin : begin + width].astype(out.dtype)


def assemble(pieces, own, kind, cuts=None):
    count = len(pieces)
    outer, inner, width = pieces[0].shape
    cuts = cuts or [(0, width)]
    results = pl.pallas_call(
        functools.partial(assemble_kernel, count, cuts),
        grid_spec=pltpu.PrefetchScalarGridSpec(
            num_scalar_prefetch=1,
            grid=(count,),
            in_specs=[pl.BlockSpec((outer, inner, width), lambda i, o: (0, 0, 0))] * count,
            out_specs=[
                pl.BlockSpec((outer, 1, inner, w), lambda i, o: (0, lax.bitwise_xor(i, o[0]), 0, 0))
                for _, w in cuts
            ],
        ),
        out_shape=[jax.ShapeDtypeStruct((outer, count, inner, w), kind) for _, w in cuts],
    )(own, *pieces)
    return results


def halves(blocks):
    count = blocks.shape[0] // 2
    slot = lax.axis_index("slot")
    kept = lax.dynamic_slice_in_dim(blocks, slot * count, count, 0)
    given = lax.dynamic_slice_in_dim(blocks, (1 - slot) * count, count, 0)
    return kept, swap(given, "slot", 1)


def nearest(blocks):
    here = lax.axis_index("ctx")
    count = blocks.shape[0]
    return [lax.dynamic_index_in_dim(blocks, here ^ r, 0, False) for r in range(count)]


def last_gather(pieces):
    return pieces + [swap(p, "slot", 1) for p in pieces]


def contract_last(left, right):
    return lax.dot_general(left, right, (((1,), (1,)), ((), ())), preferred_element_type=WIDE)


def gelu_and_slope(value):
    inner = jnp.tanh(TANH_SCALE * (value + 0.044715 * value * value * value))
    slope = 0.5 * (1.0 + inner) + 0.5 * value * (1.0 - inner * inner) * TANH_SCALE * (
        1.0 + 3.0 * 0.044715 * value * value
    )
    return 0.5 * value * (1.0 + inner), slope


def ff_forward_kernel(piece, many, count, x_ref, pair_ref, down_ref, both_ref, hidden_ref, out_ref):
    step = pl.program_id(0)

    @pl.when(step < count)
    def _():
        both = contract_last(x_ref[...], pair_ref[...])
        both_ref[...] = both
        for part in range(many):
            begin = 2 * part * piece
            gate = both[:, begin : begin + piece]
            upward = both[:, begin + piece : begin + 2 * piece]
            start = pl.multiple_of((step * many + part) * piece, piece)
            hidden_ref[:, pl.ds(start, piece)] = (gelu_tanh(gate) * upward).astype(LOW)

    @pl.when(step >= count)
    def _():
        out_ref[...] = jnp.dot(
            hidden_ref[...], down_ref[...], preferred_element_type=WIDE
        ).astype(LOW)


def ff_forward(x, pair, down, piece):
    rows, width = x.shape
    hidden = down.shape[0]
    many = math.gcd(hidden // piece, 2)
    count = hidden // piece // many
    cut = math.gcd(width, 1024)

    def now(i):
        return jnp.minimum(i, count - 1)

    def then(i):
        return jnp.maximum(i - count, 0)

    return pl.pallas_call(
        functools.partial(ff_forward_kernel, piece, many, count),
        grid=(count + width // cut,),
        in_specs=[
            pl.BlockSpec((rows, width), lambda i: (0, 0)),
            pl.BlockSpec((2 * many * piece, width), lambda i: (now(i), 0)),
            pl.BlockSpec((hidden, cut), lambda i: (0, then(i))),
        ],
        out_specs=[
            pl.BlockSpec((rows, 2 * many * piece), lambda i: (0, now(i))),
            pl.BlockSpec((rows, hidden), lambda i: (0, 0)),
            pl.BlockSpec((rows, cut), lambda i: (0, then(i))),
        ],
        out_shape=[
            jax.ShapeDtypeStruct((rows, 2 * hidden), WIDE),
            jax.ShapeDtypeStruct((rows, hidden), LOW),
            jax.ShapeDtypeStruct((rows, width), LOW),
        ],
        cost_estimate=pl.CostEstimate(
            flops=6 * rows * width * hidden,
            bytes_accessed=6 * width * hidden + 10 * rows * hidden,
            transcendentals=rows * hidden,
        ),
    )(x, pair, down)


def ff_backward_kernel(
    piece, many, count, grad_ref, down_ref, both_ref, pair_ref, grad_both_ref, out_ref
):
    step = pl.program_id(0)

    @pl.when(step < count)
    def _():
        grad_hidden = contract_last(grad_ref[...], down_ref[...])
        for part in range(many):
            grad = grad_hidden[:, part * piece : (part + 1) * piece]
            begin = 2 * part * piece
            value, slope = gelu_and_slope(both_ref[:, begin : begin + piece])
            upward = both_ref[:, begin + piece : begin + 2 * piece]
            start = pl.multiple_of((step * many + part) * 2 * piece, piece)
            grad_both_ref[:, pl.ds(start, piece)] = (grad * upward * slope).astype(LOW)
            start = pl.multiple_of((step * many + part) * 2 * piece + piece, piece)
            grad_both_ref[:, pl.ds(start, piece)] = (grad * value).astype(LOW)

    @pl.when(step >= count)
    def _():
        out_ref[...] = jnp.dot(
            grad_both_ref[...], pair_ref[...], preferred_element_type=WIDE
        ).astype(LOW)


def ff_backward(grad, pair, down, both, piece):
    rows, width = grad.shape
    hidden = down.shape[0]
    many = math.gcd(hidden // piece, 2)
    count = hidden // piece // many
    cut = math.gcd(width, 512)

    def now(i):
        return jnp.minimum(i, count - 1)

    def then(i):
        return jnp.maximum(i - count, 0)

    return pl.pallas_call(
        functools.partial(ff_backward_kernel, piece, many, count),
        grid=(count + width // cut,),
        in_specs=[
            pl.BlockSpec((rows, width), lambda i: (0, 0)),
            pl.BlockSpec((many * piece, width), lambda i: (now(i), 0)),
            pl.BlockSpec((rows, 2 * many * piece), lambda i: (0, now(i))),
            pl.BlockSpec((2 * hidden, cut), lambda i: (0, then(i))),
        ],
        out_specs=[
            pl.BlockSpec((rows, 2 * hidden), lambda i: (0, 0)),
            pl.BlockSpec((rows, cut), lambda i: (0, then(i))),
        ],
        out_shape=[
            jax.ShapeDtypeStruct((rows, 2 * hidden), LOW),
            jax.ShapeDtypeStruct((rows, width), LOW),
        ],
        cost_estimate=pl.CostEstimate(
            flops=6 * rows * width * hidden,
            bytes_accessed=6 * width * hidden + 12 * rows * hidden,
            transcendentals=rows * hidden,
        ),
    )(grad, down, both, pair)


def attention_kernel(
    raw_ref, gain_ref, cos_ref, sin_ref, places_ref, limit_ref, kv_ref,
    q_ref, probs_ref, wide_ref, low_ref,
):
    raw = raw_ref[...]
    scale = lax.rsqrt(jnp.mean(raw * raw, axis=-1, keepdims=True) + EPSILON)
    raw = raw * scale * gain_ref[...]
    half = raw.shape[1] // 2
    front, behind = raw[:, :half], raw[:, half:]
    cosine, sine = cos_ref[...], sin_ref[...]
    q_ref[:, :half] = (front * cosine - behind * sine).astype(LOW)
    q_ref[:, half:] = (behind * cosine + front * sine).astype(LOW)
    scores = contract_last(q_ref[...], kv_ref[:, :HEAD_DIM])
    scores = jnp.where(limit_ref[...] <= places_ref[...], scores, NEGATIVE)
    raised = jnp.exp(scores - jnp.max(scores, axis=-1, keepdims=True))
    probs = raised * (1.0 / jnp.sum(raised, axis=-1, keepdims=True))
    probs_ref[0] = probs
    attended = jnp.dot(probs.astype(LOW), kv_ref[:, HEAD_DIM:], preferred_element_type=WIDE)
    wide_ref[...] = attended
    low_ref[...] = attended.astype(LOW)


def attention_forward(projected, gain, cosine, sine, query_places, key_limit, keys_values, heads):
    rows = projected.shape[0]
    keys = keys_values.shape[0]
    block = min(rows, 256, (1 << 19) // keys)
    return pl.pallas_call(
        attention_kernel,
        grid=(heads, rows // block),
        in_specs=[
            pl.BlockSpec((block, HEAD_DIM), lambda h, i: (i, h)),
            pl.BlockSpec((1, HEAD_DIM), lambda h, i: (0, 0)),
            pl.BlockSpec((block, HEAD_DIM // 2), lambda h, i: (i, 0)),
            pl.BlockSpec((block, HEAD_DIM // 2), lambda h, i: (i, 0)),
            pl.BlockSpec((block, 1), lambda h, i: (i, 0)),
            pl.BlockSpec((1, keys), lambda h, i: (0, 0)),
            pl.BlockSpec((keys, 2 * HEAD_DIM), lambda h, i: (0, 0)),
        ],
        out_specs=[
            pl.BlockSpec((block, HEAD_DIM), lambda h, i: (i, h)),
            pl.BlockSpec((1, block, keys), lambda h, i: (h, i, 0)),
            pl.BlockSpec((block, HEAD_DIM), lambda h, i: (i, h)),
            pl.BlockSpec((block, HEAD_DIM), lambda h, i: (i, h)),
        ],
        out_shape=[
            jax.ShapeDtypeStruct((rows, heads * HEAD_DIM), LOW),
            jax.ShapeDtypeStruct((heads, rows, keys), WIDE),
            jax.ShapeDtypeStruct((rows, heads * HEAD_DIM), WIDE),
            jax.ShapeDtypeStruct((rows, heads * HEAD_DIM), LOW),
        ],
        cost_estimate=pl.CostEstimate(
            flops=4 * heads * rows * keys * HEAD_DIM,
            bytes_accessed=4 * heads * rows * keys + 4 * keys * HEAD_DIM + 14 * rows * heads * HEAD_DIM,
            transcendentals=heads * rows * keys,
        ),
    )(projected, gain, cosine, sine, query_places, key_limit, keys_values)


def attention_back_kernel(
    grad_ref, wide_ref, probs_ref, q_ref, raw_ref, gain_ref, cos_ref, sin_ref, kv_ref,
    grad_raw_ref, grad_gain_ref, grad_kv_ref, total,
):
    head, step = pl.program_id(0), pl.program_id(1)
    first = jnp.logical_and(head == 0, step == 0)
    last = jnp.logical_and(head == pl.num_programs(0) - 1, step == pl.num_programs(1) - 1)
    grad = grad_ref[...]
    delta = jnp.sum(grad.astype(WIDE) * wide_ref[...], axis=-1, keepdims=True)
    probs = probs_ref[0]
    grad_probs = contract_last(grad, kv_ref[:, HEAD_DIM:])
    grad_scores = (probs * (grad_probs - delta)).astype(LOW)
    rotated = jnp.dot(grad_scores, kv_ref[:, :HEAD_DIM], preferred_element_type=WIDE)
    key_part = over_rows(grad_scores, q_ref[...])
    value_part = over_rows(probs.astype(LOW), grad)

    @pl.when(first)
    def _():
        total[:, :HEAD_DIM] = key_part
        total[:, HEAD_DIM:] = value_part

    @pl.when(jnp.logical_not(first))
    def _():
        total[:, :HEAD_DIM] += key_part
        total[:, HEAD_DIM:] += value_part

    @pl.when(last)
    def _():
        grad_kv_ref[...] = total[...].astype(LOW)

    half = rotated.shape[1] // 2
    front, behind = rotated[:, :half], rotated[:, half:]
    cosine, sine = cos_ref[...], sin_ref[...]
    back = jnp.concatenate([front * cosine + behind * sine, behind * cosine - front * sine], axis=1)
    raw = raw_ref[...]
    scale = lax.rsqrt(jnp.mean(raw * raw, axis=-1, keepdims=True) + EPSILON)
    normed = raw * scale
    gain_part = jnp.sum(back * normed, axis=0, keepdims=True)

    @pl.when(first)
    def _():
        grad_gain_ref[...] = gain_part

    @pl.when(jnp.logical_not(first))
    def _():
        grad_gain_ref[...] += gain_part

    back = back * gain_ref[...]
    grad_raw_ref[...] = (
        scale * (back - normed * jnp.mean(back * normed, axis=-1, keepdims=True))
    ).astype(LOW)


def attention_backward(grad, wide, probs, q_low, projected, gain, cosine, sine, keys_values):
    heads, rows, keys = probs.shape
    block = min(rows, 256, (1 << 19) // keys)

    def tile(h, i):
        return (i, h)

    def whole(h, i):
        return (0, 0)

    return pl.pallas_call(
        attention_back_kernel,
        grid=(heads, rows // block),
        in_specs=[
            pl.BlockSpec((block, HEAD_DIM), tile),
            pl.BlockSpec((block, HEAD_DIM), tile),
            pl.BlockSpec((1, block, keys), lambda h, i: (h, i, 0)),
            pl.BlockSpec((block, HEAD_DIM), tile),
            pl.BlockSpec((block, HEAD_DIM), tile),
            pl.BlockSpec((1, HEAD_DIM), whole),
            pl.BlockSpec((block, HEAD_DIM // 2), lambda h, i: (i, 0)),
            pl.BlockSpec((block, HEAD_DIM // 2), lambda h, i: (i, 0)),
            pl.BlockSpec((keys, 2 * HEAD_DIM), whole),
        ],
        out_specs=[
            pl.BlockSpec((block, HEAD_DIM), tile),
            pl.BlockSpec((1, HEAD_DIM), whole),
            pl.BlockSpec((keys, 2 * HEAD_DIM), whole),
        ],
        out_shape=[
            jax.ShapeDtypeStruct((rows, heads * HEAD_DIM), LOW),
            jax.ShapeDtypeStruct((1, HEAD_DIM), WIDE),
            jax.ShapeDtypeStruct((keys, 2 * HEAD_DIM), LOW),
        ],
        scratch_shapes=[pltpu.VMEM((keys, 2 * HEAD_DIM), WIDE)],
        cost_estimate=pl.CostEstimate(
            flops=8 * heads * rows * keys * HEAD_DIM,
            bytes_accessed=4 * heads * rows * keys + 8 * keys * HEAD_DIM + 14 * rows * heads * HEAD_DIM,
            transcendentals=0,
        ),
    )(grad, wide, probs, q_low, projected, gain, cosine, sine, keys_values)


def widen_kernel(places, source, out):
    out[...] = source[0, 0, 0].astype(WIDE)


def widen_one(pieces, places, which):
    parts, run, _, rows, width = pieces.shape
    return pl.pallas_call(
        widen_kernel,
        grid_spec=pltpu.PrefetchScalarGridSpec(
            num_scalar_prefetch=1,
            grid=(run, parts),
            in_specs=[pl.BlockSpec((1, 1, 1, rows, width), lambda k, r, p: (r, k, which, 0, 0))],
            out_specs=pl.BlockSpec((rows, width), lambda k, r, p: (0, p[k] * parts + r)),
        ),
        out_shape=jax.ShapeDtypeStruct((rows, width * parts * run), WIDE),
        cost_estimate=pl.CostEstimate(flops=0, bytes_accessed=3 * pieces.size, transcendentals=0),
    )(places, pieces)


def shift_blocks(make):
    run = lax.axis_size("wsh")
    here = lax.axis_index("wsh")
    received = []
    for k in range(run):
        block = make((here + k) % run)
        if k:
            block = lax.ppermute(block, "wsh", [(i, (i + k) % run) for i in range(run)])
        received.append(block)
    return received


def head_piece_kernel(run, query_width, places, *refs):
    sources, (own_ref, out_ref, total) = refs[:run], refs[run:]
    kv_width = KV_HEADS * HEAD_DIM
    query_all = run * query_width
    head_width = query_width + 2 * HEAD_DIM
    total[...] = jnp.zeros_like(total)
    rest = jnp.zeros((out_ref.shape[0], sources[0].shape[1] - head_width), WIDE)
    for k, source in enumerate(sources):
        place = places[k]
        out_ref[:, pl.ds(pl.multiple_of(place * query_width, query_width), query_width)] = source[
            :, :query_width
        ]
        head = place * KV_HEADS // run
        for number in range(2):
            begin = query_width + number * HEAD_DIM
            at = pl.multiple_of(head * HEAD_DIM + number * kv_width, HEAD_DIM)
            total[:, pl.ds(at, HEAD_DIM)] += source[:, begin : begin + HEAD_DIM].astype(WIDE)
        rest += source[:, head_width:].astype(WIDE)
    begin = query_all + 2 * kv_width
    out_ref[:, query_all:begin] = total[...].astype(LOW)
    out_ref[:, begin : begin + rest.shape[1]] = rest.astype(LOW)
    out_ref[:, begin + rest.shape[1] :] = own_ref[:, run * sources[0].shape[1] :]


def head_piece_sum(sources, own, places, query_width):
    run = len(sources)
    rows, columns = sources[0].shape
    kv_width = KV_HEADS * HEAD_DIM
    rest = columns - query_width - 2 * HEAD_DIM
    width = run * query_width + 2 * kv_width + rest + own.shape[1] - run * columns

    def whole(i, p):
        return (0, 0)

    return pl.pallas_call(
        functools.partial(head_piece_kernel, run, query_width),
        grid_spec=pltpu.PrefetchScalarGridSpec(
            num_scalar_prefetch=1,
            grid=(1,),
            in_specs=[pl.BlockSpec((rows, columns), whole)] * run
            + [pl.BlockSpec(own.shape, whole)],
            out_specs=pl.BlockSpec((rows, width), whole),
            scratch_shapes=[pltpu.VMEM((rows, 2 * kv_width), WIDE)],
        ),
        out_shape=jax.ShapeDtypeStruct((rows, width), LOW),
        cost_estimate=pl.CostEstimate(
            flops=0, bytes_accessed=2 * (own.size + 2 * rows * width), transcendentals=0
        ),
    )(places, *sources, own)


def shift_exchange(make):
    run = lax.axis_size("wsh")
    order = (lax.axis_index("wsh") - jnp.arange(run, dtype=jnp.int32)) % run
    return jnp.take(jnp.stack(shift_blocks(make)), order, axis=0)


def place_kernel(places, *refs):
    step = pl.program_id(0)
    sources, out = refs[:-1], refs[-1]
    for number, source in enumerate(sources):

        @pl.when(step == number)
        def _(source=source):
            out[...] = source[...]


def place_columns(blocks, places):
    rows, width = blocks[0].shape
    count = len(blocks)
    return pl.pallas_call(
        place_kernel,
        grid_spec=pltpu.PrefetchScalarGridSpec(
            num_scalar_prefetch=1,
            grid=(count,),
            in_specs=[pl.BlockSpec((rows, width), lambda k, p: (0, 0))] * count,
            out_specs=pl.BlockSpec((rows, width), lambda k, p: (0, p[k])),
        ),
        out_shape=jax.ShapeDtypeStruct((rows, width * count), blocks[0].dtype),
        cost_estimate=pl.CostEstimate(
            flops=0, bytes_accessed=4 * count * blocks[0].size, transcendentals=0
        ),
    )(places, *blocks)


def entry(stacked):
    return lambda index: lax.dynamic_index_in_dim(stacked, index, 0, False)


def shards(
    tokens,
    cotangent,
    lengths,
    positions,
    token_ids,
    per_layer_table,
    w_query,
    w_key,
    w_value,
    w_output,
    laurel_left,
    laurel_right,
    w_gate,
    w_up,
    w_down,
    w_layer_gate,
    w_layer_proj,
    norm_gains,
    query_gain,
    key_gain,
):
    rows_dev, width = tokens.shape[1:]
    run = lax.axis_size("wsh")
    contexts = lax.axis_size("ctx")
    parts = 2 * contexts
    chip = lax.axis_index(COPIES)
    shard_rows = width // run
    heads_here = HEADS // run
    groups = HEADS // KV_HEADS
    query_width = heads_here * HEAD_DIM
    head_width = query_width + 2 * HEAD_DIM
    hidden_width = w_gate.shape[1] // run
    head_piece = shard_rows // parts
    piece = hidden_width // parts
    rank = laurel_left.shape[1]
    places = ((lax.axis_index("wsh") - jnp.arange(run)) % run).astype(jnp.int32)
    gain_cut = query_gain.shape[0]

    def share(weight):
        return lax.dynamic_slice_in_dim(weight, chip * head_piece, head_piece, 0)

    query_rows, key_rows, value_rows = share(w_query), share(w_key), share(w_value)

    indices = shift_exchange(lambda k: jnp.concatenate([token_ids, positions], axis=0))
    small = jnp.concatenate(
        [
            norm_gains.T,
            jnp.pad(
                jnp.concatenate([query_gain, key_gain])[None],
                ((0, 1), (0, shard_rows - 2 * gain_cut)),
            ),
        ],
        axis=0,
    )
    proj_rows = w_layer_proj.shape[0]
    proj_share = lax.dynamic_slice_in_dim(w_layer_proj, chip * (width // parts), width // parts, 1)
    common = jnp.concatenate(
        [
            share(laurel_left),
            share(laurel_right),
            share(w_layer_gate),
            proj_share.reshape(head_piece, -1),
        ],
        axis=1,
    )
    fetch_width = head_width + common.shape[1]
    small_flat = jnp.pad(small.reshape(-1), (0, -small.size % fetch_width)).reshape(-1, fetch_width)
    small_flat = jnp.pad(small_flat, ((0, 16 - small_flat.shape[0]), (0, 0)))
    common, query_rows, key_rows, value_rows, small_flat, indices = lax.optimization_barrier(
        (common, query_rows, key_rows, value_rows, small_flat, indices)
    )

    def head_block(index):
        kv = index * heads_here // groups * HEAD_DIM
        block = jnp.concatenate(
            [
                lax.dynamic_slice_in_dim(query_rows, index * query_width, query_width, 1),
                lax.dynamic_slice_in_dim(key_rows, kv, HEAD_DIM, 1),
                lax.dynamic_slice_in_dim(value_rows, kv, HEAD_DIM, 1),
                common,
            ],
            axis=1,
        )
        return jnp.concatenate([small_flat, block], axis=0)

    head_share = shift_exchange(head_block)
    small_all = head_share[:, :16].reshape(run, -1)[:, : small.size].reshape(run, 8, shard_rows)
    fetched = lax.all_gather(head_share[:, 16:], COPIES, axis=0)
    w_heads = fetched[:, :, :, :head_width]
    proj_at = head_width + 2 * rank + w_layer_gate.shape[1]
    layer_proj_full = fetched[:, :, :, proj_at:].reshape(parts, run, proj_rows, width // parts)
    layer_proj_full = layer_proj_full.transpose(1, 2, 0, 3).reshape(run * proj_rows, width)
    laurel_weights = fetched[:, :, :, head_width:proj_at].transpose(1, 0, 2, 3).reshape(width, -1)
    left_full = laurel_weights[:, :rank]
    right_full = laurel_weights[:, rank : 2 * rank]
    layer_gate_full = laurel_weights[:, 2 * rank :]
    w_heads = w_heads.transpose(1, 0, 2, 3).reshape(width, head_width)

    gains_full = small_all.transpose(1, 0, 2).reshape(8, width).astype(WIDE)
    query_gain_full = small_all[:, 6, :gain_cut].reshape(HEAD_DIM).astype(WIDE)
    key_gain_full = small_all[:, 6, gain_cut : 2 * gain_cut].reshape(HEAD_DIM).astype(WIDE)
    tokens_run = spread(tokens[0], "wsh")

    indices = indices[None]
    bit = 1
    while bit < contexts:
        indices = jnp.concatenate([indices, swap(indices, "ctx", bit)], axis=0)
        bit *= 2
    run_places = indices[0, :, 1].reshape(-1)
    here_ctx = lax.axis_index("ctx")
    context_order = jnp.bitwise_xor(jnp.arange(contexts, dtype=jnp.int32), here_ctx)
    key_places = jnp.take(indices[:, :, 1], context_order, axis=0).reshape(-1)
    own_ids = indices[:, :, 0].reshape(-1)
    all_ids = jnp.concatenate([own_ids, swap(own_ids, "slot", 1)])
    length = lengths[0]

    vocab_rows = per_layer_table.shape[0]
    vocab_first = lax.axis_index(EVERY) * vocab_rows
    vocab_range = jnp.arange(vocab_rows, dtype=jnp.int32)

    def one_hot():
        return ((all_ids - vocab_first)[:, None] == vocab_range[None, :]).astype(LOW)

    table_rows = matmul(one_hot(), per_layer_table).astype(LOW)
    tokens_run, table_rows = lax.optimization_barrier((tokens_run, table_rows))
    def pair_block(index):
        first = index * hidden_width + chip * piece
        gate_cut = lax.dynamic_slice_in_dim(w_gate, first, piece, 1)
        up_cut = lax.dynamic_slice_in_dim(w_up, first, piece, 1)
        gate_cut, up_cut = after((gate_cut, up_cut), head_share)
        return jnp.concatenate([gate_cut.T, up_cut.T], axis=0)

    pair_received = shift_blocks(pair_block)
    normed_run = rms_norm(tokens_run.astype(WIDE), gains_full[0]).astype(LOW)
    tokens_f = tokens[0].astype(WIDE)
    normed = rms_norm(tokens_f, gains_full[0])
    normed_low = normed.astype(LOW)
    total_rows = run * rows_dev
    projected = matmul(normed_run, w_heads)
    key = projected[:, query_width : query_width + HEAD_DIM]
    value = projected[:, query_width + HEAD_DIM :]

    def key_path(raw, gain):
        return rotate(rms_norm(raw.reshape(total_rows, 1, HEAD_DIM), gain), run_places)[:, 0]

    def value_path(raw):
        return rms_norm(raw, 1.0)

    k_low = key_path(key, key_gain_full).astype(LOW)
    v_low = value_path(value).astype(LOW)
    keys_values = spread(jnp.concatenate([k_low, v_low], axis=1), "ctx")
    half = table_rows.shape[0] // 2
    looked_up = add_low(table_rows[:half], swap(table_rows[half:], "slot", 1))
    bit = contexts // 2
    while bit:
        half = looked_up.shape[0] // 2
        looked_up = add_low(looked_up[:half], swap(looked_up[half:], "ctx", bit))
        bit //= 2
    looked_up = looked_up.reshape(run, rows_dev, -1)
    inverse = jnp.exp(
        -math.log(ROPE_BASE)
        * (2.0 * jnp.arange(HEAD_DIM // 2, dtype=jnp.float32) / HEAD_DIM)
    )
    angles = run_places.astype(WIDE)[:, None] * inverse[None, :]
    cosine, sine = jnp.cos(angles), jnp.sin(angles)
    key_limit = jnp.where(key_places < length, key_places, jnp.int32(1 << 30))
    q_low, probs, attended, attended_low = attention_forward(
        projected,
        query_gain_full[None],
        cosine,
        sine,
        run_places[:, None],
        key_limit[None],
        keys_values,
        heads_here,
    )
    attended_low, pair_received = lax.optimization_barrier((attended_low, pair_received))
    pair_share = place_columns(pair_received, places)
    pair_weight = lax.all_gather(pair_share, COPIES, axis=0, tiled=True)
    attn_proj = collect(matmul(attended_low, w_output).astype(LOW), "wsh")
    attn_proj, looked_up = lax.optimization_barrier((attn_proj, looked_up))

    first_sum = tokens_f + rms_norm(attn_proj, gains_full[1])
    low_rank_low = matmul(normed_low, left_full).astype(LOW)
    laurel_out = times_transposed(low_rank_low, right_full)
    laurel = normed + rms_norm(laurel_out, gains_full[2])
    mixed = (first_sum + laurel) * HALF_ROOT
    ff_in_low = rms_norm(mixed, gains_full[3]).astype(LOW)

    ff_run = spread(ff_in_low, "wsh")
    looked_up = after(looked_up, ff_run)
    layer_input = EMBED_SCALE * jnp.sum(shift_exchange(entry(looked_up)).astype(WIDE), axis=0)
    aligned = piece % 128 == 0
    if aligned:
        both, hidden_low, ff_part = ff_forward(ff_run, pair_weight, w_down, piece)
    else:
        both = times_transposed(ff_run, pair_weight)
        both_parts = both.reshape(total_rows, parts, 2, piece)
        gate = both_parts[:, :, 0].reshape(total_rows, hidden_width)
        upward = both_parts[:, :, 1].reshape(total_rows, hidden_width)
        hidden_low = gated_product(gate, upward).astype(LOW)
        ff_part = matmul(hidden_low, w_down).astype(LOW)
    ff_part, layer_input = lax.optimization_barrier((ff_part, layer_input))
    ff_out = collect(ff_part, "wsh")
    third_sum = mixed + rms_norm(ff_out, gains_full[4])
    third_low = third_sum.astype(LOW)

    layer_gate = matmul(third_low, layer_gate_full)
    gated_low = gated_product(layer_gate, layer_input).astype(LOW)
    layer_proj = matmul(gated_low, layer_proj_full)
    result = third_sum + rms_norm(layer_proj, gains_full[5])
    layer_out = result.astype(LOW)[None]

    valid = (positions[0] < length).astype(WIDE)
    grad_out = cotangent[0].astype(WIDE) * valid[:, None]
    _, pullback = jax.vjp(rms_norm, layer_proj, gains_full[5])
    grad_proj, grad_gain_five = pullback(grad_out)
    grad_proj_low = grad_proj.astype(LOW)
    grad_gated = times_transposed(grad_proj_low, layer_proj_full)
    _, pullback = jax.vjp(gated_product, layer_gate, layer_input)
    grad_lgate, grad_input = pullback(grad_gated)
    grad_lgate_low = grad_lgate.astype(LOW)
    grad_input_low = grad_input.astype(LOW)
    grad_third = grad_out + times_transposed(grad_lgate_low, layer_gate_full)
    _, pullback = jax.vjp(rms_norm, ff_out, gains_full[4])
    grad_ff, grad_gain_four = pullback(grad_third)
    grad_ff_low = grad_ff.astype(LOW)

    grad_ff_run = spread(grad_ff_low, "wsh")
    down_part = over_rows(hidden_low, grad_ff_run).astype(LOW)
    grad_ff_run, down_part = lax.optimization_barrier((grad_ff_run, down_part))
    down_own = lax.psum_scatter(down_part, COPIES, scatter_dimension=0, tiled=True)
    grad_input_low = after(grad_input_low, grad_ff_run)
    every_grad = shift_exchange(lambda k: grad_input_low).reshape(total_rows, -1)

    def wider(rows, axis, bit):
        return jnp.concatenate([rows, swap(rows, axis, bit)], axis=0)

    hops = [1 << power for power in range(contexts.bit_length() - 1)]
    if aligned:
        grad_both, ff_part = ff_backward(grad_ff_run, pair_weight, w_down, both, piece)
    else:
        grad_hidden = times_transposed(grad_ff_run, w_down)
        _, pullback = jax.vjp(gated_product, gate, upward)
        grad_gate, grad_upward = pullback(grad_hidden)
        grad_both = jnp.stack(
            [
                grad_gate.reshape(total_rows, parts, piece),
                grad_upward.reshape(total_rows, parts, piece),
            ],
            axis=2,
        )
        grad_both = grad_both.reshape(total_rows, 2 * hidden_width).astype(LOW)
        ff_part = matmul(grad_both, pair_weight).astype(LOW)
    ff_part, every_grad = lax.optimization_barrier((ff_part, every_grad))
    every_grad = wider(every_grad, "ctx", hops[0])
    grad_ff_in = collect(ff_part, "wsh")
    pair_part = over_rows(after(grad_both, ff_part), ff_run).astype(LOW)
    grad_ff_in, pair_part, every_grad = lax.optimization_barrier((grad_ff_in, pair_part, every_grad))
    for bit in hops[1:]:
        every_grad = wider(every_grad, "ctx", bit)
    pair_own = lax.psum_scatter(pair_part, COPIES, scatter_dimension=0, tiled=True)
    _, pullback = jax.vjp(rms_norm, mixed, gains_full[3])
    grad_mixed_norm, grad_gain_three = pullback(grad_ff_in)
    grad_branch = (grad_third + grad_mixed_norm) * HALF_ROOT
    _, pullback = jax.vjp(rms_norm, attn_proj, gains_full[1])
    grad_attn, grad_gain_one = pullback(grad_branch)
    grad_attn_low = grad_attn.astype(LOW)
    grad_attn_run = spread(grad_attn_low, "wsh")
    grad_attn_run, down_own, every_grad = lax.optimization_barrier(
        (grad_attn_run, down_own, every_grad)
    )
    every_grad = wider(every_grad, "slot", 1)
    down_grad = lax.all_gather(down_own, COPIES, axis=0, tiled=True)

    def pair_back(index):
        block = lax.dynamic_slice_in_dim(pair_own, index * shard_rows, shard_rows, 1)
        return block.reshape(2, piece, shard_rows).transpose(0, 2, 1)

    _, pullback = jax.vjp(rms_norm, laurel_out, gains_full[2])
    grad_laurel, grad_gain_two = pullback(grad_branch)
    grad_laurel_low = grad_laurel.astype(LOW)
    grad_rank_low = matmul(grad_laurel_low, right_full).astype(LOW)

    left_grad = over_rows(normed_low, grad_rank_low)
    right_grad = over_rows(grad_laurel_low, low_rank_low)
    layer_gate_grad = over_rows(third_low, grad_lgate_low)
    layer_proj_grad = over_rows(gated_low, grad_proj_low)

    narrow = jnp.concatenate([left_grad, right_grad, layer_gate_grad], axis=1).astype(LOW)
    narrow_columns = narrow.shape[1]
    proj_back = layer_proj_grad.astype(LOW).reshape(run, proj_rows, parts, width // parts)
    proj_back = proj_back.transpose(0, 2, 1, 3).reshape(run, parts, head_piece, -1)
    narrow = jnp.concatenate(
        [narrow.reshape(run, parts, head_piece, narrow_columns), proj_back], axis=3
    )

    grad_att_low = times_transposed(grad_attn_run, w_output).astype(LOW)
    grad_query, grad_query_gain, kv_part = attention_backward(
        grad_att_low,
        attended,
        probs,
        q_low,
        projected,
        query_gain_full[None],
        cosine,
        sine,
        keys_values,
    )
    grad_query_gain = grad_query_gain[0]
    kv_sum = collect(kv_part, "ctx")
    output_part = over_rows(attended_low, grad_attn_run).astype(LOW)
    kv_sum, pair_own, output_part, narrow, every_grad = lax.optimization_barrier(
        (kv_sum, pair_own, output_part, narrow, every_grad)
    )
    pair_blocks = jnp.stack(shift_blocks(pair_back))
    _, pullback = jax.vjp(key_path, key, key_gain_full)
    grad_key, grad_key_gain = pullback(kv_sum[:, :HEAD_DIM])
    _, pullback = jax.vjp(value_path, value)
    (grad_value,) = pullback(kv_sum[:, HEAD_DIM:])
    grad_heads = jnp.concatenate(
        [grad_query, grad_key.astype(LOW), grad_value.astype(LOW)], axis=1
    )
    heads_part = over_rows(normed_run, grad_heads).astype(LOW)
    heads_part = heads_part.reshape(run, parts, head_piece, head_width)
    heads_part = jnp.concatenate(
        [one[index] for index in range(run) for one in (heads_part, narrow)]
        + [output_part.reshape(parts, head_piece, width)],
        axis=2,
    )
    fetch_back = head_width + narrow.shape[3]
    heads_kept, heads_given = halves(heads_part)
    normed_part = times_transposed(grad_heads, w_heads).astype(LOW)
    heads_pieces = [add_low(a, b) for a, b in zip(nearest(heads_kept), nearest(heads_given))]
    heads_first = reduce_first(heads_pieces)
    normed_part, heads_first, pair_blocks, down_grad = lax.optimization_barrier(
        (normed_part, heads_first, pair_blocks, down_grad)
    )
    pair_all = lax.all_gather(pair_blocks, COPIES, axis=0)
    table_grad = EMBED_SCALE * over_rows(one_hot(), after(every_grad, normed_part))
    heads_second = reduce_second(heads_pieces, heads_first)
    grad_run = collect(normed_part, "wsh")
    down_grad = after(down_grad, table_grad).astype(WIDE)
    grad_run, heads_second, table_grad, down_grad = lax.optimization_barrier(
        (grad_run, heads_second, table_grad, down_grad)
    )
    heads_own = reduce_last(heads_pieces, heads_second)

    def head_back(index):
        return lax.dynamic_slice_in_dim(heads_own, index * fetch_back, fetch_back, 1)

    heads_sent = shift_blocks(head_back)
    grad_normed = (
        grad_run
        + times_transposed(grad_rank_low, left_full)
        + grad_branch
    )
    _, pullback = jax.vjp(rms_norm, tokens_f, gains_full[0])
    grad_tokens, grad_gain_zero = pullback(grad_normed)
    tokens_grad = (grad_tokens + grad_branch).astype(LOW)[None]

    vector = jnp.concatenate(
        [grad_query_gain.reshape(run, gain_cut), grad_key_gain.reshape(run, gain_cut)], axis=1
    )
    vector = jnp.pad(vector, ((0, 0), (0, shard_rows - 2 * gain_cut))).reshape(width)
    gain_sums = jnp.stack(
        [
            grad_gain_zero,
            grad_gain_one,
            grad_gain_two,
            grad_gain_three,
            grad_gain_four,
            grad_gain_five,
            vector,
            jnp.zeros_like(vector),
        ]
    )
    gain_sums = gain_sums.reshape(8, run, shard_rows).transpose(1, 0, 2).reshape(8 * run, shard_rows)
    gain_sums = collect(gain_sums, "wsh")
    heads_piece = head_piece_sum(heads_sent, heads_own, places, query_width)
    kv_width = KV_HEADS * HEAD_DIM
    cuts = []
    for size in (
        HEADS * HEAD_DIM,
        kv_width,
        kv_width,
        rank,
        rank,
        w_layer_gate.shape[1],
        narrow.shape[3] - narrow_columns,
        width,
    ):
        cuts.append((sum(w for _, w in cuts), size))
    heads_piece, gain_sums = after((heads_piece, gain_sums), pair_all)
    heads_near = gather_first(heads_piece)
    gain_sums = jnp.sum(spread(gain_sums[None], COPIES), axis=0)
    own = jnp.full((1,), chip, jnp.int32)
    if aligned:
        gate_grad, up_grad = widen_one(pair_all, places, 0), widen_one(pair_all, places, 1)
    else:
        pair_all = jnp.take(pair_all, places, axis=1)
        pair_all = pair_all.transpose(2, 3, 1, 0, 4).reshape(2, shard_rows, -1).astype(WIDE)
        gate_grad, up_grad = pair_all[0], pair_all[1]

    heads_near, gain_sums, gate_grad = lax.optimization_barrier((heads_near, gain_sums, gate_grad))
    heads_near = gather_second(heads_piece, heads_near)
    heads_near, up_grad = lax.optimization_barrier((heads_near, up_grad))
    heads_all = last_gather(heads_near)
    (
        query_grad,
        key_grad,
        value_grad,
        left_grad,
        right_grad,
        layer_gate_grad,
        layer_proj_grad,
        output_grad,
    ) = assemble(
        [p[None] for p in heads_all], own, WIDE, cuts
    )
    layer_proj_grad = layer_proj_grad.reshape(parts, proj_rows, width // parts)
    layer_proj_grad = layer_proj_grad.transpose(1, 0, 2).reshape(proj_rows, width)

    return (
        layer_out,
        tokens_grad,
        table_grad,
        query_grad.reshape(shard_rows, -1),
        key_grad.reshape(shard_rows, -1),
        value_grad.reshape(shard_rows, -1),
        output_grad.reshape(query_width, width),
        left_grad.reshape(shard_rows, -1),
        right_grad.reshape(shard_rows, -1),
        gate_grad,
        up_grad,
        down_grad,
        layer_gate_grad.reshape(shard_rows, -1),
        layer_proj_grad,
        gain_sums[:6].T,
        gain_sums[6, :gain_cut],
        gain_sums[6, gain_cut : 2 * gain_cut],
    )


def solution(mesh):
    placed = (
        P("slot", ("ctx", "wsh"), None),
        P("slot", ("ctx", "wsh"), None),
        P("slot"),
        P("slot", ("ctx", "wsh")),
        P("slot", ("ctx", "wsh")),
        P(("slot", "ctx", "wsh"), None),
        P("wsh", None),
        P("wsh", None),
        P("wsh", None),
        P("wsh", None),
        P("wsh", None),
        P("wsh", None),
        P("wsh", None),
        P("wsh", None),
        P("wsh", None),
        P("wsh", None),
        P("wsh", None),
        P("wsh", None),
        P("wsh"),
        P("wsh"),
    )
    return jax.shard_map(
        shards,
        mesh=mesh,
        in_specs=placed,
        out_specs=(
            P("slot", ("ctx", "wsh"), None),
            P("slot", ("ctx", "wsh"), None),
            P(("slot", "ctx", "wsh"), None),
            P("wsh", None),
            P("wsh", None),
            P("wsh", None),
            P("wsh", None),
            P("wsh", None),
            P("wsh", None),
            P("wsh", None),
            P("wsh", None),
            P("wsh", None),
            P("wsh", None),
            P("wsh", None),
            P("wsh", None),
            P("wsh"),
            P("wsh"),
        ),
        check_vma=False,
    )
```
